32 devices in a mesh: branch: 4 (over x, core), ty: 2 (over y), tx: 4 (over z).
Axes of the slice: x: 2, y: 2, z: 4, core: 2. Of those that a mesh axis runs over, the one named last changes fastest.
Arguments:
- feat0: bfloat16 [48, 128, 256], P(None, 'ty', 'tx'), may hold values from -6 to 6
- feat1: bfloat16 [96, 64, 128], P(None, 'ty', 'tx'), may hold values from -6 to 6
- feat2: bfloat16 [192, 32, 64], P(None, 'ty', 'tx'), may hold values from -6 to 6
- feat3: bfloat16 [384, 16, 32], P(None, 'ty', 'tx'), may hold values from -6 to 6
- block_w0: bfloat16 [2, 48, 432], replicated, may hold values from -0.3125 to 0.3125
- block_w1: bfloat16 [2, 96, 864], replicated, may hold values from -0.21875 to 0.21875
- block_w2: bfloat16 [2, 192, 1728], replicated, may hold values from -0.15625 to 0.15625
- block_w3: bfloat16 [2, 384, 3456], replicated, may hold values from -0.109375 to 0.109375
- block_b0: float32 [2, 48], replicated, may hold values from -1.8 to 1.8
- block_b1: float32 [2, 96], replicated, may hold values from -1.8 to 1.8
- block_b2: float32 [2, 192], replicated, may hold values from -1.8 to 1.8
- block_b3: float32 [2, 384], replicated, may hold values from -1.8 to 1.8
- up_w1: bfloat16 [1, 48, 96], replicated, may hold values from -0.625 to 0.625
- up_w2: bfloat16 [1, 144, 192], replicated, may hold values from -0.4375 to 0.4375
- up_w3: bfloat16 [1, 336, 384], replicated, may hold values from -0.3125 to 0.3125
- down_mid0: bfloat16 [1, 3, 48, 432], replicated, may hold values from -0.3125 to 0.3125
- down_mid1: bfloat16 [1, 1, 96, 864], replicated, may hold values from -0.21875 to 0.21875
- down_fin0: bfloat16 [1, 672, 432], replicated, may hold values from -0.3125 to 0.3125
- down_fin1: bfloat16 [1, 576, 864], replicated, may hold values from -0.21875 to 0.21875
- down_fin2: bfloat16 [1, 384, 1728], replicated, may hold values from -0.15625 to 0.15625
Outputs:
- joined0: bfloat16 [48, 128, 256], P(None, 'ty', 'tx')
- joined1: bfloat16 [96, 64, 128], P(None, 'ty', 'tx')
- joined2: bfloat16 [192, 32, 64], P(None, 'ty', 'tx')
- joined3: bfloat16 [384, 16, 32], P(None, 'ty', 'tx')
The draws below stay inside these ranges and needn't reach their ends.
All inputs are finite; a program needn't handle non-finite values.
Results may differ from the reference program's by a relative error of at most 0.0095.
Values may be sent and summed in bfloat16 or wider, within the bound.
A program may use at most 128 MiB of HBM per device.

```python
import jax
import jax.numpy as jnp

CHAN = 48
MODULES = 1
BLOCKS = 1
CONVS = 2
HEIGHT = 128
WIDTH = 256


def shard_levels(own_key, shape, split, smallest, top_value):
    level, own = 1.0, jax.random.fold_in(own_key, 6)
    for axis_at, shards_of in split:
        draws = jnp.exp(jax.random.uniform(jax.random.fold_in(own, axis_at), (shards_of,), jnp.float32, smallest / len(split), top_value / len(split)))
        level = level * jnp.repeat(draws, shape[axis_at] // shards_of).reshape([-1 if axis == axis_at else 1 for axis in range(len(shape))])
    return level


def normal_values(rng, dims, scale, most, cuts=(), kind=jnp.bfloat16):
    values = scale * jax.random.normal(rng, dims, jnp.float32)
    if cuts:
        values = values * shard_levels(rng, dims, cuts, -0.22, 0.18)
    return jnp.clip(values, -most, most).astype(kind)


def setup_inputs(seed: int = 0) -> dict:
    key_of = jax.random.split(jax.random.key(seed), 21)
    feat0 = normal_values(key_of[0], (CHAN, HEIGHT, WIDTH), 1.0, 6.0, ((1, 2), (2, 4)))
    feat1 = normal_values(key_of[1], (2 * CHAN, HEIGHT // 2, WIDTH // 2), 1.0, 6.0, ((1, 2), (2, 4)))
    feat2 = normal_values(key_of[2], (4 * CHAN, HEIGHT // 4, WIDTH // 4), 1.0, 6.0, ((1, 2), (2, 4)))
    feat3 = normal_values(key_of[3], (8 * CHAN, HEIGHT // 8, WIDTH // 8), 1.0, 6.0, ((1, 2), (2, 4)))
    block_w0 = normal_values(key_of[4], (CONVS, CHAN, 9 * CHAN), (9 * CHAN) ** -0.5, 0.3125)
    block_w1 = normal_values(key_of[5], (CONVS, 2 * CHAN, 18 * CHAN), (18 * CHAN) ** -0.5, 0.21875)
    block_w2 = normal_values(key_of[6], (CONVS, 4 * CHAN, 36 * CHAN), (36 * CHAN) ** -0.5, 0.15625)
    block_w3 = normal_values(key_of[7], (CONVS, 8 * CHAN, 72 * CHAN), (72 * CHAN) ** -0.5, 0.109375)
    block_b0 = normal_values(key_of[8], (CONVS, CHAN), 0.3, 1.8, (), jnp.float32)
    block_b1 = normal_values(key_of[9], (CONVS, 2 * CHAN), 0.3, 1.8, (), jnp.float32)
    block_b2 = normal_values(key_of[10], (CONVS, 4 * CHAN), 0.3, 1.8, (), jnp.float32)
    block_b3 = normal_values(key_of[11], (CONVS, 8 * CHAN), 0.3, 1.8, (), jnp.float32)
    up_w1 = normal_values(key_of[12], (MODULES, CHAN, 2 * CHAN), (2 * CHAN) ** -0.5, 0.625)
    up_w2 = normal_values(key_of[13], (MODULES, 3 * CHAN, 4 * CHAN), (4 * CHAN) ** -0.5, 0.4375)
    up_w3 = normal_values(key_of[14], (MODULES, 7 * CHAN, 8 * CHAN), (8 * CHAN) ** -0.5, 0.3125)
    down_mid0 = normal_values(key_of[15], (MODULES, 3, CHAN, 9 * CHAN), (9 * CHAN) ** -0.5, 0.3125)
    down_mid1 = normal_values(key_of[16], (MODULES, 1, 2 * CHAN, 18 * CHAN), (18 * CHAN) ** -0.5, 0.21875)
    down_fin0 = normal_values(key_of[17], (MODULES, 14 * CHAN, 9 * CHAN), (9 * CHAN) ** -0.5, 0.3125)
    down_fin1 = normal_values(key_of[18], (MODULES, 12 * CHAN, 18 * CHAN), (18 * CHAN) ** -0.5, 0.21875)
    down_fin2 = normal_values(key_of[19], (MODULES, 8 * CHAN, 36 * CHAN), (36 * CHAN) ** -0.5, 0.15625)
    return {"feat0": feat0, "feat1": feat1, "feat2": feat2, "feat3": feat3, "block_w0": block_w0, "block_w1": block_w1, "block_w2": block_w2, "block_w3": block_w3, "block_b0": block_b0, "block_b1": block_b1, "block_b2": block_b2, "block_b3": block_b3, "up_w1": up_w1, "up_w2": up_w2, "up_w3": up_w3, "down_mid0": down_mid0, "down_mid1": down_mid1, "down_fin0": down_fin0, "down_fin1": down_fin1, "down_fin2": down_fin2}


def convolve(feature, weight, stride):
    channels, height, breadth = feature.shape
    padded = jnp.pad(feature, ((0, 0), (1, 1), (1, 1)))
    out_height = height // stride
    out_breadth = breadth // stride
    running = jnp.zeros((weight.shape[0], out_height * out_breadth), jnp.float32)
    for tap_index in range(9):
        row_tap, col_tap = divmod(tap_index, 3)
        window = padded[:, row_tap:row_tap + stride * (out_height - 1) + 1:stride, col_tap:col_tap + stride * (out_breadth - 1) + 1:stride]
        window = window.reshape(channels, out_height * out_breadth)
        running = running + jnp.dot(weight[:, tap_index * channels:(tap_index + 1) * channels], window, preferred_element_type=jnp.float32)
    return running.reshape(weight.shape[0], out_height, out_breadth)


def residual_block(feature, first_weight, first_bias, second_weight, second_bias):
    inner = jax.nn.relu(convolve(feature, first_weight, 1) + first_bias[:, None, None]).astype(jnp.bfloat16)
    summed = feature.astype(jnp.float32) + convolve(inner, second_weight, 1) + second_bias[:, None, None]
    return jax.nn.relu(summed).astype(jnp.bfloat16)


def joining_terms(source, source_id, module_id, channels, up_weights, mid_weights, final_weights):
    result = []
    up_offset = 0
    down_offset = 0
    mid_count = 0
    if source_id > 0:
        lifted = jnp.dot(up_weights[source_id][module_id], source.reshape(source.shape[0], -1), preferred_element_type=jnp.float32)
    for target in range(4):
        if target == source_id:
            result.append(source)
        elif target < source_id:
            part = lifted[up_offset:up_offset + channels[target]].astype(jnp.bfloat16)
            up_offset = up_offset + channels[target]
            part = part.reshape(channels[target], source.shape[1], source.shape[2])
            factor = 2 ** (source_id - target)
            part = jnp.repeat(jnp.repeat(part, factor, axis=1), factor, axis=2)
            result.append(part)
        else:
            value = source
            for step_id in range(target - source_id - 1):
                value = jax.nn.relu(convolve(value, mid_weights[source_id][module_id, mid_count], 2)).astype(jnp.bfloat16)
                mid_count = mid_count + 1
            rows_used = final_weights[source_id][module_id, down_offset:down_offset + channels[target]]
            down_offset = down_offset + channels[target]
            result.append(convolve(value, rows_used, 2).astype(jnp.bfloat16))
    return result


def reference(feat0, feat1, feat2, feat3, block_w0, block_w1, block_w2, block_w3, block_b0, block_b1, block_b2, block_b3, up_w1, up_w2, up_w3, down_mid0, down_mid1, down_fin0, down_fin1, down_fin2):
    features = [feat0, feat1, feat2, feat3]
    block_weights = (block_w0, block_w1, block_w2, block_w3)
    block_biases = (block_b0, block_b1, block_b2, block_b3)
    up_weights = (None, up_w1, up_w2, up_w3)
    mid_weights = (down_mid0, down_mid1, None, None)
    final_weights = (down_fin0, down_fin1, down_fin2, None)
    channels = [feature.shape[0] for feature in features]
    for module_id in range(MODULES):
        sources = []
        for branch_id in range(4):
            source = features[branch_id]
            for block_id in range(BLOCKS):
                first_conv = (module_id * BLOCKS + block_id) * 2
                source = residual_block(source, block_weights[branch_id][first_conv], block_biases[branch_id][first_conv], block_weights[branch_id][first_conv + 1], block_biases[branch_id][first_conv + 1])
            sources.append(source)
        totals = [jnp.zeros(feature.shape, jnp.float32) for feature in features]
        for source_id in range(4):
            term_list = joining_terms(sources[source_id], source_id, module_id, channels, up_weights, mid_weights, final_weights)
            totals = [running + term.astype(jnp.float32) for running, term in zip(totals, term_list)]
        features = [jax.nn.relu(running).astype(jnp.bfloat16) for running in totals]
    return (features[0], features[1], features[2], features[3])
```

```python
import functools

import jax
import jax.numpy as jnp
from jax import lax
from jax.experimental import pallas as pl
from jax.experimental.pallas import tpu as pltpu
from jax.sharding import PartitionSpec as P

RIMS = (7, 3, 1, 0)
LANES = 128
NT = (((1,), (1,)), ((), ()))
NN = (((1,), (0,)), ((), ()))
WAYS = [(dy, dx) for dy in (-1, 0, 1) for dx in (-1, 0, 1) if dy or dx]
F32, BF16 = jnp.float32, jnp.bfloat16


def up_to(n, m):
    return -(-n // m) * m


class Level:
    def __init__(self, level, shape):
        self.rows, self.cols, self.chan = shape
        self.rim = RIMS[level]
        self.low = self.rim + 2
        self.pitch = up_to(self.cols + 2 + self.low, 8)
        self.lead = self.low + 1
        self.tail = self.pitch - self.cols
        self.planes = up_to(self.chan, LANES) // LANES
        self.near = up_to(self.low, 8)
        self.total = (self.lead + self.rows + 4) * self.pitch

    def at(self, row, col=0):
        return (row + self.lead) * self.pitch + col

    def first(self):
        start = self.at(-self.rim - 1) - self.tail
        return start, self.at(self.rows) + self.cols + 8 - start

    def second(self):
        start = self.at(-self.rim) - self.tail
        return start, self.at(self.rows - 1) + self.cols - start


def source_of(lv, way):
    dy, dx = way
    rows = (0, lv.rows) if dy == 0 else ((lv.rows - lv.low, lv.low) if dy > 0 else (0, 2))
    cols = (0, lv.cols) if dx == 0 else ((lv.cols - lv.near, lv.near) if dx > 0 else (0, 8))
    return rows, cols


def on_map(way, side):
    ok = True
    for step, axis in zip(way, ("ty", "tx")):
        if step:
            place = lax.axis_index(axis) + side * step
            ok = ok & (place >= 0) & (place < lax.axis_size(axis))
    return ok


def exchange(levels, *refs):
    feats, outs, (send, recv) = refs[:4], refs[4:36], refs[36:]
    here = {a: lax.axis_index(a) for a in ("ty", "tx")}
    barrier = pltpu.get_barrier_semaphore()

    def there(way):
        return {"ty": here["ty"] + way[0], "tx": here["tx"] + way[1]}

    count = 0
    for way in WAYS:
        ok = on_map(way, 1)

        @pl.when(ok)
        def _(way=way):
            pl.semaphore_signal(barrier, 1, device_id=there(way))

        count = count + jnp.where(ok, 1, 0)
    pl.semaphore_wait(barrier, count)

    def copy(l, k):
        way = WAYS[k]
        (r, nr), (c, nc) = source_of(levels[l], way)
        return pltpu.make_async_remote_copy(
            feats[l].at[pl.ds(r, nr), pl.ds(c, nc)],
            outs[8 * l + k],
            send.at[8 * l + k],
            recv.at[8 * l + k],
            device_id=there(way),
        )

    for k, way in enumerate(WAYS):

        @pl.when(on_map(way, 1))
        def _(k=k):
            for l in range(4):
                copy(l, k).start()

    for k, way in enumerate(WAYS):

        @pl.when(on_map(way, 1))
        def _(k=k):
            for l in range(4):
                copy(l, k).wait_send()

        @pl.when(on_map(way, -1))
        def _(k=k):
            for l in range(4):
                copy(l, k).wait_recv()


def halos_of(levels, feats):
    shapes = []
    for lv in levels:
        for way in WAYS:
            (_, nr), (_, nc) = source_of(lv, way)
            shapes.append(jax.ShapeDtypeStruct((nr, nc, lv.chan), BF16))
    hbm = pl.BlockSpec(memory_space=pl.ANY)
    return pl.pallas_call(
        functools.partial(exchange, levels),
        out_shape=shapes,
        in_specs=[hbm] * 4,
        out_specs=[hbm] * 32,
        scratch_shapes=[pltpu.SemaphoreType.DMA((32,))] * 2,
        compiler_params=pltpu.CompilerParams(collective_id=0, has_side_effects=True),
    )(*feats)


def chunking(length, most):
    n = -(-length // most)
    return n, up_to(-(-length // n), 16)


def body(levels, *refs):
    refs = list(refs)

    def take(n):
        out = refs[:n]
        del refs[:n]
        return out

    feats, halos = take(4), take(32)
    w0, w1, w2_hbm, w3_hbm = take(4)
    biases = take(4)
    up1, up2, up3, wd0, wd1a, wd1v, wd2_hbm = take(7)
    outs = take(4)
    xs, hs = take(4), take(4)
    spread, odd, cols2, cols3 = take(4)
    w2, w3, wd2 = take(3)
    t01, v0, t2, v1, u0, u1, u2 = take(7)
    (sems,) = take(1)
    l0, l1, l2, l3 = levels
    copies = [
        pltpu.make_async_copy(a, b, sems.at[i])
        for i, (a, b) in enumerate(((w2_hbm, w2), (w3_hbm, w3), (wd2_hbm, wd2)))
    ]
    for c in copies:
        c.start()

    ty, tx = lax.axis_index("ty"), lax.axis_index("tx")
    top, bottom = ty == 0, ty == lax.axis_size("ty") - 1
    left, right = tx == 0, tx == lax.axis_size("tx") - 1

    def lane(shape):
        return lax.broadcasted_iota(jnp.int32, shape, len(shape) - 1)

    def rows_loop(n, run):
        def step(i, _):
            run(i)
            return 0

        lax.fori_loop(0, n, step, 0)

    def put(l, at, value):
        lv = levels[l]
        for p in range(lv.planes):
            w = min(LANES, lv.chan - p * LANES)
            xs[l][p, pl.ds(at, value.shape[0]), 0:w] = value[:, p * LANES : p * LANES + w]

    for l, lv in enumerate(levels):
        xs[l][...] = jnp.zeros_like(xs[l])
    for ref in (v0, v1):
        ref[...] = jnp.zeros_like(ref)
    for l, lv in enumerate(levels):

        def place(source, row, col, l=l, lv=lv, skip=0, keep=None):
            def run(i):
                at = pl.multiple_of((i + row + lv.lead) * lv.pitch + col, 8)
                put(l, at + skip, source[i].astype(F32)[skip:keep])

            rows_loop(source.shape[0], run)

        place(feats[l], 0, 0)
        for k, way in enumerate(WAYS):
            dy, dx = way
            row = {0: 0, 1: -lv.low, -1: lv.rows}[dy]
            col, skip, keep = {0: (0, 0, None), 1: (-lv.near, lv.near - lv.low, None), -1: (lv.cols, 0, 2)}[dx]

            @pl.when(on_map(way, -1))
            def _(k=k, row=row, col=col, skip=skip, keep=keep):
                place(halos[8 * l + k], row, col, skip=skip, keep=keep)

    def blank(ref, lv, low, high):
        planes = ref.shape[0]

        def columns(col, n):
            start = lv.at(-low - 1)
            count = low + 1 + lv.rows + high
            for c in range(col, col + n):
                for p in range(planes):
                    ref[p, pl.ds(start + c, count, stride=lv.pitch), :] = jnp.zeros((count, LANES), F32)

        def rows(row, n):
            for p in range(planes):
                size = n * lv.pitch
                ref[p, pl.ds(lv.at(row) - lv.tail + 2, size), :] = jnp.zeros((size, LANES), F32)

        pl.when(left)(lambda: columns(lv.pitch - low, low))
        if high:
            pl.when(right)(lambda: columns(lv.cols, high))
            pl.when(bottom)(lambda: rows(lv.rows, high))

        pl.when(top)(lambda: rows(-low, low))

    def wide_conv(l, src, dst, weight, bias, span, residual):
        lv = levels[l]
        start, length = span
        n, m = chunking(length, 656)
        C = lv.chan

        def run(i):
            base = pl.multiple_of(start + i * m, 8)
            a, b, c = (
                src[0, pl.ds(pl.multiple_of(base - 8 + d * lv.pitch, 8), m + 16), :] for d in (-1, 0, 1)
            )
            if 3 * C <= 2 * LANES:
                ids = lane(a.shape)
                moved = pltpu.roll(c, 2 * C, 1)
                tile0 = a + pltpu.roll(b, C, 1) + jnp.where(ids >= 2 * C, moved, 0.0)
                tile1 = jnp.where(ids < 3 * C - LANES, moved, 0.0)
                lhs = jnp.concatenate([tile0.astype(BF16), tile1.astype(BF16)], axis=1)
            else:
                lhs = jnp.concatenate([a.astype(BF16), b.astype(BF16), c.astype(BF16)], axis=1)
            o = lax.dot_general(lhs, weight[...], NT, preferred_element_type=F32)
            for q in range(3):
                spread[q, 0 : m + 16, :] = o[:, q * LANES : (q + 1) * LANES]
            y = spread[0, 7 : 7 + m, :] + spread[1, 8 : 8 + m, :] + spread[2, 9 : 9 + m, :]
            y = y + bias
            if residual:
                y = y + dst[0, pl.ds(base, m), :]
            dst[0, pl.ds(base, m), :] = jnp.maximum(y, 0.0)

        rows_loop(n, run)

    def offset(lv, t):
        return (t // 3 - 1) * lv.pitch + t % 3 - 1

    def deep_conv2(src, dst, weight, bias, span, residual):
        lv = l2
        start, length = span
        m = up_to(length, 16)
        total = lv.total
        p0, p1 = src[0, :, :], src[1, :, :]
        ids = lane((total, LANES))
        r0, r1 = pltpu.roll(p0, 64, 1), pltpu.roll(p1, 64, 1)
        odd[0, :, :] = jnp.where(ids >= 64, r0, 0.0)
        odd[1, :, :] = jnp.where(ids < 64, r0, r1)

        def piece(ref, p, t):
            return ref[p, pl.ds(start + offset(lv, t), m), :]

        for t in range(0, 9, 2):
            k = 3 * (t // 2) * LANES
            cols2[0:m, k : k + 128] = piece(src, 0, t).astype(BF16)
            tile = piece(src, 1, t)
            if t == 8:
                cols2[0:m, k + 128 : k + 192] = tile[:, 0:64].astype(BF16)
            else:
                cols2[0:m, k + 128 : k + 256] = (tile + piece(odd, 0, t + 1)).astype(BF16)
                cols2[0:m, k + 256 : k + 384] = piece(odd, 1, t + 1).astype(BF16)
        y = lax.dot_general(cols2[0:m, :], weight, NT, preferred_element_type=F32) + bias[:, 0 : lv.chan]
        for p in range(2):
            w = min(LANES, lv.chan - p * LANES)
            part = y[:, p * LANES : p * LANES + w]
            if residual:
                part = part + dst[p, pl.ds(start, m), 0:w]
            dst[p, pl.ds(start, m), 0:w] = jnp.maximum(part, 0.0)

    def deep_conv3(src, dst, weight, bias, span, residual):
        lv = l3
        start, length = span
        m = up_to(length, 16)
        for t in range(9):
            for p in range(lv.planes):
                k = (t * lv.planes + p) * LANES
                cols3[0:m, k : k + LANES] = src[p, pl.ds(start + offset(lv, t), m), :].astype(BF16)
        y = lax.dot_general(cols3[0:m, :], weight, NT, preferred_element_type=F32) + bias
        for p in range(lv.planes):
            part = y[:, p * LANES : (p + 1) * LANES]
            if residual:
                part = part + dst[p, pl.ds(start, m), :]
            dst[p, pl.ds(start, m), :] = jnp.maximum(part, 0.0)

    for l in (0, 1):
        lv = levels[l]
        wide_conv(l, xs[l], hs[l], (w0, w1)[l].at[0], biases[l][0:1, :], lv.first(), False)
        blank(hs[l], lv, lv.rim + 1, 1)
        wide_conv(l, hs[l], xs[l], (w0, w1)[l].at[1], biases[l][1:2, :], lv.second(), True)
        blank(xs[l], lv, lv.rim, 0)

    hs[2][1, :, :] = jnp.zeros((l2.total, LANES), F32)
    copies[0].wait()
    deep_conv2(xs[2], hs[2], w2[0], biases[2][0:1, :], l2.first(), False)
    blank(hs[2], l2, l2.rim + 1, 1)
    deep_conv2(hs[2], xs[2], w2[1], biases[2][1:2, :], l2.second(), True)
    blank(xs[2], l2, l2.rim, 0)
    copies[1].wait()
    deep_conv3(xs[3], hs[3], w3[0], biases[3][0:1, :], l3.first(), False)
    blank(hs[3], l3, 1, 1)
    deep_conv3(hs[3], xs[3], w3[1], biases[3][1:2, :], l3.second(), True)

    def gathered(src, plane, big, small, i, t, width=None):
        width = small.pitch if width is None else width
        at = (2 * i + t // 3 - 1 + big.lead) * big.pitch + 2 * (small.cols - width) + t % 3 - 1
        return src[plane, pl.ds(at, width, stride=2), :]

    rim = RIMS[1]
    rows = up_to(rim + l1.rows, 4)

    def down0(k):
        i0 = l1.rows - rows + 4 * k
        taps = [
            jnp.concatenate([gathered(xs[0], 0, l0, l1, i0 + r, t) for r in range(4)], axis=0).astype(BF16)
            for t in range(9)
        ]
        o = lax.dot_general(jnp.concatenate(taps, axis=1), wd0[...], NT, preferred_element_type=F32)
        at = pl.multiple_of((i0 + l1.lead) * l1.pitch - l1.tail, 8)
        t01[0, pl.ds(at, 4 * l1.pitch), :] = o[:, 0:LANES]
        v0[0, pl.ds(at, 4 * l1.pitch), :] = jnp.maximum(o[:, LANES:], 0.0)

    rows_loop(rows // 4, down0)
    blank(v0, l1, rim, 0)

    rows = l2.rows + 2
    at = l2.at(-2) - l2.tail
    span = rows * l2.pitch

    def down1(src, weight):
        taps = [
            jnp.concatenate([gathered(src, 0, l1, l2, i, t) for i in range(-2, l2.rows)], axis=0).astype(BF16)
            for t in range(9)
        ]
        return lax.dot_general(jnp.concatenate(taps, axis=1), weight[...], NT, preferred_element_type=F32)

    o = down1(xs[1], wd1a)
    e = down1(v0, wd1v)
    second = o[:, LANES : 2 * LANES] + e[:, LANES : 2 * LANES]
    ids = lane(second.shape)
    t2[0, 0:span, :] = o[:, 0:LANES] + e[:, 0:LANES]
    t2[1, 0:span, :] = second
    v1[0, pl.ds(at, span), :] = jnp.where(ids >= 64, jnp.maximum(second, 0.0), 0.0)
    v1[1, pl.ds(at, span), :] = jnp.maximum(o[:, 2 * LANES :], 0.0)
    blank(v1, l2, 1, 0)
    taps = []
    for t in range(9):
        for p in range(3):
            parts = []
            for i in range(l3.rows):
                piece = gathered(xs[2] if p < 2 else v1, p if p < 2 else 1, l2, l3, i, t, l3.cols)
                if p == 1:
                    piece = piece + gathered(v1, 0, l2, l3, i, t, l3.cols)
                parts.append(piece)
            taps.append(jnp.concatenate(parts, axis=0).astype(BF16))
    copies[2].wait()
    t3 = lax.dot_general(jnp.concatenate(taps, axis=1), wd2[...], NN, preferred_element_type=F32)

    def center(l, i):
        lv = levels[l]
        parts = [xs[l][p, pl.ds(lv.at(i), lv.cols), :] for p in range(lv.planes)]
        return jnp.concatenate(parts, axis=1)[:, : lv.chan] if lv.planes > 1 else parts[0][:, : lv.chan]

    a3 = jnp.concatenate([center(3, i) for i in range(l3.rows)], axis=0)
    y3 = jnp.maximum(a3 + t3, 0.0).astype(BF16)
    for i in range(l3.rows):
        outs[3][i, :, :] = y3[i * l3.cols : (i + 1) * l3.cols, :]

    c0, c1, c2 = l0.chan, l1.chan, l2.chan
    a3 = a3.astype(BF16)
    up3_0 = lax.dot_general(a3, up3[0:c0, :], NT, preferred_element_type=F32)
    up3_1 = lax.dot_general(a3, up3[c0 : c0 + c1, :], NT, preferred_element_type=F32)
    up3_2 = lax.dot_general(a3, up3[c0 + c1 :, :], NT, preferred_element_type=F32)

    def enlarge(value, dst, plane, width, rows, cols):
        for i in range(rows):
            line = value[i * cols : (i + 1) * cols, :]
            for di in range(2):
                for dj in range(2):
                    base = (2 * i + di) * 2 * cols + dj
                    dst[plane, pl.ds(base, cols, stride=2), 0:width] = line

    enlarge(up3_0, u2, 0, c0, l3.rows, l3.cols)
    enlarge(up3_1, u2, 1, c1, l3.rows, l3.cols)
    enlarge(up3_2[:, 0:LANES], u2, 2, LANES, l3.rows, l3.cols)
    enlarge(up3_2[:, LANES:], u2, 3, c2 - LANES, l3.rows, l3.cols)
    a2 = jnp.concatenate([center(2, i) for i in range(l2.rows)], axis=0)
    a2b = a2.astype(BF16)
    up2_0 = lax.dot_general(a2b, up2[0:c0, :], NT, preferred_element_type=F32) + u2[0, :, 0:c0]
    up2_1 = lax.dot_general(a2b, up2[c0:, :], NT, preferred_element_type=F32) + u2[1, :, 0:c1]
    for i in range(l2.rows):
        for p in range(2):
            w = min(LANES, c2 - p * LANES)
            line = xs[2][p, pl.ds(l2.at(i), l2.cols), 0:w]
            line = line + t2[p, pl.ds((i + 2) * l2.pitch + l2.tail, l2.cols), 0:w]
            line = line + u2[2 + p, pl.ds(i * l2.cols, l2.cols), 0:w]
            outs[2][i, :, p * LANES : p * LANES + w] = jnp.maximum(line, 0.0).astype(BF16)
    enlarge(up2_0, u1, 0, c0, l2.rows, l2.cols)
    enlarge(up2_1, u1, 1, c1, l2.rows, l2.cols)

    def join1(k):
        lines = []
        for r in range(4):
            i = 4 * k + r
            at = pl.multiple_of((i + l1.lead) * l1.pitch, 8)
            line = xs[1][0, pl.ds(at, l1.cols), 0:c1]
            lines.append(line)
            total = line + t01[0, pl.ds(at, l1.cols), 0:c1]
            total = total + u1[1, pl.ds(pl.multiple_of(i * l1.cols, 8), l1.cols), 0:c1]
            outs[1][i, :, :] = jnp.maximum(total, 0.0).astype(BF16)
        a1 = jnp.concatenate(lines, axis=0).astype(BF16)
        n = 4 * l1.cols
        y = lax.dot_general(a1, up1[...], NT, preferred_element_type=F32)
        y = y + u1[0, pl.ds(pl.multiple_of(k * n, 8), n), 0:c0]
        for r in range(4):
            line = y[r * l1.cols : (r + 1) * l1.cols, :]
            for dj in range(2):
                u0[0, pl.ds(dj, l1.cols, stride=2), 0:c0] = line
            up = u0[0, 0 : l0.cols, 0:c0]
            for di in range(2):
                i = 2 * (4 * k + r) + di
                at = pl.multiple_of((i + l0.lead) * l0.pitch, 8)
                total = xs[0][0, pl.ds(at, l0.cols), 0:c0] + up
                outs[0][i, :, :] = jnp.maximum(total, 0.0).astype(BF16)

    rows_loop(l1.rows // 4, join1)


def spread_out(w, lanes):
    n = w.shape[0]
    w = w.reshape(n, 9, -1)
    return jnp.pad(w, ((0, 0), (0, 0), (0, lanes - w.shape[2])))


def tall(w, n):
    return jnp.pad(w, ((0, n - w.shape[0]),) + ((0, 0),) * (w.ndim - 1))


def per_device(*args):
    feats, weights, biases, rest = args[0:4], args[4:8], args[8:12], args[12:20]
    feats = [f.transpose(1, 2, 0) for f in feats]
    levels = [Level(l, f.shape) for l, f in enumerate(feats)]
    l0, l1, l2, l3 = levels
    c0, c1, c2, c3 = (lv.chan for lv in levels)
    halos = halos_of(levels, feats)
    up1, up2, up3, mid0, mid1, fin0, fin1, fin2 = (r[0] for r in rest)

    def wide(w, c, deep):
        w = w.reshape(2, c, 3, 3, c)
        if 3 * c > 2 * LANES:
            w = jnp.pad(w, ((0, 0),) * 4 + ((0, LANES - c),))
        w = jnp.pad(w, ((0, 0), (0, LANES - c)) + ((0, 0),) * 3)
        w = w.transpose(0, 3, 1, 2, 4).reshape(2, 3 * LANES, -1)
        return jnp.pad(w, ((0, 0), (0, 0), (0, deep - w.shape[2])))

    w0 = wide(weights[0], c0, 2 * LANES)
    w1 = wide(weights[1], c1, 3 * LANES)
    bs = [jnp.pad(b, ((0, 0), (0, up_to(b.shape[1], LANES) - b.shape[1]))) for b in biases]
    wd0 = jnp.concatenate(
        [
            tall(spread_out(fin0[:c1], LANES), LANES),
            tall(spread_out(mid0[0:2].reshape(2 * c0, -1), LANES), LANES),
        ]
    ).reshape(2 * LANES, -1)
    wd1a = jnp.concatenate(
        [tall(spread_out(fin1[:c2], LANES), 2 * LANES), tall(spread_out(mid1[0], LANES), LANES)]
    ).reshape(3 * LANES, -1)
    late = jnp.pad(spread_out(mid0[2], c0), ((0, 0), (0, 0), (c0, 0)))
    wd1v = tall(
        jnp.concatenate([spread_out(fin0[c1 : c1 + c2], 2 * c0), late]), 2 * LANES
    )
    wd1v = jnp.pad(wd1v, ((0, 0), (0, 0), (0, LANES - 2 * c0))).reshape(2 * LANES, -1)

    def deep(w, pad):
        w = w.T.reshape(9, -1, c3)
        return jnp.pad(w, ((0, 0), (0, pad - w.shape[1]), (0, 0)))

    wd2 = jnp.concatenate(
        [deep(fin2, c2), deep(fin0[c1 + c2 :], 64), deep(fin1[c2:], LANES)], axis=1
    ).reshape(-1, c3)

    vmem, any_ = pl.BlockSpec(memory_space=pltpu.VMEM), pl.BlockSpec(memory_space=pl.ANY)
    V = pltpu.VMEM
    maps = [V((lv.planes, lv.total, LANES), F32) for lv in levels]
    m2, m3 = up_to(l2.first()[1], 16), up_to(l3.first()[1], 16)
    n1 = max(chunking(s[1], 656)[1] for lv in levels[:2] for s in (lv.first(), lv.second()))
    scratch = maps * 2 + [
        V((3, n1 + 16, LANES), F32),
        V((2, l2.total, LANES), F32),
        V((m2, 9 * c2), BF16),
        V((m3, 9 * c3), BF16),
        V(weights[2].shape, BF16),
        V(weights[3].shape, BF16),
        V(wd2.shape, BF16),
        V((1, l1.total, LANES), F32),
        V((1, l1.total, LANES), F32),
        V((2, (l2.rows + 2) * l2.pitch, LANES), F32),
        V((2, l2.total, LANES), F32),
        V((1, l0.cols, LANES), F32),
        V((2, l1.rows * l1.cols, LANES), F32),
        V((4, l2.rows * l2.cols, LANES), F32),
        pltpu.SemaphoreType.DMA((3,)),
    ]
    outs = pl.pallas_call(
        functools.partial(body, levels),
        out_shape=[jax.ShapeDtypeStruct(f.shape, BF16) for f in feats],
        in_specs=[vmem] * 36 + [vmem] * 2 + [any_] * 2 + [vmem] * 4 + [vmem] * 6 + [any_],
        out_specs=[vmem] * 4,
        scratch_shapes=scratch,
        compiler_params=pltpu.CompilerParams(vmem_limit_bytes=60 * 2**20),
    )(*feats, *halos, w0, w1, weights[2], weights[3], *bs, up1, up2, up3, wd0, wd1a, wd1v, wd2)
    return tuple(o.transpose(2, 0, 1) for o in outs)


def solution(mesh):
    tiled = P(None, "ty", "tx")
    return jax.shard_map(
        per_device,
        mesh=mesh,
        in_specs=(tiled,) * 4 + (P(),) * 16,
        out_specs=(tiled,) * 4,
        check_vma=False,
    )
```

```python
import functools

import jax
import jax.numpy as jnp
from jax import lax
from jax.experimental import pallas as pl
from jax.experimental.pallas import tpu as pltpu
from jax.sharding import PartitionSpec as P

RIMS = (7, 3, 1, 0)
LANES = 128
NT = (((1,), (1,)), ((), ()))
NN = (((1,), (0,)), ((), ()))
WAYS = [(dy, dx) for dy in (-1, 0, 1) for dx in (-1, 0, 1) if dy or dx]
F32, BF16 = jnp.float32, jnp.bfloat16


def up_to(n, m):
    return -(-n // m) * m


class Level:
    def __init__(self, level, shape):
        self.rows, self.cols, self.chan = shape
        self.rim = RIMS[level]
        self.low = self.rim + 2
        self.pitch = up_to(self.cols + 2 + self.low, 8)
        self.lead = self.low + 1
        self.tail = self.pitch - self.cols
        self.planes = up_to(self.chan, LANES) // LANES
        self.near = up_to(self.low, 8)
        self.total = (self.lead + self.rows + 4) * self.pitch

    def at(self, row, col=0):
        return (row + self.lead) * self.pitch + col

    def first(self):
        start = self.at(-self.rim - 1) - self.tail
        return start, self.at(self.rows) + self.cols + 8 - start

    def second(self):
        start = self.at(-self.rim) - self.tail
        return start, self.at(self.rows - 1) + self.cols - start


def source_of(lv, way):
    dy, dx = way
    rows = (0, lv.rows) if dy == 0 else ((lv.rows - lv.low, lv.low) if dy > 0 else (0, 2))
    cols = (0, lv.cols) if dx == 0 else ((lv.cols - lv.near, lv.near) if dx > 0 else (0, 8))
    return rows, cols


def on_map(way, side):
    ok = True
    for step, axis in zip(way, ("ty", "tx")):
        if step:
            place = lax.axis_index(axis) + side * step
            ok = ok & (place >= 0) & (place < lax.axis_size(axis))
    return ok


def exchange(levels, *refs):
    feats, outs, (send, recv) = refs[:4], refs[4:36], refs[36:]
    here = {a: lax.axis_index(a) for a in ("ty", "tx")}
    barrier = pltpu.get_barrier_semaphore()

    def there(way):
        return {"ty": here["ty"] + way[0], "tx": here["tx"] + way[1]}

    count = 0
    for way in WAYS:
        ok = on_map(way, 1)

        @pl.when(ok)
        def _(way=way):
            pl.semaphore_signal(barrier, 1, device_id=there(way))

        count = count + jnp.where(ok, 1, 0)
    pl.semaphore_wait(barrier, count)

    def copy(l, k):
        way = WAYS[k]
        (r, nr), (c, nc) = source_of(levels[l], way)
        return pltpu.make_async_remote_copy(
            feats[l].at[pl.ds(r, nr), pl.ds(c, nc)],
            outs[8 * l + k],
            send.at[8 * l + k],
            recv.at[8 * l + k],
            device_id=there(way),
        )

    for k, way in enumerate(WAYS):

        @pl.when(on_map(way, 1))
        def _(k=k):
            for l in range(4):
                copy(l, k).start()

    for k, way in enumerate(WAYS):

        @pl.when(on_map(way, 1))
        def _(k=k):
            for l in range(4):
                copy(l, k).wait_send()

        @pl.when(on_map(way, -1))
        def _(k=k):
            for l in range(4):
                copy(l, k).wait_recv()


def halos_of(levels, feats):
    shapes = []
    for lv in levels:
        for way in WAYS:
            (_, nr), (_, nc) = source_of(lv, way)
            shapes.append(jax.ShapeDtypeStruct((nr, nc, lv.chan), BF16))
    hbm = pl.BlockSpec(memory_space=pl.ANY)
    return pl.pallas_call(
        functools.partial(exchange, levels),
        out_shape=shapes,
        in_specs=[hbm] * 4,
        out_specs=[hbm] * 32,
        scratch_shapes=[pltpu.SemaphoreType.DMA((32,))] * 2,
        compiler_params=pltpu.CompilerParams(collective_id=0, has_side_effects=True),
    )(*feats)


def chunking(length, most):
    n = -(-length // most)
    return n, up_to(-(-length // n), 16)


def prepare(levels, given, made, stage):
    w0_in, w1_in, mid0, mid1, fin0, fin1 = given
    w0, w1, wd0, wd1a, wd1v, wd2, wd2v = made
    c0, c1, c2, c3 = (lv.chan for lv in levels)

    def shifted(row, n, off, width, to):
        k, s = divmod(off, LANES)
        a = stage[row : row + n, k * LANES : (k + 1) * LANES]
        ids = lax.broadcasted_iota(jnp.int32, a.shape, 1)
        if s + width > LANES:
            a = jnp.where(ids >= s, a, stage[row : row + n, (k + 1) * LANES : (k + 2) * LANES])
        if (to - s) % LANES:
            a = pltpu.roll(a, (to - s) % LANES, 1)
        if width == LANES:
            return a
        return jnp.where((ids >= to) & (ids < to + width), a, 0.0)

    def fill(value):
        n, k = value.shape
        stage[0:n, 0:k] = value.astype(F32)

    for i in range(2):
        fill(w0_in[i])
        for q in range(3):
            offs = [c0 * (3 * p + q) for p in range(3)]
            cut = LANES - 2 * c0
            tile = shifted(0, c0, offs[0], c0, 0) + shifted(0, c0, offs[1], c0, c0)
            tile = tile + shifted(0, c0, offs[2], cut, 2 * c0)
            w0[i, q * LANES : q * LANES + c0, 0:LANES] = tile.astype(BF16)
            tile = shifted(0, c0, offs[2] + cut, c0 - cut, 0)
            w0[i, q * LANES : q * LANES + c0, LANES : 2 * LANES] = tile.astype(BF16)
        fill(w1_in[i])
        for q in range(3):
            for p in range(3):
                tile = shifted(0, c1, c1 * (3 * p + q), c1, 0)
                w1[i, q * LANES : q * LANES + c1, p * LANES : (p + 1) * LANES] = tile.astype(BF16)

    def apart(value, to, row):
        fill(value)
        for t in range(9):
            to[row : row + c1, t * LANES : (t + 1) * LANES] = shifted(0, c1, c1 * t, c1, 0).astype(BF16)

    for k in range(c2 // c1):
        apart(fin1[0, k * c1 : (k + 1) * c1, :], wd1a, k * c1)
    apart(mid1[0, 0], wd1a, 2 * LANES)
    for k in range(c3 // c1):
        apart(fin1[0, c2 + k * c1 : c2 + (k + 1) * c1, :], wd2v, k * c1)

    tall = up_to(9 * c0, LANES)

    def turned():
        return stage[0:LANES, 0:tall].T.astype(BF16)

    stage[0:LANES, 0:tall] = jnp.zeros((LANES, tall), F32)
    for k in range(2):
        stage[k * c0 : (k + 1) * c0, 0 : 9 * c0] = mid0[0, k].astype(F32)
    flat = turned()
    for t in range(9):
        wd0[t * LANES : t * LANES + c0, LANES : 2 * LANES] = flat[t * c0 : (t + 1) * c0, :]
        wd0[t * LANES : t * LANES + c0, 0:LANES] = fin0[t * c0 : (t + 1) * c0, 0:LANES]
    stage[0:LANES, 0:tall] = jnp.zeros((LANES, tall), F32)
    stage[c2 - LANES : c2 - LANES + c0, 0 : 9 * c0] = mid0[0, 2].astype(F32)
    flat = turned()
    for t in range(9):
        wd1v[t * LANES + c0 : t * LANES + 2 * c0, LANES : 2 * LANES] = flat[t * c0 : (t + 1) * c0, :]
    fill(fin0[...])
    depth = wd2.shape[0] // 9
    for t in range(9):
        wd1v[t * LANES : t * LANES + c0, 0:LANES] = shifted(t * c0, c0, c1, LANES, 0).astype(BF16)
        tile = shifted(t * c0, c0, c1 + LANES, c2 - LANES, 0)
        wd1v[t * LANES : t * LANES + c0, LANES : 2 * LANES] = tile.astype(BF16)
        row = t * depth + c2
        wd2[row : row + depth - c2, :] = jnp.zeros((depth - c2, c3), BF16)
        for j in range(c3 // LANES):
            tile = shifted(t * c0, c0, c1 + c2 + j * LANES, LANES, 0)
            wd2[row : row + c0, j * LANES : (j + 1) * LANES] = tile.astype(BF16)


def body(levels, *refs):
    refs = list(refs)

    def take(n):
        out = refs[:n]
        del refs[:n]
        return out

    feats, halos = take(4), take(32)
    w0_in, w1_in, w2_hbm, w3_hbm = take(4)
    biases = take(4)
    up1, up2, up3, mid0, mid1, fin0, fin1, fin2_hbm = take(8)
    outs = take(4)
    xs, hs = take(4), take(4)
    spread, odd, cols2, cols3 = take(4)
    w2, w3 = take(2)
    w0, w1, wd0, wd1a, wd1v, wd2, wd2v, stage, bpad = take(9)
    t01, v0, t2, v1, u0, u1, u2 = take(7)
    (sems,) = take(1)
    l0, l1, l2, l3 = levels
    copies = [pltpu.make_async_copy(a, b, sems.at[i]) for i, (a, b) in enumerate(((w2_hbm, w2), (w3_hbm, w3)))]
    depth = wd2.shape[0] // 9
    for ref in (w0, w1, wd0, wd1a, wd1v, bpad):
        ref[...] = jnp.zeros_like(ref)
    fin2_copies = [
        pltpu.make_async_copy(
            fin2_hbm.at[pl.ds(t * l2.chan, l2.chan)], wd2.at[pl.ds(t * depth, l2.chan)], sems.at[2 + t]
        )
        for t in range(9)
    ]
    for c in copies + fin2_copies:
        c.start()

    prepare(levels, (w0_in, w1_in, mid0, mid1, fin0, fin1), (w0, w1, wd0, wd1a, wd1v, wd2, wd2v), stage)
    for l in (0, 1):
        bpad[l, 0:2, 0 : levels[l].chan] = biases[l][...]

    ty, tx = lax.axis_index("ty"), lax.axis_index("tx")
    top, bottom = ty == 0, ty == lax.axis_size("ty") - 1
    left, right = tx == 0, tx == lax.axis_size("tx") - 1

    def lane(shape):
        return lax.broadcasted_iota(jnp.int32, shape, len(shape) - 1)

    def rows_loop(n, run):
        def step(i, _):
            run(i)
            return 0

        lax.fori_loop(0, n, step, 0)

    def put(l, at, value):
        lv = levels[l]
        for p in range(lv.planes):
            w = min(LANES, lv.chan - p * LANES)
            xs[l][p, pl.ds(at, value.shape[0]), 0:w] = value[:, p * LANES : p * LANES + w]

    for l, lv in enumerate(levels):
        xs[l][...] = jnp.zeros_like(xs[l])
    for ref in (v0, v1):
        ref[...] = jnp.zeros_like(ref)
    for l, lv in enumerate(levels):

        def place(source, row, col, l=l, lv=lv, skip=0, keep=None):
            def run(i):
                at = pl.multiple_of((i + row + lv.lead) * lv.pitch + col, 8)
                put(l, at + skip, source[i].astype(F32)[skip:keep])

            rows_loop(source.shape[0], run)

        place(feats[l], 0, 0)
        for k, way in enumerate(WAYS):
            dy, dx = way
            row = {0: 0, 1: -lv.low, -1: lv.rows}[dy]
            col, skip, keep = {0: (0, 0, None), 1: (-lv.near, lv.near - lv.low, None), -1: (lv.cols, 0, 2)}[dx]

            @pl.when(on_map(way, -1))
            def _(k=k, row=row, col=col, skip=skip, keep=keep):
                place(halos[8 * l + k], row, col, skip=skip, keep=keep)

    def blank(ref, lv, low, high):
        planes = ref.shape[0]

        def columns(col, n):
            start = lv.at(-low - 1)
            count = low + 1 + lv.rows + high
            for c in range(col, col + n):
                for p in range(planes):
                    ref[p, pl.ds(start + c, count, stride=lv.pitch), :] = jnp.zeros((count, LANES), F32)

        def rows(row, n):
            for p in range(planes):
                size = n * lv.pitch
                ref[p, pl.ds(lv.at(row) - lv.tail + 2, size), :] = jnp.zeros((size, LANES), F32)

        pl.when(left)(lambda: columns(lv.pitch - low, low))
        if high:
            pl.when(right)(lambda: columns(lv.cols, high))
            pl.when(bottom)(lambda: rows(lv.rows, high))

        pl.when(top)(lambda: rows(-low, low))

    def wide_conv(l, src, dst, weight, bias, span, residual):
        lv = levels[l]
        start, length = span
        n, m = chunking(length, 656)
        C = lv.chan

        def run(i):
            base = pl.multiple_of(start + i * m, 8)
            a, b, c = (
                src[0, pl.ds(pl.multiple_of(base - 8 + d * lv.pitch, 8), m + 16), :] for d in (-1, 0, 1)
            )
            if 3 * C <= 2 * LANES:
                ids = lane(a.shape)
                moved = pltpu.roll(c, 2 * C, 1)
                tile0 = a + pltpu.roll(b, C, 1) + jnp.where(ids >= 2 * C, moved, 0.0)
                tile1 = jnp.where(ids < 3 * C - LANES, moved, 0.0)
                lhs = jnp.concatenate([tile0.astype(BF16), tile1.astype(BF16)], axis=1)
            else:
                lhs = jnp.concatenate([a.astype(BF16), b.astype(BF16), c.astype(BF16)], axis=1)
            o = lax.dot_general(lhs, weight[...], NT, preferred_element_type=F32)
            for q in range(3):
                spread[q, 0 : m + 16, :] = o[:, q * LANES : (q + 1) * LANES]
            y = spread[0, 7 : 7 + m, :] + spread[1, 8 : 8 + m, :] + spread[2, 9 : 9 + m, :]
            y = y + bias
            if residual:
                y = y + dst[0, pl.ds(base, m), :]
            dst[0, pl.ds(base, m), :] = jnp.maximum(y, 0.0)

        rows_loop(n, run)

    def offset(lv, t):
        return (t // 3 - 1) * lv.pitch + t % 3 - 1

    def deep_conv2(src, dst, weight, bias, span, residual):
        lv = l2
        start, length = span
        m = up_to(length, 16)
        total = lv.total
        p0, p1 = src[0, :, :], src[1, :, :]
        ids = lane((total, LANES))
        r0, r1 = pltpu.roll(p0, 64, 1), pltpu.roll(p1, 64, 1)
        odd[0, :, :] = jnp.where(ids >= 64, r0, 0.0)
        odd[1, :, :] = jnp.where(ids < 64, r0, r1)

        def piece(ref, p, t):
            return ref[p, pl.ds(start + offset(lv, t), m), :]

        for t in range(0, 9, 2):
            k = 3 * (t // 2) * LANES
            cols2[0:m, k : k + 128] = piece(src, 0, t).astype(BF16)
            tile = piece(src, 1, t)
            if t == 8:
                cols2[0:m, k + 128 : k + 192] = tile[:, 0:64].astype(BF16)
            else:
                cols2[0:m, k + 128 : k + 256] = (tile + piece(odd, 0, t + 1)).astype(BF16)
                cols2[0:m, k + 256 : k + 384] = piece(odd, 1, t + 1).astype(BF16)
        y = lax.dot_general(cols2[0:m, :], weight, NT, preferred_element_type=F32) + bias
        for p in range(2):
            w = min(LANES, lv.chan - p * LANES)
            part = y[:, p * LANES : p * LANES + w]
            if residual:
                part = part + dst[p, pl.ds(start, m), 0:w]
            dst[p, pl.ds(start, m), 0:w] = jnp.maximum(part, 0.0)

    def deep_conv3(src, dst, weight, bias, span, residual):
        lv = l3
        start, length = span
        m = up_to(length, 16)
        for t in range(9):
            for p in range(lv.planes):
                k = (t * lv.planes + p) * LANES
                cols3[0:m, k : k + LANES] = src[p, pl.ds(start + offset(lv, t), m), :].astype(BF16)
        y = lax.dot_general(cols3[0:m, :], weight, NT, preferred_element_type=F32) + bias
        for p in range(lv.planes):
            part = y[:, p * LANES : (p + 1) * LANES]
            if residual:
                part = part + dst[p, pl.ds(start, m), :]
            dst[p, pl.ds(start, m), :] = jnp.maximum(part, 0.0)

    for l in (0, 1):
        lv = levels[l]
        wide_conv(l, xs[l], hs[l], (w0, w1)[l].at[0], bpad[l, 0:1, :], lv.first(), False)
        blank(hs[l], lv, lv.rim + 1, 1)
        wide_conv(l, hs[l], xs[l], (w0, w1)[l].at[1], bpad[l, 1:2, :], lv.second(), True)
        blank(xs[l], lv, lv.rim, 0)

    hs[2][1, :, :] = jnp.zeros((l2.total, LANES), F32)
    copies[0].wait()
    deep_conv2(xs[2], hs[2], w2[0], biases[2][0:1, :], l2.first(), False)
    blank(hs[2], l2, l2.rim + 1, 1)
    deep_conv2(hs[2], xs[2], w2[1], biases[2][1:2, :], l2.second(), True)
    blank(xs[2], l2, l2.rim, 0)
    copies[1].wait()
    deep_conv3(xs[3], hs[3], w3[0], biases[3][0:1, :], l3.first(), False)
    blank(hs[3], l3, 1, 1)
    deep_conv3(hs[3], xs[3], w3[1], biases[3][1:2, :], l3.second(), True)

    def gathered(src, plane, big, small, i, t, width=None):
        width = small.pitch if width is None else width
        at = (2 * i + t // 3 - 1 + big.lead) * big.pitch + 2 * (small.cols - width) + t % 3 - 1
        return src[plane, pl.ds(at, width, stride=2), :]

    rim = RIMS[1]
    rows = up_to(rim + l1.rows, 4)

    def down0(k):
        i0 = l1.rows - rows + 4 * k
        taps = [
            jnp.concatenate([gathered(xs[0], 0, l0, l1, i0 + r, t) for r in range(4)], axis=0).astype(BF16)
            for t in range(9)
        ]
        o = lax.dot_general(jnp.concatenate(taps, axis=1), wd0[...], NN, preferred_element_type=F32)
        at = pl.multiple_of((i0 + l1.lead) * l1.pitch - l1.tail, 8)
        t01[0, pl.ds(at, 4 * l1.pitch), :] = o[:, 0:LANES]
        v0[0, pl.ds(at, 4 * l1.pitch), :] = jnp.maximum(o[:, LANES:], 0.0)

    rows_loop(rows // 4, down0)
    blank(v0, l1, rim, 0)

    rows = l2.rows + 2
    at = l2.at(-2) - l2.tail
    span = rows * l2.pitch

    def down1(src, weight, form):
        taps = [
            jnp.concatenate([gathered(src, 0, l1, l2, i, t) for i in range(-2, l2.rows)], axis=0).astype(BF16)
            for t in range(9)
        ]
        return lax.dot_general(jnp.concatenate(taps, axis=1), weight[...], form, preferred_element_type=F32)

    o = down1(xs[1], wd1a, NT)
    e = down1(v0, wd1v, NN)
    second = o[:, LANES : 2 * LANES] + e[:, LANES : 2 * LANES]
    ids = lane(second.shape)
    t2[0, 0:span, :] = o[:, 0:LANES] + e[:, 0:LANES]
    t2[1, 0:span, :] = second
    v1[0, pl.ds(at, span), :] = jnp.where(ids >= 64, jnp.maximum(second, 0.0), 0.0)
    v1[1, pl.ds(at, span), :] = jnp.maximum(o[:, 2 * LANES :], 0.0)
    blank(v1, l2, 1, 0)
    def tap3(p, t):
        parts = []
        for i in range(l3.rows):
            piece = gathered(xs[2] if p < 2 else v1, p if p < 2 else 1, l2, l3, i, t, l3.cols)
            if p == 1:
                piece = piece + gathered(v1, 0, l2, l3, i, t, l3.cols)
            parts.append(piece)
        return jnp.concatenate(parts, axis=0).astype(BF16)

    taps = jnp.concatenate([tap3(2, t) for t in range(9)], axis=1)
    t3 = lax.dot_general(taps, wd2v[...], NT, preferred_element_type=F32)
    taps = jnp.concatenate([tap3(p, t) for t in range(9) for p in range(2)], axis=1)
    for c in fin2_copies:
        c.wait()
    t3 = t3 + lax.dot_general(taps, wd2[...], NN, preferred_element_type=F32)

    def center(l, i):
        lv = levels[l]
        parts = [xs[l][p, pl.ds(lv.at(i), lv.cols), :] for p in range(lv.planes)]
        return jnp.concatenate(parts, axis=1)[:, : lv.chan] if lv.planes > 1 else parts[0][:, : lv.chan]

    a3 = jnp.concatenate([center(3, i) for i in range(l3.rows)], axis=0)
    y3 = jnp.maximum(a3 + t3, 0.0).astype(BF16)
    for i in range(l3.rows):
        outs[3][i, :, :] = y3[i * l3.cols : (i + 1) * l3.cols, :]

    c0, c1, c2 = l0.chan, l1.chan, l2.chan
    a3 = a3.astype(BF16)
    up3_0 = lax.dot_general(a3, up3[0, 0:c0, :], NT, preferred_element_type=F32)
    up3_1 = lax.dot_general(a3, up3[0, c0 : c0 + c1, :], NT, preferred_element_type=F32)
    up3_2 = lax.dot_general(a3, up3[0, c0 + c1 :, :], NT, preferred_element_type=F32)

    def enlarge(value, dst, plane, width, rows, cols):
        for i in range(rows):
            line = value[i * cols : (i + 1) * cols, :]
            for di in range(2):
                for dj in range(2):
                    base = (2 * i + di) * 2 * cols + dj
                    dst[plane, pl.ds(base, cols, stride=2), 0:width] = line

    enlarge(up3_0, u2, 0, c0, l3.rows, l3.cols)
    enlarge(up3_1, u2, 1, c1, l3.rows, l3.cols)
    enlarge(up3_2[:, 0:LANES], u2, 2, LANES, l3.rows, l3.cols)
    enlarge(up3_2[:, LANES:], u2, 3, c2 - LANES, l3.rows, l3.cols)
    a2 = jnp.concatenate([center(2, i) for i in range(l2.rows)], axis=0)
    a2b = a2.astype(BF16)
    up2_0 = lax.dot_general(a2b, up2[0, 0:c0, :], NT, preferred_element_type=F32) + u2[0, :, 0:c0]
    up2_1 = lax.dot_general(a2b, up2[0, c0:, :], NT, preferred_element_type=F32) + u2[1, :, 0:c1]
    for i in range(l2.rows):
        for p in range(2):
            w = min(LANES, c2 - p * LANES)
            line = xs[2][p, pl.ds(l2.at(i), l2.cols), 0:w]
            line = line + t2[p, pl.ds((i + 2) * l2.pitch + l2.tail, l2.cols), 0:w]
            line = line + u2[2 + p, pl.ds(i * l2.cols, l2.cols), 0:w]
            outs[2][i, :, p * LANES : p * LANES + w] = jnp.maximum(line, 0.0).astype(BF16)
    enlarge(up2_0, u1, 0, c0, l2.rows, l2.cols)
    enlarge(up2_1, u1, 1, c1, l2.rows, l2.cols)

    def join1(k):
        lines = []
        for r in range(4):
            i = 4 * k + r
            at = pl.multiple_of((i + l1.lead) * l1.pitch, 8)
            line = xs[1][0, pl.ds(at, l1.cols), 0:c1]
            lines.append(line)
            total = line + t01[0, pl.ds(at, l1.cols), 0:c1]
            total = total + u1[1, pl.ds(pl.multiple_of(i * l1.cols, 8), l1.cols), 0:c1]
            outs[1][i, :, :] = jnp.maximum(total, 0.0).astype(BF16)
        a1 = jnp.concatenate(lines, axis=0).astype(BF16)
        n = 4 * l1.cols
        y = lax.dot_general(a1, up1[0], NT, preferred_element_type=F32)
        y = y + u1[0, pl.ds(pl.multiple_of(k * n, 8), n), 0:c0]
        for r in range(4):
            line = y[r * l1.cols : (r + 1) * l1.cols, :]
            for dj in range(2):
                u0[0, pl.ds(dj, l1.cols, stride=2), 0:c0] = line
            up = u0[0, 0 : l0.cols, 0:c0]
            for di in range(2):
                i = 2 * (4 * k + r) + di
                at = pl.multiple_of((i + l0.lead) * l0.pitch, 8)
                total = xs[0][0, pl.ds(at, l0.cols), 0:c0] + up
                outs[0][i, :, :] = jnp.maximum(total, 0.0).astype(BF16)

    rows_loop(l1.rows // 4, join1)


def per_device(*args):
    feats, weights, biases, rest = args[0:4], args[4:8], args[8:12], args[12:20]
    feats = [f.transpose(1, 2, 0) for f in feats]
    levels = [Level(l, f.shape) for l, f in enumerate(feats)]
    l0, l1, l2, l3 = levels
    c0, c1, c2, c3 = (lv.chan for lv in levels)
    halos = halos_of(levels, feats)
    up1, up2, up3, mid0, mid1, fin0, fin1, fin2 = rest
    fin0, fin2 = fin0[0].T, fin2[0].T
    vmem, any_ = pl.BlockSpec(memory_space=pltpu.VMEM), pl.BlockSpec(memory_space=pl.ANY)
    V = pltpu.VMEM
    maps = [V((lv.planes, lv.total, LANES), F32) for lv in levels]
    m2, m3 = up_to(l2.first()[1], 16), up_to(l3.first()[1], 16)
    n1 = max(chunking(s[1], 656)[1] for lv in levels[:2] for s in (lv.first(), lv.second()))
    scratch = maps * 2 + [
        V((3, n1 + 16, LANES), F32),
        V((2, l2.total, LANES), F32),
        V((m2, 9 * c2), BF16),
        V((m3, 9 * c3), BF16),
        V(weights[2].shape, BF16),
        V(weights[3].shape, BF16),
        V((2, 3 * LANES, 2 * LANES), BF16),
        V((2, 3 * LANES, 3 * LANES), BF16),
        V((9 * LANES, 2 * LANES), BF16),
        V((3 * LANES, 9 * LANES), BF16),
        V((9 * LANES, 2 * LANES), BF16),
        V((9 * up_to(c2, LANES), c3), BF16),
        V((c3, 9 * LANES), BF16),
        V((up_to(9 * c0, 8), up_to(max(9 * c1, fin0.shape[1]), LANES) + LANES), F32),
        V((2, 8, LANES), F32),
        V((1, l1.total, LANES), F32),
        V((1, l1.total, LANES), F32),
        V((2, (l2.rows + 2) * l2.pitch, LANES), F32),
        V((2, l2.total, LANES), F32),
        V((1, l0.cols, LANES), F32),
        V((2, l1.rows * l1.cols, LANES), F32),
        V((4, l2.rows * l2.cols, LANES), F32),
        pltpu.SemaphoreType.DMA((11,)),
    ]
    outs = pl.pallas_call(
        functools.partial(body, levels),
        out_shape=[jax.ShapeDtypeStruct(f.shape, BF16) for f in feats],
        in_specs=[vmem] * 38 + [any_] * 2 + [vmem] * 11 + [any_],
        out_specs=[vmem] * 4,
        scratch_shapes=scratch,
        compiler_params=pltpu.CompilerParams(vmem_limit_bytes=60 * 2**20),
    )(*feats, *halos, *weights, *biases, up1, up2, up3, mid0, mid1, fin0, fin1, fin2)
    return tuple(o.transpose(2, 0, 1) for o in outs)


def solution(mesh):
    tiled = P(None, "ty", "tx")
    return jax.shard_map(
        per_device,
        mesh=mesh,
        in_specs=(tiled,) * 4 + (P(),) * 16,
        out_specs=(tiled,) * 4,
        check_vma=False,
    )
```

```python
import functools

import jax
import jax.numpy as jnp
from jax import lax
from jax.experimental import pallas as pl
from jax.experimental.pallas import tpu as pltpu
from jax.sharding import PartitionSpec as P

RIMS = (7, 3, 1, 0)
LANES = 128
NT = (((1,), (1,)), ((), ()))
NN = (((1,), (0,)), ((), ()))
WAYS = [(dy, dx) for dy in (-1, 0, 1) for dx in (-1, 0, 1) if dy or dx]
F32, BF16 = jnp.float32, jnp.bfloat16


def up_to(n, m):
    return -(-n // m) * m


class Level:
    def __init__(self, level, shape):
        self.rows, self.cols, self.chan = shape
        self.rim = RIMS[level]
        self.low = self.rim + 2
        self.pitch = up_to(self.cols + 2 + self.low, 8)
        self.lead = self.low + 1
        self.tail = self.pitch - self.cols
        self.planes = up_to(self.chan, LANES) // LANES
        self.near = up_to(self.low, 8)
        self.total = (self.lead + self.rows + 4) * self.pitch
        self.folds = 2 if 2 * self.chan <= LANES else 1
        self.lines = self.rows // self.folds
        self.wide = LANES if self.folds == 2 else self.chan

    def at(self, row, col=0):
        return (row + self.lead) * self.pitch + col

    def first(self):
        start = self.at(-self.rim - 1) - self.tail
        return start, self.at(self.rows) + self.cols + 8 - start

    def second(self):
        start = self.at(-self.rim) - self.tail
        return start, self.at(self.rows - 1) + self.cols - start


def window(lv, way):
    lines = lv.lines
    if way[0] == 0:
        return 0, lines
    return (lines - lv.near, lv.near) if way[0] > 0 else (0, 8)


def message(lv, way):
    dy, dx = way
    if dx == 0:
        rows = lv.low if dy > 0 else 2
        return (rows, lv.cols // lv.folds, lv.wide)
    return (lv.low if dx > 0 else 2, window(lv, way)[1], lv.wide)


def on_map(way, side):
    ok = True
    for step, axis in zip(way, ("ty", "tx")):
        if step:
            place = lax.axis_index(axis) + side * step
            ok = ok & (place >= 0) & (place < lax.axis_size(axis))
    return ok


def exchange(levels, *refs):
    feats, outs, turned = refs[:4], refs[4:36], refs[36]
    rows_sent, cols_sent = refs[37:39], refs[39:47]
    stage, maps, side, send, recv = refs[47:]
    here = {a: lax.axis_index(a) for a in ("ty", "tx")}
    barrier = pltpu.get_barrier_semaphore()
    l0 = levels[0]

    def there(way):
        return {"ty": here["ty"] + way[0], "tx": here["tx"] + way[1]}

    count = 0
    for way in WAYS:
        ok = on_map(way, 1)

        @pl.when(ok)
        def _(way=way):
            pl.semaphore_signal(barrier, 1, device_id=there(way))

        count = count + jnp.where(ok, 1, 0)

    C, R, W = l0.chan, l0.rows, l0.cols

    def load(i, _):
        stage[pl.ds(pl.multiple_of(i * R, 8), R), :] = feats[0][i].astype(F32)
        return 0

    lax.fori_loop(0, C, load, 0)

    def turn(r, _):
        value = stage[pl.ds(r, C, stride=R), :].T
        maps[pl.ds(pl.multiple_of(r * W, 8), W), 0:C] = value
        turned[r] = value.astype(BF16)
        return 0

    lax.fori_loop(0, R, turn, 0)

    def folded(a, b):
        ids = lax.broadcasted_iota(jnp.int32, a.shape, 1)
        a, b = jnp.where(ids < C, a, 0.0), jnp.where(ids < C, b, 0.0)
        return (a + pltpu.roll(b, LANES // 2, 1)).astype(BF16)

    half = W // 2
    for to, first, n in ((rows_sent[0], R - l0.low, l0.low), (rows_sent[1], 0, 2)):
        for i in range(n):
            at = (first + i) * W
            to[i] = folded(maps[at : at + half, :], maps[at + half : at + W, :])
    half = R // 2
    for to, first, n in ((cols_sent[0], W - l0.low, l0.low), (cols_sent[1], 0, 2)):
        for i in range(n):
            a = maps[pl.ds(first + i, half, stride=W), :]
            to[i] = folded(a, maps[pl.ds(half * W + first + i, half, stride=W), :])
    for l in range(1, 4):
        lv = levels[l]
        for d, (base, n) in enumerate(((lv.cols - 8, lv.low), (0, 2))):
            to = cols_sent[2 * l + d]
            size = lv.rows * 8
            for p in range(lv.planes):
                w = min(LANES, lv.chan - p * LANES)
                block = feats[l][:, base : base + 8, p * LANES : p * LANES + w].astype(F32)
                side[6 * l + 3 * d + p, 0:size, 0:w] = block.reshape(size, w)
                for i in range(n):
                    at = i + (8 - n if d == 0 else 0)
                    value = side[6 * l + 3 * d + p, pl.ds(at, lv.rows, stride=8), 0:w]
                    to[i, :, p * LANES : p * LANES + w] = value.astype(BF16)

    pl.semaphore_wait(barrier, count)

    def copy(l, k):
        lv, way = levels[l], WAYS[k]
        dy, dx = way
        if dx:
            src = cols_sent[2 * l + (0 if dx > 0 else 1)]
            first, n = window(lv, way)
            if dy:
                src = src.at[:, pl.ds(first, n)]
        elif l == 0:
            src = rows_sent[0 if dy > 0 else 1]
        else:
            src = feats[l].at[pl.ds(lv.rows - lv.low, lv.low) if dy > 0 else pl.ds(0, 2)]
        return pltpu.make_async_remote_copy(
            src, outs[8 * l + k], send.at[8 * l + k], recv.at[8 * l + k], device_id=there(way)
        )

    for k, way in enumerate(WAYS):

        @pl.when(on_map(way, 1))
        def _(k=k):
            for l in range(4):
                copy(l, k).start()

    for k, way in enumerate(WAYS):

        @pl.when(on_map(way, 1))
        def _(k=k):
            for l in range(4):
                copy(l, k).wait_send()

        @pl.when(on_map(way, -1))
        def _(k=k):
            for l in range(4):
                copy(l, k).wait_recv()


def halos_of(levels, feats):
    V = pltpu.VMEM
    l0 = levels[0]
    shapes = [jax.ShapeDtypeStruct(message(lv, way), BF16) for lv in levels for way in WAYS]
    shapes.append(jax.ShapeDtypeStruct((l0.rows, l0.cols, l0.chan), BF16))
    vmem, hbm = pl.BlockSpec(memory_space=pltpu.VMEM), pl.BlockSpec(memory_space=pl.ANY)
    scratch = [V(message(l0, (d, 0)), BF16) for d in (1, -1)]
    scratch += [V(message(lv, (0, d)), BF16) for lv in levels for d in (1, -1)]
    scratch += [
        V((l0.chan * l0.rows, l0.cols), F32),
        V((l0.rows * l0.cols, LANES), F32),
        V((24, 8 * levels[1].rows, LANES), F32),
        pltpu.SemaphoreType.DMA((32,)),
        pltpu.SemaphoreType.DMA((32,)),
    ]
    return pl.pallas_call(
        functools.partial(exchange, levels),
        out_shape=shapes,
        in_specs=[vmem] * 4,
        out_specs=[hbm] * 32 + [vmem],
        scratch_shapes=scratch,
        compiler_params=pltpu.CompilerParams(collective_id=0, has_side_effects=True),
    )(*feats)


def chunking(length, most):
    n = -(-length // most)
    return n, up_to(-(-length // n), 16)


def prepare(levels, given, made, stage):
    w0_in, w1_in, mid0, mid1, fin0, fin1 = given
    w0, w1, wd0, wd1a, wd1v, wd2, wd2v = made
    c0, c1, c2, c3 = (lv.chan for lv in levels)

    def shifted(row, n, off, width, to):
        k, s = divmod(off, LANES)
        a = stage[row : row + n, k * LANES : (k + 1) * LANES]
        ids = lax.broadcasted_iota(jnp.int32, a.shape, 1)
        if s + width > LANES:
            a = jnp.where(ids >= s, a, stage[row : row + n, (k + 1) * LANES : (k + 2) * LANES])
        if (to - s) % LANES:
            a = pltpu.roll(a, (to - s) % LANES, 1)
        if width == LANES:
            return a
        return jnp.where((ids >= to) & (ids < to + width), a, 0.0)

    def fill(value):
        n, k = value.shape
        stage[0:n, 0:k] = value.astype(F32)

    for i in range(2):
        fill(w0_in[i])
        for q in range(3):
            offs = [c0 * (3 * p + q) for p in range(3)]
            cut = LANES - 2 * c0
            tile = shifted(0, c0, offs[0], c0, 0) + shifted(0, c0, offs[1], c0, c0)
            tile = tile + shifted(0, c0, offs[2], cut, 2 * c0)
            w0[i, q * LANES : q * LANES + c0, 0:LANES] = tile.astype(BF16)
            tile = shifted(0, c0, offs[2] + cut, c0 - cut, 0)
            w0[i, q * LANES : q * LANES + c0, LANES : 2 * LANES] = tile.astype(BF16)
        fill(w1_in[i])
        for q in range(3):
            for p in range(3):
                tile = shifted(0, c1, c1 * (3 * p + q), c1, 0)
                w1[i, q * LANES : q * LANES + c1, p * LANES : (p + 1) * LANES] = tile.astype(BF16)

    def apart(value, to, row):
        fill(value)
        for t in range(9):
            to[row : row + c1, t * LANES : (t + 1) * LANES] = shifted(0, c1, c1 * t, c1, 0).astype(BF16)

    for k in range(c2 // c1):
        apart(fin1[0, k * c1 : (k + 1) * c1, :], wd1a, k * c1)
    apart(mid1[0, 0], wd1a, 2 * LANES)
    for k in range(c3 // c1):
        apart(fin1[0, c2 + k * c1 : c2 + (k + 1) * c1, :], wd2v, k * c1)

    tall = up_to(9 * c0, LANES)

    def turned():
        return stage[0:LANES, 0:tall].T.astype(BF16)

    stage[0:LANES, 0:tall] = jnp.zeros((LANES, tall), F32)
    for k in range(2):
        stage[k * c0 : (k + 1) * c0, 0 : 9 * c0] = mid0[0, k].astype(F32)
    flat = turned()
    for t in range(9):
        wd0[t * LANES : t * LANES + c0, LANES : 2 * LANES] = flat[t * c0 : (t + 1) * c0, :]
        wd0[t * LANES : t * LANES + c0, 0:LANES] = fin0[t * c0 : (t + 1) * c0, 0:LANES]
    stage[0:LANES, 0:tall] = jnp.zeros((LANES, tall), F32)
    stage[c2 - LANES : c2 - LANES + c0, 0 : 9 * c0] = mid0[0, 2].astype(F32)
    flat = turned()
    for t in range(9):
        wd1v[t * LANES + c0 : t * LANES + 2 * c0, LANES : 2 * LANES] = flat[t * c0 : (t + 1) * c0, :]
    fill(fin0[...])
    depth = wd2.shape[0] // 9
    for t in range(9):
        wd1v[t * LANES : t * LANES + c0, 0:LANES] = shifted(t * c0, c0, c1, LANES, 0).astype(BF16)
        tile = shifted(t * c0, c0, c1 + LANES, c2 - LANES, 0)
        wd1v[t * LANES : t * LANES + c0, LANES : 2 * LANES] = tile.astype(BF16)
        row = t * depth + c2
        wd2[row : row + depth - c2, :] = jnp.zeros((depth - c2, c3), BF16)
        for j in range(c3 // LANES):
            tile = shifted(t * c0, c0, c1 + c2 + j * LANES, LANES, 0)
            wd2[row : row + c0, j * LANES : (j + 1) * LANES] = tile.astype(BF16)


def body(levels, *refs):
    refs = list(refs)

    def take(n):
        out = refs[:n]
        del refs[:n]
        return out

    feats, halos = take(4), take(32)
    w0_in, w1_in, w2_hbm, w3_hbm = take(4)
    biases = take(4)
    up1, up2, up3, mid0, mid1, fin0, fin1, fin2_hbm = take(8)
    outs = take(4)
    xs, hs = take(4), take(4)
    spread, odd, cols2, cols3 = take(4)
    w2, w3 = take(2)
    w0, w1, wd0, wd1a, wd1v, wd2, wd2v, stage, bpad = take(9)
    t01, v0, t2, v1, u0, u1, u2 = take(7)
    (sems,) = take(1)
    l0, l1, l2, l3 = levels
    copies = [pltpu.make_async_copy(a, b, sems.at[i]) for i, (a, b) in enumerate(((w2_hbm, w2), (w3_hbm, w3)))]
    depth = wd2.shape[0] // 9
    for ref in (w0, w1, wd0, wd1a, wd1v, bpad):
        ref[...] = jnp.zeros_like(ref)
    fin2_copies = [
        pltpu.make_async_copy(
            fin2_hbm.at[pl.ds(t * l2.chan, l2.chan)], wd2.at[pl.ds(t * depth, l2.chan)], sems.at[2 + t]
        )
        for t in range(9)
    ]
    for c in copies + fin2_copies:
        c.start()

    prepare(levels, (w0_in, w1_in, mid0, mid1, fin0, fin1), (w0, w1, wd0, wd1a, wd1v, wd2, wd2v), stage)
    for l in (0, 1):
        bpad[l, 0:2, 0 : levels[l].chan] = biases[l][...]

    ty, tx = lax.axis_index("ty"), lax.axis_index("tx")
    top, bottom = ty == 0, ty == lax.axis_size("ty") - 1
    left, right = tx == 0, tx == lax.axis_size("tx") - 1

    def lane(shape):
        return lax.broadcasted_iota(jnp.int32, shape, len(shape) - 1)

    def rows_loop(n, run):
        def step(i, _):
            run(i)
            return 0

        lax.fori_loop(0, n, step, 0)

    def put(l, at, value):
        lv = levels[l]
        for p in range(lv.planes):
            w = min(LANES, lv.chan - p * LANES)
            xs[l][p, pl.ds(at, value.shape[0]), 0:w] = value[:, p * LANES : p * LANES + w]

    for l, lv in enumerate(levels):
        xs[l][...] = jnp.zeros_like(xs[l])
    for ref in (v0, v1):
        ref[...] = jnp.zeros_like(ref)
    for l, lv in enumerate(levels):

        def place(source, row, l=l, lv=lv):
            def run(i):
                at = pl.multiple_of((i + row + lv.lead) * lv.pitch, 8)
                put(l, at, source[i].astype(F32))

            rows_loop(source.shape[0], run)

        def place_rows(source, row, l=l, lv=lv):
            if lv.folds == 1:
                return place(source, row)
            half = lv.cols // 2
            for i in range(source.shape[0]):
                value = source[i].astype(F32)
                put(l, lv.at(row + i), value[:, : lv.chan])
                put(l, lv.at(row + i, half), pltpu.roll(value, LANES // 2, 1)[:, : lv.chan])

        def place_cols(source, way, l=l, lv=lv):
            dy, dx = way
            for i in range(source.shape[0]):
                col = i - lv.low if dx > 0 else lv.cols + i
                value = source[i].astype(F32)
                both = [value]
                if lv.folds == 2:
                    both = [value, pltpu.roll(value, LANES // 2, 1)]
                if dy > 0:
                    pieces = [(-lv.low, both[-1][lv.near - lv.low :])]
                elif dy < 0:
                    pieces = [(lv.rows, both[0][:2])]
                else:
                    pieces = [(j * lv.lines, v) for j, v in enumerate(both)]
                for row, v in pieces:
                    for p in range(lv.planes):
                        w = min(LANES, lv.chan - p * LANES)
                        at = pl.ds(lv.at(row, col), v.shape[0], stride=lv.pitch)
                        part = v[:, p * LANES : p * LANES + w]
                        if w < LANES:
                            part = jnp.concatenate([part, jnp.zeros((v.shape[0], LANES - w), F32)], axis=1)
                        xs[l][p, at, :] = part

        place(feats[l], 0)
        for k, way in enumerate(WAYS):

            @pl.when(on_map(way, -1))
            def _(k=k, way=way):
                source = halos[8 * l + k]
                if way[1]:
                    place_cols(source, way)
                else:
                    place_rows(source, -lv.low if way[0] > 0 else lv.rows)

    def blank(ref, lv, low, high):
        planes = ref.shape[0]

        def columns(col, n):
            start = lv.at(-low - 1)
            count = low + 1 + lv.rows + high
            for c in range(col, col + n):
                for p in range(planes):
                    ref[p, pl.ds(start + c, count, stride=lv.pitch), :] = jnp.zeros((count, LANES), F32)

        def rows(row, n):
            for p in range(planes):
                size = n * lv.pitch
                ref[p, pl.ds(lv.at(row) - lv.tail + 2, size), :] = jnp.zeros((size, LANES), F32)

        pl.when(left)(lambda: columns(lv.pitch - low, low))
        if high:
            pl.when(right)(lambda: columns(lv.cols, high))
            pl.when(bottom)(lambda: rows(lv.rows, high))

        pl.when(top)(lambda: rows(-low, low))

    def wide_conv(l, src, dst, weight, bias, span, residual):
        lv = levels[l]
        start, length = span
        n, m = chunking(length, 656)
        C = lv.chan

        def run(i):
            base = pl.multiple_of(start + i * m, 8)
            a, b, c = (
                src[0, pl.ds(pl.multiple_of(base - 8 + d * lv.pitch, 8), m + 16), :] for d in (-1, 0, 1)
            )
            if 3 * C <= 2 * LANES:
                ids = lane(a.shape)
                moved = pltpu.roll(c, 2 * C, 1)
                tile0 = a + pltpu.roll(b, C, 1) + jnp.where(ids >= 2 * C, moved, 0.0)
                tile1 = jnp.where(ids < 3 * C - LANES, moved, 0.0)
                lhs = jnp.concatenate([tile0.astype(BF16), tile1.astype(BF16)], axis=1)
            else:
                lhs = jnp.concatenate([a.astype(BF16), b.astype(BF16), c.astype(BF16)], axis=1)
            o = lax.dot_general(lhs, weight[...], NT, preferred_element_type=F32)
            for q in range(3):
                spread[q, 0 : m + 16, :] = o[:, q * LANES : (q + 1) * LANES]
            y = spread[0, 7 : 7 + m, :] + spread[1, 8 : 8 + m, :] + spread[2, 9 : 9 + m, :]
            y = y + bias
            if residual:
                y = y + dst[0, pl.ds(base, m), :]
            dst[0, pl.ds(base, m), :] = jnp.maximum(y, 0.0)

        rows_loop(n, run)

    def offset(lv, t):
        return (t // 3 - 1) * lv.pitch + t % 3 - 1

    def deep_conv2(src, dst, weight, bias, span, residual):
        lv = l2
        start, length = span
        m = up_to(length, 16)
        total = lv.total
        p0, p1 = src[0, :, :], src[1, :, :]
        ids = lane((total, LANES))
        r0, r1 = pltpu.roll(p0, 64, 1), pltpu.roll(p1, 64, 1)
        odd[0, :, :] = jnp.where(ids >= 64, r0, 0.0)
        odd[1, :, :] = jnp.where(ids < 64, r0, r1)

        def piece(ref, p, t):
            return ref[p, pl.ds(start + offset(lv, t), m), :]

        for t in range(0, 9, 2):
            k = 3 * (t // 2) * LANES
            cols2[0:m, k : k + 128] = piece(src, 0, t).astype(BF16)
            tile = piece(src, 1, t)
            if t == 8:
                cols2[0:m, k + 128 : k + 192] = tile[:, 0:64].astype(BF16)
            else:
                cols2[0:m, k + 128 : k + 256] = (tile + piece(odd, 0, t + 1)).astype(BF16)
                cols2[0:m, k + 256 : k + 384] = piece(odd, 1, t + 1).astype(BF16)
        y = lax.dot_general(cols2[0:m, :], weight, NT, preferred_element_type=F32) + bias
        for p in range(2):
            w = min(LANES, lv.chan - p * LANES)
            part = y[:, p * LANES : p * LANES + w]
            if residual:
                part = part + dst[p, pl.ds(start, m), 0:w]
            dst[p, pl.ds(start, m), 0:w] = jnp.maximum(part, 0.0)

    def deep_conv3(src, dst, weight, bias, span, residual):
        lv = l3
        start, length = span
        m = up_to(length, 16)
        for t in range(9):
            for p in range(lv.planes):
                k = (t * lv.planes + p) * LANES
                cols3[0:m, k : k + LANES] = src[p, pl.ds(start + offset(lv, t), m), :].astype(BF16)
        y = lax.dot_general(cols3[0:m, :], weight, NT, preferred_element_type=F32) + bias
        for p in range(lv.planes):
            part = y[:, p * LANES : (p + 1) * LANES]
            if residual:
                part = part + dst[p, pl.ds(start, m), :]
            dst[p, pl.ds(start, m), :] = jnp.maximum(part, 0.0)

    for l in (0, 1):
        lv = levels[l]
        wide_conv(l, xs[l], hs[l], (w0, w1)[l].at[0], bpad[l, 0:1, :], lv.first(), False)
        blank(hs[l], lv, lv.rim + 1, 1)
        wide_conv(l, hs[l], xs[l], (w0, w1)[l].at[1], bpad[l, 1:2, :], lv.second(), True)
        blank(xs[l], lv, lv.rim, 0)

    hs[2][1, :, :] = jnp.zeros((l2.total, LANES), F32)
    copies[0].wait()
    deep_conv2(xs[2], hs[2], w2[0], biases[2][0:1, :], l2.first(), False)
    blank(hs[2], l2, l2.rim + 1, 1)
    deep_conv2(hs[2], xs[2], w2[1], biases[2][1:2, :], l2.second(), True)
    blank(xs[2], l2, l2.rim, 0)
    copies[1].wait()
    deep_conv3(xs[3], hs[3], w3[0], biases[3][0:1, :], l3.first(), False)
    blank(hs[3], l3, 1, 1)
    deep_conv3(hs[3], xs[3], w3[1], biases[3][1:2, :], l3.second(), True)

    def gathered(src, plane, big, small, i, t, width=None):
        width = small.pitch if width is None else width
        at = (2 * i + t // 3 - 1 + big.lead) * big.pitch + 2 * (small.cols - width) + t % 3 - 1
        return src[plane, pl.ds(at, width, stride=2), :]

    rim = RIMS[1]
    rows = up_to(rim + l1.rows, 4)

    def down0(k):
        i0 = l1.rows - rows + 4 * k
        taps = [
            jnp.concatenate([gathered(xs[0], 0, l0, l1, i0 + r, t) for r in range(4)], axis=0).astype(BF16)
            for t in range(9)
        ]
        o = lax.dot_general(jnp.concatenate(taps, axis=1), wd0[...], NN, preferred_element_type=F32)
        at = pl.multiple_of((i0 + l1.lead) * l1.pitch - l1.tail, 8)
        t01[0, pl.ds(at, 4 * l1.pitch), :] = o[:, 0:LANES]
        v0[0, pl.ds(at, 4 * l1.pitch), :] = jnp.maximum(o[:, LANES:], 0.0)

    rows_loop(rows // 4, down0)
    blank(v0, l1, rim, 0)

    rows = l2.rows + 2
    at = l2.at(-2) - l2.tail
    span = rows * l2.pitch

    def down1(src, weight, form):
        taps = [
            jnp.concatenate([gathered(src, 0, l1, l2, i, t) for i in range(-2, l2.rows)], axis=0).astype(BF16)
            for t in range(9)
        ]
        return lax.dot_general(jnp.concatenate(taps, axis=1), weight[...], form, preferred_element_type=F32)

    o = down1(xs[1], wd1a, NT)
    e = down1(v0, wd1v, NN)
    second = o[:, LANES : 2 * LANES] + e[:, LANES : 2 * LANES]
    ids = lane(second.shape)
    t2[0, 0:span, :] = o[:, 0:LANES] + e[:, 0:LANES]
    t2[1, 0:span, :] = second
    v1[0, pl.ds(at, span), :] = jnp.where(ids >= 64, jnp.maximum(second, 0.0), 0.0)
    v1[1, pl.ds(at, span), :] = jnp.maximum(o[:, 2 * LANES :], 0.0)
    blank(v1, l2, 1, 0)
    def tap3(p, t):
        parts = []
        for i in range(l3.rows):
            piece = gathered(xs[2] if p < 2 else v1, p if p < 2 else 1, l2, l3, i, t, l3.cols)
            if p == 1:
                piece = piece + gathered(v1, 0, l2, l3, i, t, l3.cols)
            parts.append(piece)
        return jnp.concatenate(parts, axis=0).astype(BF16)

    taps = jnp.concatenate([tap3(2, t) for t in range(9)], axis=1)
    t3 = lax.dot_general(taps, wd2v[...], NT, preferred_element_type=F32)
    taps = jnp.concatenate([tap3(p, t) for t in range(9) for p in range(2)], axis=1)
    for c in fin2_copies:
        c.wait()
    t3 = t3 + lax.dot_general(taps, wd2[...], NN, preferred_element_type=F32)

    def center(l, i):
        lv = levels[l]
        parts = [xs[l][p, pl.ds(lv.at(i), lv.cols), :] for p in range(lv.planes)]
        return jnp.concatenate(parts, axis=1)[:, : lv.chan] if lv.planes > 1 else parts[0][:, : lv.chan]

    a3 = jnp.concatenate([center(3, i) for i in range(l3.rows)], axis=0)
    y3 = jnp.maximum(a3 + t3, 0.0).astype(BF16)
    for i in range(l3.rows):
        outs[3][i, :, :] = y3[i * l3.cols : (i + 1) * l3.cols, :]

    c0, c1, c2 = l0.chan, l1.chan, l2.chan
    a3 = a3.astype(BF16)
    up3_0 = lax.dot_general(a3, up3[0, 0:c0, :], NT, preferred_element_type=F32)
    up3_1 = lax.dot_general(a3, up3[0, c0 : c0 + c1, :], NT, preferred_element_type=F32)
    up3_2 = lax.dot_general(a3, up3[0, c0 + c1 :, :], NT, preferred_element_type=F32)

    def enlarge(value, dst, plane, width, rows, cols):
        for i in range(rows):
            line = value[i * cols : (i + 1) * cols, :]
            for di in range(2):
                for dj in range(2):
                    base = (2 * i + di) * 2 * cols + dj
                    dst[plane, pl.ds(base, cols, stride=2), 0:width] = line

    enlarge(up3_0, u2, 0, c0, l3.rows, l3.cols)
    enlarge(up3_1, u2, 1, c1, l3.rows, l3.cols)
    enlarge(up3_2[:, 0:LANES], u2, 2, LANES, l3.rows, l3.cols)
    enlarge(up3_2[:, LANES:], u2, 3, c2 - LANES, l3.rows, l3.cols)
    a2 = jnp.concatenate([center(2, i) for i in range(l2.rows)], axis=0)
    a2b = a2.astype(BF16)
    up2_0 = lax.dot_general(a2b, up2[0, 0:c0, :], NT, preferred_element_type=F32) + u2[0, :, 0:c0]
    up2_1 = lax.dot_general(a2b, up2[0, c0:, :], NT, preferred_element_type=F32) + u2[1, :, 0:c1]
    for i in range(l2.rows):
        for p in range(2):
            w = min(LANES, c2 - p * LANES)
            line = xs[2][p, pl.ds(l2.at(i), l2.cols), 0:w]
            line = line + t2[p, pl.ds((i + 2) * l2.pitch + l2.tail, l2.cols), 0:w]
            line = line + u2[2 + p, pl.ds(i * l2.cols, l2.cols), 0:w]
            outs[2][i, :, p * LANES : p * LANES + w] = jnp.maximum(line, 0.0).astype(BF16)
    enlarge(up2_0, u1, 0, c0, l2.rows, l2.cols)
    enlarge(up2_1, u1, 1, c1, l2.rows, l2.cols)

    def join1(k):
        lines = []
        for r in range(4):
            i = 4 * k + r
            at = pl.multiple_of((i + l1.lead) * l1.pitch, 8)
            line = xs[1][0, pl.ds(at, l1.cols), 0:c1]
            lines.append(line)
            total = line + t01[0, pl.ds(at, l1.cols), 0:c1]
            total = total + u1[1, pl.ds(pl.multiple_of(i * l1.cols, 8), l1.cols), 0:c1]
            outs[1][i, :, :] = jnp.maximum(total, 0.0).astype(BF16)
        a1 = jnp.concatenate(lines, axis=0).astype(BF16)
        n = 4 * l1.cols
        y = lax.dot_general(a1, up1[0], NT, preferred_element_type=F32)
        y = y + u1[0, pl.ds(pl.multiple_of(k * n, 8), n), 0:c0]
        for r in range(4):
            line = y[r * l1.cols : (r + 1) * l1.cols, :]
            for dj in range(2):
                u0[0, pl.ds(dj, l1.cols, stride=2), 0:c0] = line
            up = u0[0, 0 : l0.cols, 0:c0]
            for di in range(2):
                i = 2 * (4 * k + r) + di
                at = pl.multiple_of((i + l0.lead) * l0.pitch, 8)
                total = xs[0][0, pl.ds(at, l0.cols), 0:c0] + up
                outs[0][i, :, :] = jnp.maximum(total, 0.0).astype(BF16)

    rows_loop(l1.rows // 4, join1)


def per_device(*args):
    feats, weights, biases, rest = args[0:4], args[4:8], args[8:12], args[12:20]
    levels = [Level(l, f.shape[1:] + f.shape[:1]) for l, f in enumerate(feats)]
    feats = [feats[0]] + [f.transpose(1, 2, 0) for f in feats[1:]]
    l0, l1, l2, l3 = levels
    c0, c1, c2, c3 = (lv.chan for lv in levels)
    *halos, first = halos_of(levels, feats)
    feats[0] = first
    up1, up2, up3, mid0, mid1, fin0, fin1, fin2 = rest
    fin0, fin2 = fin0[0].T, fin2[0].T
    vmem, any_ = pl.BlockSpec(memory_space=pltpu.VMEM), pl.BlockSpec(memory_space=pl.ANY)
    V = pltpu.VMEM
    maps = [V((lv.planes, lv.total, LANES), F32) for lv in levels]
    m2, m3 = up_to(l2.first()[1], 16), up_to(l3.first()[1], 16)
    n1 = max(chunking(s[1], 656)[1] for lv in levels[:2] for s in (lv.first(), lv.second()))
    scratch = maps * 2 + [
        V((3, n1 + 16, LANES), F32),
        V((2, l2.total, LANES), F32),
        V((m2, 9 * c2), BF16),
        V((m3, 9 * c3), BF16),
        V(weights[2].shape, BF16),
        V(weights[3].shape, BF16),
        V((2, 3 * LANES, 2 * LANES), BF16),
        V((2, 3 * LANES, 3 * LANES), BF16),
        V((9 * LANES, 2 * LANES), BF16),
        V((3 * LANES, 9 * LANES), BF16),
        V((9 * LANES, 2 * LANES), BF16),
        V((9 * up_to(c2, LANES), c3), BF16),
        V((c3, 9 * LANES), BF16),
        V((up_to(9 * c0, 8), up_to(max(9 * c1, fin0.shape[1]), LANES) + LANES), F32),
        V((2, 8, LANES), F32),
        V((1, l1.total, LANES), F32),
        V((1, l1.total, LANES), F32),
        V((2, (l2.rows + 2) * l2.pitch, LANES), F32),
        V((2, l2.total, LANES), F32),
        V((1, l0.cols, LANES), F32),
        V((2, l1.rows * l1.cols, LANES), F32),
        V((4, l2.rows * l2.cols, LANES), F32),
        pltpu.SemaphoreType.DMA((11,)),
    ]
    outs = pl.pallas_call(
        functools.partial(body, levels),
        out_shape=[jax.ShapeDtypeStruct(f.shape, BF16) for f in feats],
        in_specs=[vmem] * 38 + [any_] * 2 + [vmem] * 11 + [any_],
        out_specs=[vmem] * 4,
        scratch_shapes=scratch,
        compiler_params=pltpu.CompilerParams(vmem_limit_bytes=60 * 2**20),
    )(*feats, *halos, *weights, *biases, up1, up2, up3, mid0, mid1, fin0, fin1, fin2)
    return tuple(o.transpose(2, 0, 1) for o in outs)


def solution(mesh):
    tiled = P(None, "ty", "tx")
    return jax.shard_map(
        per_device,
        mesh=mesh,
        in_specs=(tiled,) * 4 + (P(),) * 16,
        out_specs=(tiled,) * 4,
        check_vma=False,
    )
```

```python
import functools

import jax
import jax.numpy as jnp
from jax import lax
from jax.experimental import pallas as pl
from jax.experimental.pallas import tpu as pltpu
from jax.sharding import PartitionSpec as P

RIMS = (7, 3, 1, 0)
GROUP = 3
LANES = 128
NT = (((1,), (1,)), ((), ()))
NN = (((1,), (0,)), ((), ()))
WAYS = [(dy, dx) for dy in (-1, 0, 1) for dx in (-1, 0, 1) if dy or dx]
F32, BF16 = jnp.float32, jnp.bfloat16


def up_to(n, m):
    return -(-n // m) * m


class Level:
    def __init__(self, level, shape):
        self.rows, self.cols, self.chan = shape
        self.rim = RIMS[level]
        self.low = self.rim + 2
        self.pitch = up_to(self.cols + 2 + self.low, 8)
        self.lead = self.low + 1
        self.tail = self.pitch - self.cols
        self.planes = up_to(self.chan, LANES) // LANES
        self.near = up_to(self.low, 8)
        self.total = (self.lead + self.rows + 4) * self.pitch
        self.folds = 2 if 2 * self.chan <= LANES else 1
        self.lines = self.rows // self.folds
        self.wide = LANES if self.folds == 2 else self.chan

    def at(self, row, col=0):
        return (row + self.lead) * self.pitch + col

    def first(self):
        start = self.at(-self.rim - 1) - self.tail
        return start, self.at(self.rows) + self.cols + 8 - start

    def second(self):
        start = self.at(-self.rim) - self.tail
        return start, self.at(self.rows - 1) + self.cols - start


def window(lv, way):
    lines = lv.lines
    if way[0] == 0:
        return 0, lines
    return (lines - lv.near, lv.near) if way[0] > 0 else (0, 8)


def message(lv, way):
    dy, dx = way
    if dx == 0:
        rows = lv.low if dy > 0 else 2
        return (rows, lv.cols // lv.folds, lv.wide)
    return (lv.low if dx > 0 else 2, window(lv, way)[1], lv.wide)


def on_map(way, side):
    ok = True
    for step, axis in zip(way, ("ty", "tx")):
        if step:
            place = lax.axis_index(axis) + side * step
            ok = ok & (place >= 0) & (place < lax.axis_size(axis))
    return ok


def exchange(levels, *refs):
    feats, outs, turned = refs[:4], refs[4:36], refs[36]
    rows_sent, cols_sent = refs[37:39], refs[39:47]
    stage, maps, side, send, recv = refs[47:]
    here = {a: lax.axis_index(a) for a in ("ty", "tx")}
    barrier = pltpu.get_barrier_semaphore()
    l0 = levels[0]

    def there(way):
        return {"ty": here["ty"] + way[0], "tx": here["tx"] + way[1]}

    count = 0
    for way in WAYS:
        ok = on_map(way, 1)

        @pl.when(ok)
        def _(way=way):
            pl.semaphore_signal(barrier, 1, device_id=there(way))

        count = count + jnp.where(ok, 1, 0)

    C, R, W = l0.chan, l0.rows, l0.cols

    tall, wide = R + 1, W + 1

    def load(i, _):
        for j in range(8):
            at = pl.multiple_of(i * 8 * tall, 8) + j * tall
            stage[pl.ds(at, R), :] = feats[0][8 * i + j].astype(F32)
        return 0

    lax.fori_loop(0, C // 8, load, 0)

    def turn(i, _):
        for j in range(8):
            r = 8 * i + j
            value = stage[pl.ds(r, C, stride=tall), :].T
            at = pl.multiple_of(i * 8 * wide, 8) + j * wide
            maps[pl.ds(at, W), 0:C] = value
            turned[r] = value.astype(BF16)
        return 0

    lax.fori_loop(0, R // 8, turn, 0)

    def folded(a, b):
        ids = lax.broadcasted_iota(jnp.int32, a.shape, 1)
        a, b = jnp.where(ids < C, a, 0.0), jnp.where(ids < C, b, 0.0)
        return (a + pltpu.roll(b, LANES // 2, 1)).astype(BF16)

    half = W // 2
    for to, first, n in ((rows_sent[0], R - l0.low, l0.low), (rows_sent[1], 0, 2)):
        for i in range(n):
            at = (first + i) * wide
            to[i] = folded(maps[at : at + half, :], maps[at + half : at + W, :])
    half = R // 2
    for to, first, n in ((cols_sent[0], W - l0.low, l0.low), (cols_sent[1], 0, 2)):
        for i in range(n):
            a = maps[pl.ds(first + i, half, stride=wide), :]
            to[i] = folded(a, maps[pl.ds(half * wide + first + i, half, stride=wide), :])
    for l in range(1, 4):
        lv = levels[l]
        for d, (base, n) in enumerate(((lv.cols - 8, lv.low), (0, 2))):
            to = cols_sent[2 * l + d]
            for p in range(lv.planes):
                w = min(LANES, lv.chan - p * LANES)
                slot = 6 * l + 3 * d + p
                for r in range(lv.rows):
                    block = feats[l][r, base : base + 8, p * LANES : p * LANES + w]
                    side[slot, 9 * r : 9 * r + 8, 0:w] = block.astype(F32)
                for i in range(n):
                    at = i + (8 - n if d == 0 else 0)
                    value = side[slot, pl.ds(at, lv.rows, stride=9), 0:w]
                    to[i, :, p * LANES : p * LANES + w] = value.astype(BF16)

    pl.semaphore_wait(barrier, count)

    def copy(l, k):
        lv, way = levels[l], WAYS[k]
        dy, dx = way
        if dx:
            src = cols_sent[2 * l + (0 if dx > 0 else 1)]
            first, n = window(lv, way)
            if dy:
                src = src.at[:, pl.ds(first, n)]
        elif l == 0:
            src = rows_sent[0 if dy > 0 else 1]
        else:
            src = feats[l].at[pl.ds(lv.rows - lv.low, lv.low) if dy > 0 else pl.ds(0, 2)]
        return pltpu.make_async_remote_copy(
            src, outs[8 * l + k], send.at[8 * l + k], recv.at[8 * l + k], device_id=there(way)
        )

    for k, way in enumerate(WAYS):

        @pl.when(on_map(way, 1))
        def _(k=k):
            for l in range(4):
                copy(l, k).start()

    for k, way in enumerate(WAYS):

        @pl.when(on_map(way, 1))
        def _(k=k):
            for l in range(4):
                copy(l, k).wait_send()

        @pl.when(on_map(way, -1))
        def _(k=k):
            for l in range(4):
                copy(l, k).wait_recv()


def halos_of(levels, feats):
    V = pltpu.VMEM
    l0 = levels[0]
    shapes = [jax.ShapeDtypeStruct(message(lv, way), BF16) for lv in levels for way in WAYS]
    shapes.append(jax.ShapeDtypeStruct((l0.rows, l0.cols, l0.chan), BF16))
    vmem, hbm = pl.BlockSpec(memory_space=pltpu.VMEM), pl.BlockSpec(memory_space=pl.ANY)
    scratch = [V(message(l0, (d, 0)), BF16) for d in (1, -1)]
    scratch += [V(message(lv, (0, d)), BF16) for lv in levels for d in (1, -1)]
    scratch += [
        V((l0.chan * (l0.rows + 1), l0.cols), F32),
        V((l0.rows * (l0.cols + 1), LANES), F32),
        V((24, 9 * levels[1].rows, LANES), F32),
        pltpu.SemaphoreType.DMA((32,)),
        pltpu.SemaphoreType.DMA((32,)),
    ]
    return pl.pallas_call(
        functools.partial(exchange, levels),
        out_shape=shapes,
        in_specs=[vmem] * 4,
        out_specs=[hbm] * 32 + [vmem],
        scratch_shapes=scratch,
        compiler_params=pltpu.CompilerParams(collective_id=0, has_side_effects=True),
    )(*feats)


def chunking(length, most):
    n = -(-length // most)
    return n, up_to(-(-length // n), 16)


def prepare(levels, given, made, stage):
    w0_in, w1_in, mid0, mid1, fin0, fin1 = given
    w0, w1, wd0, wd1a, wd1v, wd2, wd2v = made
    c0, c1, c2, c3 = (lv.chan for lv in levels)

    def shifted(row, n, off, width, to):
        k, s = divmod(off, LANES)
        a = stage[row : row + n, k * LANES : (k + 1) * LANES]
        ids = lax.broadcasted_iota(jnp.int32, a.shape, 1)
        if s + width > LANES:
            a = jnp.where(ids >= s, a, stage[row : row + n, (k + 1) * LANES : (k + 2) * LANES])
        if (to - s) % LANES:
            a = pltpu.roll(a, (to - s) % LANES, 1)
        if width == LANES:
            return a
        return jnp.where((ids >= to) & (ids < to + width), a, 0.0)

    def fill(value):
        n, k = value.shape
        stage[0:n, 0:k] = value.astype(F32)

    for i in range(2):
        fill(w0_in[i])
        for q in range(3):
            offs = [c0 * (3 * p + q) for p in range(3)]
            cut = LANES - 2 * c0
            tile = shifted(0, c0, offs[0], c0, 0) + shifted(0, c0, offs[1], c0, c0)
            tile = tile + shifted(0, c0, offs[2], cut, 2 * c0)
            w0[i, q * LANES : q * LANES + c0, 0:LANES] = tile.astype(BF16)
            tile = shifted(0, c0, offs[2] + cut, c0 - cut, 0)
            w0[i, q * LANES : q * LANES + c0, LANES : 2 * LANES] = tile.astype(BF16)
        fill(w1_in[i])
        for q in range(3):
            for p in range(3):
                tile = shifted(0, c1, c1 * (3 * p + q), c1, 0)
                w1[i, q * LANES : q * LANES + c1, p * LANES : (p + 1) * LANES] = tile.astype(BF16)

    def apart(value, to, row):
        fill(value)
        for t in range(9):
            to[row : row + c1, t * LANES : (t + 1) * LANES] = shifted(0, c1, c1 * t, c1, 0).astype(BF16)

    for k in range(c2 // c1):
        apart(fin1[0, k * c1 : (k + 1) * c1, :], wd1a, k * c1)
    apart(mid1[0, 0], wd1a, 2 * LANES)
    for k in range(c3 // c1):
        apart(fin1[0, c2 + k * c1 : c2 + (k + 1) * c1, :], wd2v, k * c1)

    tall = up_to(9 * c0, LANES)

    def turned():
        return stage[0:LANES, 0:tall].T.astype(BF16)

    stage[0:LANES, 0:tall] = jnp.zeros((LANES, tall), F32)
    for k in range(2):
        stage[k * c0 : (k + 1) * c0, 0 : 9 * c0] = mid0[0, k].astype(F32)
    flat = turned()
    for t in range(9):
        wd0[t * LANES : t * LANES + c0, LANES : 2 * LANES] = flat[t * c0 : (t + 1) * c0, :]
        wd0[t * LANES : t * LANES + c0, 0:LANES] = fin0[t * c0 : (t + 1) * c0, 0:LANES]
    stage[0:LANES, 0:tall] = jnp.zeros((LANES, tall), F32)
    stage[c2 - LANES : c2 - LANES + c0, 0 : 9 * c0] = mid0[0, 2].astype(F32)
    flat = turned()
    for t in range(9):
        wd1v[t * LANES + c0 : t * LANES + 2 * c0, LANES : 2 * LANES] = flat[t * c0 : (t + 1) * c0, :]
    fill(fin0[...])
    depth = wd2.shape[0] // 9
    for t in range(9):
        wd1v[t * LANES : t * LANES + c0, 0:LANES] = shifted(t * c0, c0, c1, LANES, 0).astype(BF16)
        tile = shifted(t * c0, c0, c1 + LANES, c2 - LANES, 0)
        wd1v[t * LANES : t * LANES + c0, LANES : 2 * LANES] = tile.astype(BF16)
        row = t * depth + c2
        wd2[row : row + depth - c2, :] = jnp.zeros((depth - c2, c3), BF16)
        for j in range(c3 // LANES):
            tile = shifted(t * c0, c0, c1 + c2 + j * LANES, LANES, 0)
            wd2[row : row + c0, j * LANES : (j + 1) * LANES] = tile.astype(BF16)


def body(levels, *refs):
    refs = list(refs)

    def take(n):
        out = refs[:n]
        del refs[:n]
        return out

    feats, halos = take(4), take(32)
    w0_in, w1_in, w2_hbm, w3_hbm = take(4)
    biases = take(4)
    up1, up2, up3, mid0, mid1, fin0, fin1, fin2_hbm = take(8)
    outs = take(4)
    xs, hs = take(4), take(4)
    spread, odd, cols2, cols3 = take(4)
    w2, w3 = take(2)
    w0, w1, wd0, wd1a, wd1v, wd2, wd2v, stage, bpad = take(9)
    t01, v0, t2, v1, u0, u1, u2 = take(7)
    (sems,) = take(1)
    l0, l1, l2, l3 = levels
    copies = [pltpu.make_async_copy(a, b, sems.at[i]) for i, (a, b) in enumerate(((w2_hbm, w2), (w3_hbm, w3)))]
    depth = wd2.shape[0] // 9
    for ref in (w0, w1, wd0, wd1a, wd1v, bpad):
        ref[...] = jnp.zeros_like(ref)
    fin2_copies = [
        pltpu.make_async_copy(
            fin2_hbm.at[pl.ds(t * l2.chan, l2.chan)], wd2.at[pl.ds(t * depth, l2.chan)], sems.at[2 + t]
        )
        for t in range(9)
    ]
    for c in copies + fin2_copies:
        c.start()

    prepare(levels, (w0_in, w1_in, mid0, mid1, fin0, fin1), (w0, w1, wd0, wd1a, wd1v, wd2, wd2v), stage)
    for l in (0, 1):
        bpad[l, 0:2, 0 : levels[l].chan] = biases[l][...]

    ty, tx = lax.axis_index("ty"), lax.axis_index("tx")
    top, bottom = ty == 0, ty == lax.axis_size("ty") - 1
    left, right = tx == 0, tx == lax.axis_size("tx") - 1

    def lane(shape):
        return lax.broadcasted_iota(jnp.int32, shape, len(shape) - 1)

    def rows_loop(n, run):
        def step(i, _):
            run(i)
            return 0

        if n == 1:
            run(0)
        else:
            lax.fori_loop(0, n, step, 0)

    def put(l, at, value):
        lv = levels[l]
        for p in range(lv.planes):
            w = min(LANES, lv.chan - p * LANES)
            xs[l][p, pl.ds(at, value.shape[0]), 0:w] = value[:, p * LANES : p * LANES + w]

    for l, lv in enumerate(levels):
        xs[l][...] = jnp.zeros_like(xs[l])
    for ref in (v0, v1):
        ref[...] = jnp.zeros_like(ref)
    for l, lv in enumerate(levels):

        def place(source, row, l=l, lv=lv):
            def run(i):
                at = pl.multiple_of((i + row + lv.lead) * lv.pitch, 8)
                put(l, at, source[i].astype(F32))

            rows_loop(source.shape[0], run)

        def place_rows(source, row, l=l, lv=lv):
            if lv.folds == 1:
                return place(source, row)
            half = lv.cols // 2
            for i in range(source.shape[0]):
                value = source[i].astype(F32)
                put(l, lv.at(row + i), value[:, : lv.chan])
                put(l, lv.at(row + i, half), pltpu.roll(value, LANES // 2, 1)[:, : lv.chan])

        def place_cols(source, way, l=l, lv=lv):
            dy, dx = way
            for i in range(source.shape[0]):
                col = i - lv.low if dx > 0 else lv.cols + i
                value = source[i].astype(F32)
                both = [value]
                if lv.folds == 2:
                    both = [value, pltpu.roll(value, LANES // 2, 1)]
                if dy > 0:
                    pieces = [(-lv.low, both[-1][lv.near - lv.low :])]
                elif dy < 0:
                    pieces = [(lv.rows, both[0][:2])]
                else:
                    pieces = [(j * lv.lines, v) for j, v in enumerate(both)]
                for row, v in pieces:
                    for p in range(lv.planes):
                        w = min(LANES, lv.chan - p * LANES)
                        at = pl.ds(lv.at(row, col), v.shape[0], stride=lv.pitch)
                        part = v[:, p * LANES : p * LANES + w]
                        if w < LANES:
                            part = jnp.concatenate([part, jnp.zeros((v.shape[0], LANES - w), F32)], axis=1)
                        xs[l][p, at, :] = part

        place(feats[l], 0)
        for k, way in enumerate(WAYS):

            @pl.when(on_map(way, -1))
            def _(k=k, way=way):
                source = halos[8 * l + k]
                if way[1]:
                    place_cols(source, way)
                else:
                    place_rows(source, -lv.low if way[0] > 0 else lv.rows)

    def blank(ref, lv, low, high):
        planes = ref.shape[0]

        def columns(col, n):
            start = lv.at(-low - 1)
            count = low + 1 + lv.rows + high
            for c in range(col, col + n):
                for p in range(planes):
                    ref[p, pl.ds(start + c, count, stride=lv.pitch), :] = jnp.zeros((count, LANES), F32)

        def rows(row, n):
            for p in range(planes):
                size = n * lv.pitch
                ref[p, pl.ds(lv.at(row) - lv.tail + 2, size), :] = jnp.zeros((size, LANES), F32)

        pl.when(left)(lambda: columns(lv.pitch - low, low))
        if high:
            pl.when(right)(lambda: columns(lv.cols, high))
            pl.when(bottom)(lambda: rows(lv.rows, high))

        pl.when(top)(lambda: rows(-low, low))

    def wide_conv(l, src, dst, weight, bias, span, residual):
        lv = levels[l]
        start, length = span
        n, m = chunking(length, 656)
        group = GROUP if n % GROUP == 0 else 1
        C = lv.chan

        def run(i, j):
            base = pl.multiple_of(start + (i * group + j) * m, 8)
            a, b, c = (
                src[0, pl.ds(pl.multiple_of(base - 8 + d * lv.pitch, 8), m + 16), :] for d in (-1, 0, 1)
            )
            if 3 * C <= 2 * LANES:
                ids = lane(a.shape)
                moved = pltpu.roll(c, 2 * C, 1)
                tile0 = a + pltpu.roll(b, C, 1) + jnp.where(ids >= 2 * C, moved, 0.0)
                tile1 = jnp.where(ids < 3 * C - LANES, moved, 0.0)
                lhs = jnp.concatenate([tile0.astype(BF16), tile1.astype(BF16)], axis=1)
            else:
                lhs = jnp.concatenate([a.astype(BF16), b.astype(BF16), c.astype(BF16)], axis=1)
            o = lax.dot_general(lhs, weight[...], NT, preferred_element_type=F32)
            for q in range(3):
                spread[3 * j + q, 0 : m + 16, :] = o[:, q * LANES : (q + 1) * LANES]
            y = spread[3 * j, 7 : 7 + m, :] + spread[3 * j + 1, 8 : 8 + m, :] + spread[3 * j + 2, 9 : 9 + m, :]
            y = y + bias
            if residual:
                y = y + dst[0, pl.ds(base, m), :]
            dst[0, pl.ds(base, m), :] = jnp.maximum(y, 0.0)

        def several(i):
            for j in range(group):
                run(i, j)

        rows_loop(n // group, several)

    def offset(lv, t):
        return (t // 3 - 1) * lv.pitch + t % 3 - 1

    def deep_conv2(src, dst, weight, bias, span, residual):
        lv = l2
        start, length = span
        m = up_to(length, 16)
        total = lv.total
        p0, p1 = src[0, :, :], src[1, :, :]
        ids = lane((total, LANES))
        r0, r1 = pltpu.roll(p0, 64, 1), pltpu.roll(p1, 64, 1)
        odd[0, :, :] = jnp.where(ids >= 64, r0, 0.0)
        odd[1, :, :] = jnp.where(ids < 64, r0, r1)

        def piece(ref, p, t):
            return ref[p, pl.ds(start + offset(lv, t), m), :]

        for t in range(0, 9, 2):
            k = 3 * (t // 2) * LANES
            cols2[0:m, k : k + 128] = piece(src, 0, t).astype(BF16)
            tile = piece(src, 1, t)
            if t == 8:
                cols2[0:m, k + 128 : k + 192] = tile[:, 0:64].astype(BF16)
            else:
                cols2[0:m, k + 128 : k + 256] = (tile + piece(odd, 0, t + 1)).astype(BF16)
                cols2[0:m, k + 256 : k + 384] = piece(odd, 1, t + 1).astype(BF16)
        y = lax.dot_general(cols2[0:m, :], weight, NT, preferred_element_type=F32) + bias
        for p in range(2):
            w = min(LANES, lv.chan - p * LANES)
            part = y[:, p * LANES : p * LANES + w]
            if residual:
                part = part + dst[p, pl.ds(start, m), 0:w]
            dst[p, pl.ds(start, m), 0:w] = jnp.maximum(part, 0.0)

    def deep_conv3(src, dst, weight, bias, span, residual):
        lv = l3
        start, length = span
        m = up_to(length, 16)
        for t in range(9):
            for p in range(lv.planes):
                k = (t * lv.planes + p) * LANES
                cols3[0:m, k : k + LANES] = src[p, pl.ds(start + offset(lv, t), m), :].astype(BF16)
        y = lax.dot_general(cols3[0:m, :], weight, NT, preferred_element_type=F32) + bias
        for p in range(lv.planes):
            part = y[:, p * LANES : (p + 1) * LANES]
            if residual:
                part = part + dst[p, pl.ds(start, m), :]
            dst[p, pl.ds(start, m), :] = jnp.maximum(part, 0.0)

    for l in (0, 1):
        lv = levels[l]
        wide_conv(l, xs[l], hs[l], (w0, w1)[l].at[0], bpad[l, 0:1, :], lv.first(), False)
        blank(hs[l], lv, lv.rim + 1, 1)
        wide_conv(l, hs[l], xs[l], (w0, w1)[l].at[1], bpad[l, 1:2, :], lv.second(), True)
        blank(xs[l], lv, lv.rim, 0)

    hs[2][1, :, :] = jnp.zeros((l2.total, LANES), F32)
    copies[0].wait()
    deep_conv2(xs[2], hs[2], w2[0], biases[2][0:1, :], l2.first(), False)
    blank(hs[2], l2, l2.rim + 1, 1)
    deep_conv2(hs[2], xs[2], w2[1], biases[2][1:2, :], l2.second(), True)
    blank(xs[2], l2, l2.rim, 0)
    copies[1].wait()
    deep_conv3(xs[3], hs[3], w3[0], biases[3][0:1, :], l3.first(), False)
    blank(hs[3], l3, 1, 1)
    deep_conv3(hs[3], xs[3], w3[1], biases[3][1:2, :], l3.second(), True)

    def gathered(src, plane, big, small, i, t, width=None):
        width = small.pitch if width is None else width
        at = (2 * i + t // 3 - 1 + big.lead) * big.pitch + 2 * (small.cols - width) + t % 3 - 1
        return src[plane, pl.ds(at, width, stride=2), :]

    rim = RIMS[1]
    rows = up_to(rim + l1.rows, 4)

    def down0(k):
        i0 = l1.rows - rows + 4 * k
        taps = [
            jnp.concatenate([gathered(xs[0], 0, l0, l1, i0 + r, t) for r in range(4)], axis=0).astype(BF16)
            for t in range(9)
        ]
        o = lax.dot_general(jnp.concatenate(taps, axis=1), wd0[...], NN, preferred_element_type=F32)
        at = pl.multiple_of((i0 + l1.lead) * l1.pitch - l1.tail, 8)
        t01[0, pl.ds(at, 4 * l1.pitch), :] = o[:, 0:LANES]
        v0[0, pl.ds(at, 4 * l1.pitch), :] = jnp.maximum(o[:, LANES:], 0.0)

    rows_loop(rows // 4, down0)
    blank(v0, l1, rim, 0)

    rows = l2.rows + 2
    at = l2.at(-2) - l2.tail
    span = rows * l2.pitch

    def down1(src, weight, form):
        taps = [
            jnp.concatenate([gathered(src, 0, l1, l2, i, t) for i in range(-2, l2.rows)], axis=0).astype(BF16)
            for t in range(9)
        ]
        return lax.dot_general(jnp.concatenate(taps, axis=1), weight[...], form, preferred_element_type=F32)

    o = down1(xs[1], wd1a, NT)
    e = down1(v0, wd1v, NN)
    second = o[:, LANES : 2 * LANES] + e[:, LANES : 2 * LANES]
    ids = lane(second.shape)
    t2[0, 0:span, :] = o[:, 0:LANES] + e[:, 0:LANES]
    t2[1, 0:span, :] = second
    v1[0, pl.ds(at, span), :] = jnp.where(ids >= 64, jnp.maximum(second, 0.0), 0.0)
    v1[1, pl.ds(at, span), :] = jnp.maximum(o[:, 2 * LANES :], 0.0)
    blank(v1, l2, 1, 0)
    def tap3(p, t):
        parts = []
        for i in range(l3.rows):
            piece = gathered(xs[2] if p < 2 else v1, p if p < 2 else 1, l2, l3, i, t, l3.cols)
            if p == 1:
                piece = piece + gathered(v1, 0, l2, l3, i, t, l3.cols)
            parts.append(piece)
        return jnp.concatenate(parts, axis=0).astype(BF16)

    taps = jnp.concatenate([tap3(2, t) for t in range(9)], axis=1)
    t3 = lax.dot_general(taps, wd2v[...], NT, preferred_element_type=F32)
    taps = jnp.concatenate([tap3(p, t) for t in range(9) for p in range(2)], axis=1)
    for c in fin2_copies:
        c.wait()
    t3 = t3 + lax.dot_general(taps, wd2[...], NN, preferred_element_type=F32)

    def center(l, i):
        lv = levels[l]
        parts = [xs[l][p, pl.ds(lv.at(i), lv.cols), :] for p in range(lv.planes)]
        return jnp.concatenate(parts, axis=1)[:, : lv.chan] if lv.planes > 1 else parts[0][:, : lv.chan]

    a3 = jnp.concatenate([center(3, i) for i in range(l3.rows)], axis=0)
    y3 = jnp.maximum(a3 + t3, 0.0).astype(BF16)
    for i in range(l3.rows):
        outs[3][i, :, :] = y3[i * l3.cols : (i + 1) * l3.cols, :]

    c0, c1, c2 = l0.chan, l1.chan, l2.chan
    a3 = a3.astype(BF16)
    up3_0 = lax.dot_general(a3, up3[0, 0:c0, :], NT, preferred_element_type=F32)
    up3_1 = lax.dot_general(a3, up3[0, c0 : c0 + c1, :], NT, preferred_element_type=F32)
    up3_2 = lax.dot_general(a3, up3[0, c0 + c1 :, :], NT, preferred_element_type=F32)

    def enlarge(value, dst, plane, width, rows, cols):
        for i in range(rows):
            line = value[i * cols : (i + 1) * cols, :]
            for di in range(2):
                for dj in range(2):
                    base = (2 * i + di) * 2 * cols + dj
                    dst[plane, pl.ds(base, cols, stride=2), 0:width] = line

    enlarge(up3_0, u2, 0, c0, l3.rows, l3.cols)
    enlarge(up3_1, u2, 1, c1, l3.rows, l3.cols)
    enlarge(up3_2[:, 0:LANES], u2, 2, LANES, l3.rows, l3.cols)
    enlarge(up3_2[:, LANES:], u2, 3, c2 - LANES, l3.rows, l3.cols)
    a2 = jnp.concatenate([center(2, i) for i in range(l2.rows)], axis=0)
    a2b = a2.astype(BF16)
    up2_0 = lax.dot_general(a2b, up2[0, 0:c0, :], NT, preferred_element_type=F32) + u2[0, :, 0:c0]
    up2_1 = lax.dot_general(a2b, up2[0, c0:, :], NT, preferred_element_type=F32) + u2[1, :, 0:c1]
    for i in range(l2.rows):
        for p in range(2):
            w = min(LANES, c2 - p * LANES)
            line = xs[2][p, pl.ds(l2.at(i), l2.cols), 0:w]
            line = line + t2[p, pl.ds((i + 2) * l2.pitch + l2.tail, l2.cols), 0:w]
            line = line + u2[2 + p, pl.ds(i * l2.cols, l2.cols), 0:w]
            outs[2][i, :, p * LANES : p * LANES + w] = jnp.maximum(line, 0.0).astype(BF16)
    enlarge(up2_0, u1, 0, c0, l2.rows, l2.cols)
    enlarge(up2_1, u1, 1, c1, l2.rows, l2.cols)

    def join1(k):
        lines = []
        for r in range(4):
            i = 4 * k + r
            at = pl.multiple_of((i + l1.lead) * l1.pitch, 8)
            line = xs[1][0, pl.ds(at, l1.cols), 0:c1]
            lines.append(line)
            total = line + t01[0, pl.ds(at, l1.cols), 0:c1]
            total = total + u1[1, pl.ds(pl.multiple_of(i * l1.cols, 8), l1.cols), 0:c1]
            outs[1][i, :, :] = jnp.maximum(total, 0.0).astype(BF16)
        a1 = jnp.concatenate(lines, axis=0).astype(BF16)
        n = 4 * l1.cols
        y = lax.dot_general(a1, up1[0], NT, preferred_element_type=F32)
        y = y + u1[0, pl.ds(pl.multiple_of(k * n, 8), n), 0:c0]
        for r in range(4):
            line = y[r * l1.cols : (r + 1) * l1.cols, :]
            for dj in range(2):
                u0[0, pl.ds(dj, l1.cols, stride=2), 0:c0] = line
            up = u0[0, 0 : l0.cols, 0:c0]
            for di in range(2):
                i = 2 * (4 * k + r) + di
                at = pl.multiple_of((i + l0.lead) * l0.pitch, 8)
                total = xs[0][0, pl.ds(at, l0.cols), 0:c0] + up
                outs[0][i, :, :] = jnp.maximum(total, 0.0).astype(BF16)

    rows_loop(l1.rows // 4, join1)


def per_device(*args):
    feats, weights, biases, rest = args[0:4], args[4:8], args[8:12], args[12:20]
    levels = [Level(l, f.shape[1:] + f.shape[:1]) for l, f in enumerate(feats)]
    feats = [feats[0]] + [f.transpose(1, 2, 0) for f in feats[1:]]
    l0, l1, l2, l3 = levels
    c0, c1, c2, c3 = (lv.chan for lv in levels)
    *halos, first = halos_of(levels, feats)
    feats[0] = first
    up1, up2, up3, mid0, mid1, fin0, fin1, fin2 = rest
    fin0, fin2 = fin0[0].T, fin2[0].T
    vmem, any_ = pl.BlockSpec(memory_space=pltpu.VMEM), pl.BlockSpec(memory_space=pl.ANY)
    V = pltpu.VMEM
    maps = [V((lv.planes, lv.total, LANES), F32) for lv in levels]
    m2, m3 = up_to(l2.first()[1], 16), up_to(l3.first()[1], 16)
    n1 = max(chunking(s[1], 656)[1] for lv in levels[:2] for s in (lv.first(), lv.second()))
    scratch = maps * 2 + [
        V((3 * GROUP, n1 + 16, LANES), F32),
        V((2, l2.total, LANES), F32),
        V((m2, 9 * c2), BF16),
        V((m3, 9 * c3), BF16),
        V(weights[2].shape, BF16),
        V(weights[3].shape, BF16),
        V((2, 3 * LANES, 2 * LANES), BF16),
        V((2, 3 * LANES, 3 * LANES), BF16),
        V((9 * LANES, 2 * LANES), BF16),
        V((3 * LANES, 9 * LANES), BF16),
        V((9 * LANES, 2 * LANES), BF16),
        V((9 * up_to(c2, LANES), c3), BF16),
        V((c3, 9 * LANES), BF16),
        V((up_to(9 * c0, 8), up_to(max(9 * c1, fin0.shape[1]), LANES) + LANES), F32),
        V((2, 8, LANES), F32),
        V((1, l1.total, LANES), F32),
        V((1, l1.total, LANES), F32),
        V((2, (l2.rows + 2) * l2.pitch, LANES), F32),
        V((2, l2.total, LANES), F32),
        V((1, l0.cols, LANES), F32),
        V((2, l1.rows * l1.cols, LANES), F32),
        V((4, l2.rows * l2.cols, LANES), F32),
        pltpu.SemaphoreType.DMA((11,)),
    ]
    outs = pl.pallas_call(
        functools.partial(body, levels),
        out_shape=[jax.ShapeDtypeStruct(f.shape, BF16) for f in feats],
        in_specs=[vmem] * 38 + [any_] * 2 + [vmem] * 11 + [any_],
        out_specs=[vmem] * 4,
        scratch_shapes=scratch,
        compiler_params=pltpu.CompilerParams(vmem_limit_bytes=60 * 2**20),
    )(*feats, *halos, *weights, *biases, up1, up2, up3, mid0, mid1, fin0, fin1, fin2)
    return tuple(o.transpose(2, 0, 1) for o in outs)


def solution(mesh):
    tiled = P(None, "ty", "tx")
    return jax.shard_map(
        per_device,
        mesh=mesh,
        in_specs=(tiled,) * 4 + (P(),) * 16,
        out_specs=(tiled,) * 4,
        check_vma=False,
    )
```

```python
import functools

import jax
import jax.numpy as jnp
from jax import lax
from jax.experimental import pallas as pl
from jax.experimental.pallas import tpu as pltpu
from jax.sharding import PartitionSpec as P

RIMS = (7, 3, 1, 0)
GROUP = 3
LANES = 128
NT = (((1,), (1,)), ((), ()))
NN = (((1,), (0,)), ((), ()))
WAYS = [(dy, dx) for dy in (-1, 0, 1) for dx in (-1, 0, 1) if dy or dx]
F32, BF16 = jnp.float32, jnp.bfloat16


def up_to(n, m):
    return -(-n // m) * m


class Level:
    def __init__(self, level, shape):
        self.rows, self.cols, self.chan = shape
        self.rim = RIMS[level]
        self.low = self.rim + 2
        self.pitch = up_to(self.cols + 2 + self.low, 8)
        self.lead = self.low + 1
        self.tail = self.pitch - self.cols
        self.planes = up_to(self.chan, LANES) // LANES
        self.near = up_to(self.low, 8)
        self.total = (self.lead + self.rows + 4) * self.pitch
        self.folds = 2 if 2 * self.chan <= LANES else 1
        self.lines = self.rows // self.folds
        self.wide = LANES if self.folds == 2 else self.chan

    def at(self, row, col=0):
        return (row + self.lead) * self.pitch + col

    def first(self):
        start = self.at(-self.rim - 1) - self.tail
        return start, self.at(self.rows) + self.cols + 8 - start

    def second(self):
        start = self.at(-self.rim) - self.tail
        return start, self.at(self.rows - 1) + self.cols - start


def window(lv, way):
    lines = lv.lines
    if way[0] == 0:
        return 0, lines
    return (lines - lv.near, lv.near) if way[0] > 0 else (0, 8)


def message(lv, way):
    dy, dx = way
    if dx == 0:
        rows = lv.low if dy > 0 else 2
        return (rows, lv.cols // lv.folds, lv.wide)
    return (lv.low if dx > 0 else 2, window(lv, way)[1], lv.wide)


def on_map(way, side):
    ok = True
    for step, axis in zip(way, ("ty", "tx")):
        if step:
            place = lax.axis_index(axis) + side * step
            ok = ok & (place >= 0) & (place < lax.axis_size(axis))
    return ok


def exchange(levels, *refs):
    feats, outs, turned = refs[:4], refs[4:36], refs[36]
    rows_sent, cols_sent = refs[37:39], refs[39:47]
    stage, maps, side, send, recv = refs[47:]
    here = {a: lax.axis_index(a) for a in ("ty", "tx")}
    barrier = pltpu.get_barrier_semaphore()
    l0 = levels[0]

    def there(way):
        return {"ty": here["ty"] + way[0], "tx": here["tx"] + way[1]}

    count = 0
    for way in WAYS:
        ok = on_map(way, 1)

        @pl.when(ok)
        def _(way=way):
            pl.semaphore_signal(barrier, 1, device_id=there(way))

        count = count + jnp.where(ok, 1, 0)

    C, R, W = l0.chan, l0.rows, l0.cols

    tall, wide = R + 1, W + 1

    def load(i, _):
        for j in range(8):
            at = pl.multiple_of(i * 8 * tall, 8) + j * tall
            stage[pl.ds(at, R), :] = feats[0][8 * i + j].astype(F32)
        return 0

    lax.fori_loop(0, C // 8, load, 0)

    def turn(i, _):
        for j in range(8):
            r = 8 * i + j
            value = stage[pl.ds(r, C, stride=tall), :].T
            at = pl.multiple_of(i * 8 * wide, 8) + j * wide
            maps[pl.ds(at, W), 0:C] = value
            turned[r] = value.astype(BF16)
        return 0

    lax.fori_loop(0, R // 8, turn, 0)

    def folded(a, b):
        ids = lax.broadcasted_iota(jnp.int32, a.shape, 1)
        a, b = jnp.where(ids < C, a, 0.0), jnp.where(ids < C, b, 0.0)
        return (a + pltpu.roll(b, LANES // 2, 1)).astype(BF16)

    half = W // 2
    for to, first, n in ((rows_sent[0], R - l0.low, l0.low), (rows_sent[1], 0, 2)):
        for i in range(n):
            at = (first + i) * wide
            to[i] = folded(maps[at : at + half, :], maps[at + half : at + W, :])
    half = R // 2
    for to, first, n in ((cols_sent[0], W - l0.low, l0.low), (cols_sent[1], 0, 2)):
        for i in range(n):
            a = maps[pl.ds(first + i, half, stride=wide), :]
            to[i] = folded(a, maps[pl.ds(half * wide + first + i, half, stride=wide), :])
    for l in range(1, 4):
        lv = levels[l]
        for d, (base, n) in enumerate(((lv.cols - 8, lv.low), (0, 2))):
            to = cols_sent[2 * l + d]
            for p in range(lv.planes):
                w = min(LANES, lv.chan - p * LANES)
                slot = 6 * l + 3 * d + p
                for r in range(lv.rows):
                    block = feats[l][r, base : base + 8, p * LANES : p * LANES + w]
                    side[slot, 9 * r : 9 * r + 8, 0:w] = block.astype(F32)
                for i in range(n):
                    at = i + (8 - n if d == 0 else 0)
                    value = side[slot, pl.ds(at, lv.rows, stride=9), 0:w]
                    to[i, :, p * LANES : p * LANES + w] = value.astype(BF16)

    pl.semaphore_wait(barrier, count)

    def copy(l, k):
        lv, way = levels[l], WAYS[k]
        dy, dx = way
        if dx:
            src = cols_sent[2 * l + (0 if dx > 0 else 1)]
            first, n = window(lv, way)
            if dy:
                src = src.at[:, pl.ds(first, n)]
        elif l == 0:
            src = rows_sent[0 if dy > 0 else 1]
        else:
            src = feats[l].at[pl.ds(lv.rows - lv.low, lv.low) if dy > 0 else pl.ds(0, 2)]
        return pltpu.make_async_remote_copy(
            src, outs[8 * l + k], send.at[8 * l + k], recv.at[8 * l + k], device_id=there(way)
        )

    for k, way in enumerate(WAYS):

        @pl.when(on_map(way, 1))
        def _(k=k):
            for l in range(4):
                copy(l, k).start()

    for k, way in enumerate(WAYS):

        @pl.when(on_map(way, 1))
        def _(k=k):
            for l in range(4):
                copy(l, k).wait_send()

        @pl.when(on_map(way, -1))
        def _(k=k):
            for l in range(4):
                copy(l, k).wait_recv()


def halos_of(levels, feats):
    V = pltpu.VMEM
    l0 = levels[0]
    shapes = [jax.ShapeDtypeStruct(message(lv, way), BF16) for lv in levels for way in WAYS]
    shapes.append(jax.ShapeDtypeStruct((l0.rows, l0.cols, l0.chan), BF16))
    vmem, hbm = pl.BlockSpec(memory_space=pltpu.VMEM), pl.BlockSpec(memory_space=pl.ANY)
    scratch = [V(message(l0, (d, 0)), BF16) for d in (1, -1)]
    scratch += [V(message(lv, (0, d)), BF16) for lv in levels for d in (1, -1)]
    scratch += [
        V((l0.chan * (l0.rows + 1), l0.cols), F32),
        V((l0.rows * (l0.cols + 1), LANES), F32),
        V((24, 9 * levels[1].rows, LANES), F32),
        pltpu.SemaphoreType.DMA((32,)),
        pltpu.SemaphoreType.DMA((32,)),
    ]
    return pl.pallas_call(
        functools.partial(exchange, levels),
        out_shape=shapes,
        in_specs=[vmem] * 4,
        out_specs=[hbm] * 32 + [vmem],
        scratch_shapes=scratch,
        compiler_params=pltpu.CompilerParams(collective_id=0, has_side_effects=True),
    )(*feats)


def chunking(length, most):
    n = -(-length // most)
    return n, up_to(-(-length // n), 16)


def prepare(levels, given, made, stage):
    w0_in, w1_in, mid0, mid1, fin0, fin1 = given
    w0, w1, wd0, wd1a, wd1v, wd2, wd2v = made
    c0, c1, c2, c3 = (lv.chan for lv in levels)

    def blank(ref, row, n, col, m):
        ref[row : row + n, col : col + m] = jnp.zeros((n, m), BF16)

    def shifted(ref, row, n, off, width, to):
        def tile(k):
            part = ref[row : row + n, k * LANES : min((k + 1) * LANES, ref.shape[1])].astype(F32)
            if part.shape[1] < LANES:
                part = jnp.concatenate([part, jnp.zeros((n, LANES - part.shape[1]), F32)], axis=1)
            return part

        k, s = divmod(off, LANES)
        a = tile(k)
        ids = lax.broadcasted_iota(jnp.int32, a.shape, 1)
        if s + width > LANES:
            a = jnp.where(ids >= s, a, tile(k + 1))
        if (to - s) % LANES:
            a = pltpu.roll(a, (to - s) % LANES, 1)
        if width == LANES:
            return a
        return jnp.where((ids >= to) & (ids < to + width), a, 0.0)

    for i in range(2):
        ref = w0_in.at[i]
        for q in range(3):
            offs = [c0 * (3 * p + q) for p in range(3)]
            cut = LANES - 2 * c0
            tile = shifted(ref, 0, c0, offs[0], c0, 0) + shifted(ref, 0, c0, offs[1], c0, c0)
            tile = tile + shifted(ref, 0, c0, offs[2], cut, 2 * c0)
            w0[i, q * LANES : q * LANES + c0, 0:LANES] = tile.astype(BF16)
            tile = shifted(ref, 0, c0, offs[2] + cut, c0 - cut, 0)
            w0[i, q * LANES : q * LANES + c0, LANES : 2 * LANES] = tile.astype(BF16)
        ref = w1_in.at[i]
        for q in range(3):
            blank(w1.at[i], q * LANES + c1, LANES - c1, 0, 3 * LANES)
            for p in range(3):
                tile = shifted(ref, 0, c1, c1 * (3 * p + q), c1, 0)
                w1[i, q * LANES : q * LANES + c1, p * LANES : (p + 1) * LANES] = tile.astype(BF16)

    def apart(ref, first, to, row):
        for t in range(9):
            tile = shifted(ref, first, c1, c1 * t, c1, 0)
            to[row : row + c1, t * LANES : (t + 1) * LANES] = tile.astype(BF16)

    blank(wd1a, c2, 2 * LANES - c2, 0, 9 * LANES)
    blank(wd1a, 2 * LANES + c1, LANES - c1, 0, 9 * LANES)
    for k in range(c2 // c1):
        apart(fin1.at[0], k * c1, wd1a, k * c1)
    apart(mid1.at[0, 0], 0, wd1a, 2 * LANES)
    for k in range(c3 // c1):
        apart(fin1.at[0], c2 + k * c1, wd2v, k * c1)

    tall = up_to(9 * c0, LANES)

    def turned():
        return stage[0:LANES, 0:tall].T.astype(BF16)

    stage[0:LANES, 0:tall] = jnp.zeros((LANES, tall), F32)
    for k in range(2):
        stage[k * c0 : (k + 1) * c0, 0 : 9 * c0] = mid0[0, k].astype(F32)
    flat = turned()
    for t in range(9):
        wd0[t * LANES : t * LANES + c0, LANES : 2 * LANES] = flat[t * c0 : (t + 1) * c0, :]
        wd0[t * LANES : t * LANES + c0, 0:LANES] = fin0[t * c0 : (t + 1) * c0, 0:LANES]
        blank(wd0, t * LANES + c0, LANES - c0, 0, 2 * LANES)
    stage[0:LANES, 0:tall] = jnp.zeros((LANES, tall), F32)
    stage[c2 - LANES : c2 - LANES + c0, 0 : 9 * c0] = mid0[0, 2].astype(F32)
    flat = turned()
    for t in range(9):
        blank(wd1v, t * LANES + c0, c0, 0, LANES)
        wd1v[t * LANES + c0 : t * LANES + 2 * c0, LANES : 2 * LANES] = flat[t * c0 : (t + 1) * c0, :]
        blank(wd1v, t * LANES + 2 * c0, LANES - 2 * c0, 0, 2 * LANES)
    depth = wd2.shape[0] // 9
    for t in range(9):
        wd1v[t * LANES : t * LANES + c0, 0:LANES] = shifted(fin0, t * c0, c0, c1, LANES, 0).astype(BF16)
        tile = shifted(fin0, t * c0, c0, c1 + LANES, c2 - LANES, 0)
        wd1v[t * LANES : t * LANES + c0, LANES : 2 * LANES] = tile.astype(BF16)
        row = t * depth + c2
        wd2[row : row + depth - c2, :] = jnp.zeros((depth - c2, c3), BF16)
        for j in range(c3 // LANES):
            tile = shifted(fin0, t * c0, c0, c1 + c2 + j * LANES, LANES, 0)
            wd2[row : row + c0, j * LANES : (j + 1) * LANES] = tile.astype(BF16)


def body(levels, *refs):
    refs = list(refs)

    def take(n):
        out = refs[:n]
        del refs[:n]
        return out

    feats, halos = take(4), take(32)
    w0_in, w1_in, w2_hbm, w3_hbm = take(4)
    biases = take(4)
    up1, up2, up3, mid0, mid1, fin0, fin1, fin2_hbm = take(8)
    outs = take(4)
    xs, hs = take(4), take(4)
    spread, odd, cols2, cols3 = take(4)
    w2, w3 = take(2)
    w0, w1, wd0, wd1a, wd1v, wd2, wd2v, stage, bpad = take(9)
    t01, v0, t2, v1, u0, u1, u2, last = take(8)
    (sems,) = take(1)
    l0, l1, l2, l3 = levels
    copies = [pltpu.make_async_copy(a, b, sems.at[i]) for i, (a, b) in enumerate(((w2_hbm, w2), (w3_hbm, w3)))]
    depth = wd2.shape[0] // 9
    for ref in (w0, bpad):
        ref[...] = jnp.zeros_like(ref)
    fin2_copies = [
        pltpu.make_async_copy(
            fin2_hbm.at[pl.ds(t * l2.chan, l2.chan)], wd2.at[pl.ds(t * depth, l2.chan)], sems.at[2 + t]
        )
        for t in range(9)
    ]
    for c in copies + fin2_copies:
        c.start()

    prepare(levels, (w0_in, w1_in, mid0, mid1, fin0, fin1), (w0, w1, wd0, wd1a, wd1v, wd2, wd2v), stage)
    for l in (0, 1):
        bpad[l, 0:2, 0 : levels[l].chan] = biases[l][...]

    ty, tx = lax.axis_index("ty"), lax.axis_index("tx")
    top, bottom = ty == 0, ty == lax.axis_size("ty") - 1
    left, right = tx == 0, tx == lax.axis_size("tx") - 1

    def lane(shape):
        return lax.broadcasted_iota(jnp.int32, shape, len(shape) - 1)

    def rows_loop(n, run):
        def step(i, _):
            run(i)
            return 0

        if n == 1:
            run(0)
        else:
            lax.fori_loop(0, n, step, 0)

    def put(l, at, value):
        lv = levels[l]
        for p in range(lv.planes):
            w = min(LANES, lv.chan - p * LANES)
            part = value[:, p * LANES : p * LANES + w]
            if w < LANES:
                part = jnp.concatenate([part, jnp.zeros((part.shape[0], LANES - w), F32)], axis=1)
            xs[l][p, pl.ds(at, value.shape[0]), :] = part

    for l, lv in enumerate(levels):
        for p in range(lv.planes):
            for i in range(lv.lead + lv.rows + 2):
                at = i * lv.pitch + lv.cols
                xs[l][p, at : at + lv.tail, :] = jnp.zeros((lv.tail, LANES), F32)

        @pl.when(top)
        def _(l=l, lv=lv):
            for p in range(lv.planes):
                xs[l][p, 0 : lv.at(0) - lv.tail, :] = jnp.zeros((lv.at(0) - lv.tail, LANES), F32)

        @pl.when(bottom)
        def _(l=l, lv=lv):
            for p in range(lv.planes):
                xs[l][p, lv.at(lv.rows) : lv.total, :] = jnp.zeros((lv.total - lv.at(lv.rows), LANES), F32)

    for l, lv in enumerate(levels):

        def place(source, row, l=l, lv=lv):
            def run(i):
                at = pl.multiple_of((i + row + lv.lead) * lv.pitch, 8)
                put(l, at, source[i].astype(F32))

            rows_loop(source.shape[0], run)

        def place_rows(source, row, l=l, lv=lv):
            if lv.folds == 1:
                return place(source, row)
            half = lv.cols // 2
            for i in range(source.shape[0]):
                value = source[i].astype(F32)
                put(l, lv.at(row + i), value[:, : lv.chan])
                put(l, lv.at(row + i, half), pltpu.roll(value, LANES // 2, 1)[:, : lv.chan])

        def place_cols(source, way, l=l, lv=lv):
            dy, dx = way
            for i in range(source.shape[0]):
                col = i - lv.low if dx > 0 else lv.cols + i
                value = source[i].astype(F32)
                both = [value]
                if lv.folds == 2:
                    both = [value, pltpu.roll(value, LANES // 2, 1)]
                if dy > 0:
                    pieces = [(-lv.low, both[-1][lv.near - lv.low :])]
                elif dy < 0:
                    pieces = [(lv.rows, both[0][:2])]
                else:
                    pieces = [(j * lv.lines, v) for j, v in enumerate(both)]
                for row, v in pieces:
                    for p in range(lv.planes):
                        w = min(LANES, lv.chan - p * LANES)
                        at = pl.ds(lv.at(row, col), v.shape[0], stride=lv.pitch)
                        part = v[:, p * LANES : p * LANES + w]
                        if w < LANES:
                            part = jnp.concatenate([part, jnp.zeros((v.shape[0], LANES - w), F32)], axis=1)
                        xs[l][p, at, :] = part

        place(feats[l], 0)
        for k, way in enumerate(WAYS):

            @pl.when(on_map(way, -1))
            def _(k=k, way=way):
                source = halos[8 * l + k]
                if way[1]:
                    place_cols(source, way)
                else:
                    place_rows(source, -lv.low if way[0] > 0 else lv.rows)

    def blank(ref, lv, low, high):
        planes = ref.shape[0]

        def columns(col, n):
            start = lv.at(-low - 1)
            count = low + 1 + lv.rows + high
            for c in range(col, col + n):
                for p in range(planes):
                    ref[p, pl.ds(start + c, count, stride=lv.pitch), :] = jnp.zeros((count, LANES), F32)

        def rows(row, n):
            for p in range(planes):
                size = n * lv.pitch
                ref[p, pl.ds(lv.at(row) - lv.tail + 2, size), :] = jnp.zeros((size, LANES), F32)

        pl.when(left)(lambda: columns(lv.pitch - low, low))
        if high:
            pl.when(right)(lambda: columns(lv.cols, high))
            pl.when(bottom)(lambda: rows(lv.rows, high))

        pl.when(top)(lambda: rows(-low, low))

    def wide_conv(l, src, dst, weight, bias, span, residual):
        lv = levels[l]
        start, length = span
        n, m = chunking(length, 656)
        group = GROUP if n % GROUP == 0 else 1
        C = lv.chan

        def run(i, j):
            base = pl.multiple_of(start + (i * group + j) * m, 8)
            a, b, c = (
                src[0, pl.ds(pl.multiple_of(base - 8 + d * lv.pitch, 8), m + 16), :] for d in (-1, 0, 1)
            )
            if 3 * C <= 2 * LANES:
                ids = lane(a.shape)
                moved = pltpu.roll(c, 2 * C, 1)
                tile0 = a + pltpu.roll(b, C, 1) + jnp.where(ids >= 2 * C, moved, 0.0)
                tile1 = jnp.where(ids < 3 * C - LANES, moved, 0.0)
                lhs = jnp.concatenate([tile0.astype(BF16), tile1.astype(BF16)], axis=1)
            else:
                lhs = jnp.concatenate([a.astype(BF16), b.astype(BF16), c.astype(BF16)], axis=1)
            o = lax.dot_general(lhs, weight[...], NT, preferred_element_type=F32)
            for q in range(3):
                spread[3 * j + q, 0 : m + 16, :] = o[:, q * LANES : (q + 1) * LANES]
            y = spread[3 * j, 7 : 7 + m, :] + spread[3 * j + 1, 8 : 8 + m, :] + spread[3 * j + 2, 9 : 9 + m, :]
            y = y + bias
            if residual:
                y = y + dst[0, pl.ds(base, m), :]
            dst[0, pl.ds(base, m), :] = jnp.maximum(y, 0.0)

        def several(i):
            for j in range(group):
                run(i, j)

        rows_loop(n // group, several)

    def offset(lv, t):
        return (t // 3 - 1) * lv.pitch + t % 3 - 1

    def deep_conv2(src, dst, weight, bias, span, residual):
        lv = l2
        start, length = span
        m = up_to(length, 16)
        total = lv.total
        p0, p1 = src[0, :, :], src[1, :, :]
        ids = lane((total, LANES))
        r0, r1 = pltpu.roll(p0, 64, 1), pltpu.roll(p1, 64, 1)
        odd[0, :, :] = jnp.where(ids >= 64, r0, 0.0)
        odd[1, :, :] = jnp.where(ids < 64, r0, r1)

        def piece(ref, p, t):
            return ref[p, pl.ds(start + offset(lv, t), m), :]

        for t in range(0, 9, 2):
            k = 3 * (t // 2) * LANES
            cols2[0:m, k : k + 128] = piece(src, 0, t).astype(BF16)
            tile = piece(src, 1, t)
            if t == 8:
                cols2[0:m, k + 128 : k + 192] = tile[:, 0:64].astype(BF16)
            else:
                cols2[0:m, k + 128 : k + 256] = (tile + piece(odd, 0, t + 1)).astype(BF16)
                cols2[0:m, k + 256 : k + 384] = piece(odd, 1, t + 1).astype(BF16)
        y = lax.dot_general(cols2[0:m, :], weight, NT, preferred_element_type=F32) + bias
        for p in range(2):
            w = min(LANES, lv.chan - p * LANES)
            part = y[:, p * LANES : p * LANES + w]
            if residual:
                part = part + dst[p, pl.ds(start, m), 0:w]
            dst[p, pl.ds(start, m), 0:w] = jnp.maximum(part, 0.0)

    def deep_conv3(src, dst, weight, bias, span, residual):
        lv = l3
        start, length = span
        m = up_to(length, 16)
        for t in range(9):
            for p in range(lv.planes):
                k = (t * lv.planes + p) * LANES
                cols3[0:m, k : k + LANES] = src[p, pl.ds(start + offset(lv, t), m), :].astype(BF16)
        y = lax.dot_general(cols3[0:m, :], weight, NT, preferred_element_type=F32) + bias
        for p in range(lv.planes):
            part = y[:, p * LANES : (p + 1) * LANES]
            if residual:
                part = part + dst[p, pl.ds(start, m), :]
            dst[p, pl.ds(start, m), :] = jnp.maximum(part, 0.0)

    for l in (0, 1):
        lv = levels[l]
        wide_conv(l, xs[l], hs[l], (w0, w1)[l].at[0], bpad[l, 0:1, :], lv.first(), False)
        blank(hs[l], lv, lv.rim + 1, 1)
        wide_conv(l, hs[l], xs[l], (w0, w1)[l].at[1], bpad[l, 1:2, :], lv.second(), True)
        blank(xs[l], lv, lv.rim, 0)

    hs[2][1, :, :] = jnp.zeros((l2.total, LANES), F32)
    copies[0].wait()
    deep_conv2(xs[2], hs[2], w2[0], biases[2][0:1, :], l2.first(), False)
    blank(hs[2], l2, l2.rim + 1, 1)
    deep_conv2(hs[2], xs[2], w2[1], biases[2][1:2, :], l2.second(), True)
    blank(xs[2], l2, l2.rim, 0)
    copies[1].wait()
    deep_conv3(xs[3], hs[3], w3[0], biases[3][0:1, :], l3.first(), False)
    blank(hs[3], l3, 1, 1)
    deep_conv3(hs[3], xs[3], w3[1], biases[3][1:2, :], l3.second(), True)

    def gathered(src, plane, big, small, i, t, width=None):
        width = small.pitch if width is None else width
        at = (2 * i + t // 3 - 1 + big.lead) * big.pitch + 2 * (small.cols - width) + t % 3 - 1
        return src[plane, pl.ds(at, width, stride=2), :]

    rim = RIMS[1]
    rows = up_to(rim + l1.rows, 4)

    def down0(k):
        i0 = l1.rows - rows + 4 * k
        taps = [
            jnp.concatenate([gathered(xs[0], 0, l0, l1, i0 + r, t) for r in range(4)], axis=0).astype(BF16)
            for t in range(9)
        ]
        o = lax.dot_general(jnp.concatenate(taps, axis=1), wd0[...], NN, preferred_element_type=F32)
        at = pl.multiple_of((i0 + l1.lead) * l1.pitch - l1.tail, 8)
        t01[0, pl.ds(at, 4 * l1.pitch), :] = o[:, 0:LANES]
        v0[0, pl.ds(at, 4 * l1.pitch), :] = jnp.maximum(o[:, LANES:], 0.0)

    count = rows // 4
    group = GROUP if count % GROUP == 0 else 1

    def downs0(k):
        for j in range(group):
            down0(k * group + j)

    rows_loop(count // group, downs0)
    blank(v0, l1, rim, 0)

    rows = l2.rows + 2
    at = l2.at(-2) - l2.tail
    span = rows * l2.pitch

    def down1(src, weight, form):
        taps = [
            jnp.concatenate([gathered(src, 0, l1, l2, i, t) for i in range(-2, l2.rows)], axis=0).astype(BF16)
            for t in range(9)
        ]
        return lax.dot_general(jnp.concatenate(taps, axis=1), weight[...], form, preferred_element_type=F32)

    o = down1(xs[1], wd1a, NT)
    e = down1(v0, wd1v, NN)
    second = o[:, LANES : 2 * LANES] + e[:, LANES : 2 * LANES]
    ids = lane(second.shape)
    t2[0, 0:span, :] = o[:, 0:LANES] + e[:, 0:LANES]
    t2[1, 0:span, :] = second
    v1[0, pl.ds(at, span), :] = jnp.where(ids >= 64, jnp.maximum(second, 0.0), 0.0)
    v1[1, pl.ds(at, span), :] = jnp.maximum(o[:, 2 * LANES :], 0.0)
    blank(v1, l2, 1, 0)
    def tap3(p, t):
        parts = []
        for i in range(l3.rows):
            piece = gathered(xs[2] if p < 2 else v1, p if p < 2 else 1, l2, l3, i, t, l3.cols)
            if p == 1:
                piece = piece + gathered(v1, 0, l2, l3, i, t, l3.cols)
            parts.append(piece)
        return jnp.concatenate(parts, axis=0).astype(BF16)

    taps = jnp.concatenate([tap3(2, t) for t in range(9)], axis=1)
    t3 = lax.dot_general(taps, wd2v[...], NT, preferred_element_type=F32)
    taps = jnp.concatenate([tap3(p, t) for t in range(9) for p in range(2)], axis=1)
    for c in fin2_copies:
        c.wait()
    t3 = t3 + lax.dot_general(taps, wd2[...], NN, preferred_element_type=F32)

    def center(l, i):
        lv = levels[l]
        parts = [xs[l][p, pl.ds(lv.at(i), lv.cols), :] for p in range(lv.planes)]
        return jnp.concatenate(parts, axis=1)[:, : lv.chan] if lv.planes > 1 else parts[0][:, : lv.chan]

    a3 = jnp.concatenate([center(3, i) for i in range(l3.rows)], axis=0)
    y3 = jnp.maximum(a3 + t3, 0.0).astype(BF16)
    for i in range(l3.rows):
        outs[3][i, :, :] = y3[i * l3.cols : (i + 1) * l3.cols, :]

    c0, c1, c2 = l0.chan, l1.chan, l2.chan
    a3 = a3.astype(BF16)
    up3_0 = lax.dot_general(a3, up3[0, 0:c0, :], NT, preferred_element_type=F32)
    up3_1 = lax.dot_general(a3, up3[0, c0 : c0 + c1, :], NT, preferred_element_type=F32)
    up3_2 = lax.dot_general(a3, up3[0, c0 + c1 :, :], NT, preferred_element_type=F32)

    def enlarge(value, dst, plane, width, rows, cols):
        for i in range(rows):
            line = value[i * cols : (i + 1) * cols, :]
            for di in range(2):
                for dj in range(2):
                    base = (2 * i + di) * 2 * cols + dj
                    dst[plane, pl.ds(base, cols, stride=2), 0:width] = line

    enlarge(up3_0, u2, 0, c0, l3.rows, l3.cols)
    enlarge(up3_1, u2, 1, c1, l3.rows, l3.cols)
    enlarge(up3_2[:, 0:LANES], u2, 2, LANES, l3.rows, l3.cols)
    enlarge(up3_2[:, LANES:], u2, 3, c2 - LANES, l3.rows, l3.cols)
    a2 = jnp.concatenate([center(2, i) for i in range(l2.rows)], axis=0)
    a2b = a2.astype(BF16)
    up2_0 = lax.dot_general(a2b, up2[0, 0:c0, :], NT, preferred_element_type=F32) + u2[0, :, 0:c0]
    up2_1 = lax.dot_general(a2b, up2[0, c0:, :], NT, preferred_element_type=F32) + u2[1, :, 0:c1]
    for i in range(l2.rows):
        for p in range(2):
            w = min(LANES, c2 - p * LANES)
            line = xs[2][p, pl.ds(l2.at(i), l2.cols), 0:w]
            line = line + t2[p, pl.ds((i + 2) * l2.pitch + l2.tail, l2.cols), 0:w]
            line = line + u2[2 + p, pl.ds(i * l2.cols, l2.cols), 0:w]
            outs[2][i, :, p * LANES : p * LANES + w] = jnp.maximum(line, 0.0).astype(BF16)
    enlarge(up2_0, u1, 0, c0, l2.rows, l2.cols)
    enlarge(up2_1, u1, 1, c1, l2.rows, l2.cols)

    def join1(k):
        lines = []
        for r in range(4):
            i = 4 * k + r
            at = pl.multiple_of((i + l1.lead) * l1.pitch, 8)
            line = xs[1][0, pl.ds(at, l1.cols), 0:c1]
            lines.append(line)
            total = line + t01[0, pl.ds(at, l1.cols), 0:c1]
            total = total + u1[1, pl.ds(pl.multiple_of(i * l1.cols, 8), l1.cols), 0:c1]
            outs[1][i, :, :] = jnp.maximum(total, 0.0).astype(BF16)
        a1 = jnp.concatenate(lines, axis=0).astype(BF16)
        n = 4 * l1.cols
        y = lax.dot_general(a1, up1[0], NT, preferred_element_type=F32)
        y = y + u1[0, pl.ds(pl.multiple_of(k * n, 8), n), 0:c0]
        for r in range(4):
            line = y[r * l1.cols : (r + 1) * l1.cols, :]
            for dj in range(2):
                u0[0, pl.ds(dj, l1.cols, stride=2), 0:c0] = line
            up = u0[0, 0 : l0.cols, 0:c0]
            for di in range(2):
                i = 2 * (4 * k + r) + di
                at = pl.multiple_of((i + l0.lead) * l0.pitch, 8)
                total = jnp.maximum(xs[0][0, pl.ds(at, l0.cols), 0:c0] + up, 0.0)
                last[pl.ds(i, c0, stride=l0.rows + 1), :] = total.T

    rows_loop(l1.rows // 4, join1)

    def leave(k):
        for j in range(8):
            at = pl.multiple_of(8 * k * (l0.rows + 1), 8) + j * (l0.rows + 1)
            outs[0][8 * k + j] = last[pl.ds(at, l0.rows), :].astype(BF16)

    rows_loop(c0 // 8, leave)


def per_device(*args):
    feats, weights, biases, rest = args[0:4], args[4:8], args[8:12], args[12:20]
    levels = [Level(l, f.shape[1:] + f.shape[:1]) for l, f in enumerate(feats)]
    feats = [feats[0]] + [f.transpose(1, 2, 0) for f in feats[1:]]
    l0, l1, l2, l3 = levels
    c0, c1, c2, c3 = (lv.chan for lv in levels)
    *halos, first = halos_of(levels, feats)
    feats[0] = first
    up1, up2, up3, mid0, mid1, fin0, fin1, fin2 = rest
    fin0, fin2 = fin0[0].T, fin2[0].T
    vmem, any_ = pl.BlockSpec(memory_space=pltpu.VMEM), pl.BlockSpec(memory_space=pl.ANY)
    V = pltpu.VMEM
    maps = [V((lv.planes, lv.total, LANES), F32) for lv in levels]
    m2, m3 = up_to(l2.first()[1], 16), up_to(l3.first()[1], 16)
    n1 = max(chunking(s[1], 656)[1] for lv in levels[:2] for s in (lv.first(), lv.second()))
    scratch = maps * 2 + [
        V((3 * GROUP, n1 + 16, LANES), F32),
        V((2, l2.total, LANES), F32),
        V((m2, 9 * c2), BF16),
        V((m3, 9 * c3), BF16),
        V(weights[2].shape, BF16),
        V(weights[3].shape, BF16),
        V((2, 3 * LANES, 2 * LANES), BF16),
        V((2, 3 * LANES, 3 * LANES), BF16),
        V((9 * LANES, 2 * LANES), BF16),
        V((3 * LANES, 9 * LANES), BF16),
        V((9 * LANES, 2 * LANES), BF16),
        V((9 * up_to(c2, LANES), c3), BF16),
        V((c3, 9 * LANES), BF16),
        V((LANES, up_to(9 * c0, LANES)), F32),
        V((2, 8, LANES), F32),
        V((1, l1.total, LANES), F32),
        V((1, l1.total, LANES), F32),
        V((2, (l2.rows + 2) * l2.pitch, LANES), F32),
        V((2, l2.total, LANES), F32),
        V((1, l0.cols, LANES), F32),
        V((2, l1.rows * l1.cols, LANES), F32),
        V((4, l2.rows * l2.cols, LANES), F32),
        V((c0 * (l0.rows + 1), l0.cols), F32),
        pltpu.SemaphoreType.DMA((11,)),
    ]
    outs = pl.pallas_call(
        functools.partial(body, levels),
        out_shape=[jax.ShapeDtypeStruct(args[0].shape, BF16)]
        + [jax.ShapeDtypeStruct(f.shape, BF16) for f in feats[1:]],
        in_specs=[vmem] * 38 + [any_] * 2 + [vmem] * 11 + [any_],
        out_specs=[vmem] * 4,
        scratch_shapes=scratch,
        compiler_params=pltpu.CompilerParams(vmem_limit_bytes=60 * 2**20),
    )(*feats, *halos, *weights, *biases, up1, up2, up3, mid0, mid1, fin0, fin1, fin2)
    return (outs[0], *(o.transpose(2, 0, 1) for o in outs[1:]))


def solution(mesh):
    tiled = P(None, "ty", "tx")
    return jax.shard_map(
        per_device,
        mesh=mesh,
        in_specs=(tiled,) * 4 + (P(),) * 16,
        out_specs=(tiled,) * 4,
        check_vma=False,
    )
```

```python
import functools

import jax
import jax.numpy as jnp
from jax import lax
from jax.experimental import pallas as pl
from jax.experimental.pallas import tpu as pltpu
from jax.sharding import PartitionSpec as P

RIMS = (7, 3, 1, 0)
GROUP = 3
MOST = 656
LANES = 128
HALF = 64
NT = (((1,), (1,)), ((), ()))
NN = (((1,), (0,)), ((), ()))
WAYS = [(dy, dx) for dy in (-1, 0, 1) for dx in (-1, 0, 1) if dy or dx]
F32, BF16 = jnp.float32, jnp.bfloat16


def up_to(n, m):
    return -(-n // m) * m


class Level:
    def __init__(self, level, shape):
        self.rows, self.cols, self.chan = shape
        self.rim = RIMS[level]
        self.low = self.rim + 2
        self.pitch = up_to(self.cols + 2 + self.low, 8)
        self.lead = self.low + 1
        self.tail = self.pitch - self.cols
        self.planes = up_to(self.chan, LANES) // LANES
        self.near = up_to(self.low, 8)
        self.total = (self.lead + self.rows + 4) * self.pitch
        self.folds = 2 if 2 * self.chan <= LANES else 1
        self.lines = self.rows // self.folds
        self.wide = LANES if self.folds == 2 else self.chan

    def at(self, row, col=0):
        return (row + self.lead) * self.pitch + col

    def first(self):
        start = self.at(-self.rim - 1) - self.tail
        return start, self.at(self.rows) + self.cols + 8 - start

    def second(self):
        start = self.at(-self.rim) - self.tail
        return start, self.at(self.rows - 1) + self.cols - start


def window(lv, way):
    lines = lv.lines
    if way[0] == 0:
        return 0, lines
    return (lines - lv.near, lv.near) if way[0] > 0 else (0, 8)


def message(lv, way):
    dy, dx = way
    if dx == 0:
        rows = lv.low if dy > 0 else 2
        return (rows, lv.cols // lv.folds, lv.wide)
    return (lv.low if dx > 0 else 2, window(lv, way)[1], lv.wide)


def on_map(way, side):
    ok = True
    for step, axis in zip(way, ("ty", "tx")):
        if step:
            place = lax.axis_index(axis) + side * step
            ok = ok & (place >= 0) & (place < lax.axis_size(axis))
    return ok


def exchange(levels, *refs):
    feats, outs, turned = refs[:4], refs[4:36], refs[36]
    rows_sent, cols_sent = refs[37:39], refs[39:47]
    stage, maps, side, send, recv = refs[47:]
    here = {a: lax.axis_index(a) for a in ("ty", "tx")}
    barrier = pltpu.get_barrier_semaphore()
    l0 = levels[0]

    def there(way):
        return {"ty": here["ty"] + way[0], "tx": here["tx"] + way[1]}

    count = 0
    for way in WAYS:
        ok = on_map(way, 1)

        @pl.when(ok)
        def _(way=way):
            pl.semaphore_signal(barrier, 1, device_id=there(way))

        count = count + jnp.where(ok, 1, 0)

    C, R, W = l0.chan, l0.rows, l0.cols

    tall, wide = R + 1, W + 1

    def load(i, _):
        for j in range(8):
            at = pl.multiple_of(i * 8 * tall, 8) + j * tall
            stage[pl.ds(at, R), :] = feats[0][8 * i + j].astype(F32)
        return 0

    lax.fori_loop(0, C // 8, load, 0)

    def turn(i, _):
        for j in range(8):
            r = 8 * i + j
            value = stage[pl.ds(r, C, stride=tall), :]
            value = jnp.concatenate([value, jnp.zeros((HALF - C, W), F32), value], axis=0).T
            at = pl.multiple_of(i * 8 * wide, 8) + j * wide
            maps[pl.ds(at, W), 0 : HALF + C] = value
            turned[r] = value.astype(BF16)
        return 0

    lax.fori_loop(0, R // 8, turn, 0)

    def folded(a, b):
        ids = lax.broadcasted_iota(jnp.int32, a.shape, 1)
        a, b = jnp.where(ids < C, a, 0.0), jnp.where(ids < C, b, 0.0)
        return (a + pltpu.roll(b, HALF, 1)).astype(BF16)

    half = W // 2
    for to, first, n in ((rows_sent[0], R - l0.low, l0.low), (rows_sent[1], 0, 2)):
        for i in range(n):
            at = (first + i) * wide
            to[i] = folded(maps[at : at + half, :], maps[at + half : at + W, :])
    half = R // 2
    for to, first, n in ((cols_sent[0], W - l0.low, l0.low), (cols_sent[1], 0, 2)):
        for i in range(n):
            a = maps[pl.ds(first + i, half, stride=wide), :]
            to[i] = folded(a, maps[pl.ds(half * wide + first + i, half, stride=wide), :])
    for l in range(1, 4):
        lv = levels[l]
        for d, (base, n) in enumerate(((lv.cols - 8, lv.low), (0, 2))):
            to = cols_sent[2 * l + d]
            for p in range(lv.planes):
                w = min(LANES, lv.chan - p * LANES)
                slot = 6 * l + 3 * d + p
                for r in range(lv.rows):
                    block = feats[l][r, base : base + 8, p * LANES : p * LANES + w]
                    side[slot, 9 * r : 9 * r + 8, 0:w] = block.astype(F32)
                for i in range(n):
                    at = i + (8 - n if d == 0 else 0)
                    value = side[slot, pl.ds(at, lv.rows, stride=9), 0:w]
                    to[i, :, p * LANES : p * LANES + w] = value.astype(BF16)

    pl.semaphore_wait(barrier, count)

    def copy(l, k):
        lv, way = levels[l], WAYS[k]
        dy, dx = way
        if dx:
            src = cols_sent[2 * l + (0 if dx > 0 else 1)]
            first, n = window(lv, way)
            if dy:
                src = src.at[:, pl.ds(first, n)]
        elif l == 0:
            src = rows_sent[0 if dy > 0 else 1]
        else:
            src = feats[l].at[pl.ds(lv.rows - lv.low, lv.low) if dy > 0 else pl.ds(0, 2)]
        return pltpu.make_async_remote_copy(
            src, outs[8 * l + k], send.at[8 * l + k], recv.at[8 * l + k], device_id=there(way)
        )

    for k, way in enumerate(WAYS):

        @pl.when(on_map(way, 1))
        def _(k=k):
            for l in range(4):
                copy(l, k).start()

    for k, way in enumerate(WAYS):

        @pl.when(on_map(way, 1))
        def _(k=k):
            for l in range(4):
                copy(l, k).wait_send()

        @pl.when(on_map(way, -1))
        def _(k=k):
            for l in range(4):
                copy(l, k).wait_recv()


def halos_of(levels, feats):
    V = pltpu.VMEM
    l0 = levels[0]
    shapes = [jax.ShapeDtypeStruct(message(lv, way), BF16) for lv in levels for way in WAYS]
    shapes.append(jax.ShapeDtypeStruct((l0.rows, l0.cols, HALF + l0.chan), BF16))
    vmem, hbm = pl.BlockSpec(memory_space=pltpu.VMEM), pl.BlockSpec(memory_space=pl.ANY)
    scratch = [V(message(l0, (d, 0)), BF16) for d in (1, -1)]
    scratch += [V(message(lv, (0, d)), BF16) for lv in levels for d in (1, -1)]
    scratch += [
        V((l0.chan * (l0.rows + 1), l0.cols), F32),
        V((l0.rows * (l0.cols + 1), LANES), F32),
        V((24, 9 * levels[1].rows, LANES), F32),
        pltpu.SemaphoreType.DMA((32,)),
        pltpu.SemaphoreType.DMA((32,)),
    ]
    return pl.pallas_call(
        functools.partial(exchange, levels),
        out_shape=shapes,
        in_specs=[vmem] * 4,
        out_specs=[hbm] * 32 + [vmem],
        scratch_shapes=scratch,
        compiler_params=pltpu.CompilerParams(collective_id=0, has_side_effects=True),
    )(*feats)


def slot(t):
    p, q = divmod(t, 3)
    return (q, p) if p < 2 else (3 + q // 2, q % 2)


def chunking(length, most):
    n = -(-length // most)
    return n, up_to(-(-length // n), 16)


def prepare(levels, given, made, stage):
    w0_in, w1_in, mid0, mid1, fin0, fin1 = given
    w0, w1, wd0, wd1a, wd1v, wd2, wd2v = made
    c0, c1, c2, c3 = (lv.chan for lv in levels)

    def blank(ref, row, n, col, m):
        ref[row : row + n, col : col + m] = jnp.zeros((n, m), BF16)

    def shifted(ref, row, n, off, width, to):
        def tile(k):
            part = ref[row : row + n, k * LANES : min((k + 1) * LANES, ref.shape[1])].astype(F32)
            if part.shape[1] < LANES:
                part = jnp.concatenate([part, jnp.zeros((n, LANES - part.shape[1]), F32)], axis=1)
            return part

        k, s = divmod(off, LANES)
        a = tile(k)
        ids = lax.broadcasted_iota(jnp.int32, a.shape, 1)
        if s + width > LANES:
            a = jnp.where(ids >= s, a, tile(k + 1))
        if (to - s) % LANES:
            a = pltpu.roll(a, (to - s) % LANES, 1)
        if width == LANES:
            return a
        return jnp.where((ids >= to) & (ids < to + width), a, 0.0)

    w0[...] = jnp.zeros_like(w0)
    for i in range(2):
        for q, rows in ((0, (0,)), (2, (HALF,)), (1, (LANES, LANES + HALF))):
            tile0 = shifted(w0_in.at[i], 0, c0, c0 * q, c0, 0) + shifted(w0_in.at[i], 0, c0, c0 * (3 + q), c0, HALF)
            tile1 = shifted(w0_in.at[i], 0, c0, c0 * (6 + q), c0, 0)
            for row in rows:
                w0[i, row : row + c0, 0:LANES] = tile0.astype(BF16)
                w0[i, row : row + c0, LANES : 2 * LANES] = tile1.astype(BF16)
        for row in (0, LANES):
            blank(w1.at[i], row + c1, LANES - c1, 0, 6 * LANES)
        blank(w1.at[i], LANES, c1, 3 * LANES, 3 * LANES)
        for p in range(3):
            for q, row, col in ((0, 0, p), (2, 0, 3 + p), (1, LANES, p)):
                tile = shifted(w1_in.at[i], 0, c1, c1 * (3 * p + q), c1, 0)
                w1[i, row : row + c1, col * LANES : (col + 1) * LANES] = tile.astype(BF16)

    def apart(ref, first, to, row):
        for t in range(9):
            tile = shifted(ref, first, c1, c1 * t, c1, 0)
            to[row : row + c1, t * LANES : (t + 1) * LANES] = tile.astype(BF16)

    blank(wd1a, c2, 2 * LANES - c2, 0, 9 * LANES)
    blank(wd1a, 2 * LANES + c1, LANES - c1, 0, 9 * LANES)
    for k in range(c2 // c1):
        apart(fin1.at[0], k * c1, wd1a, k * c1)
    apart(mid1.at[0, 0], 0, wd1a, 2 * LANES)
    for k in range(c3 // c1):
        apart(fin1.at[0], c2 + k * c1, wd2v, k * c1)

    tall = up_to(9 * c0, LANES)

    def turned():
        return stage[0:LANES, 0:tall].T.astype(BF16)

    stage[0:LANES, 0:tall] = jnp.zeros((LANES, tall), F32)
    for k in range(2):
        stage[k * c0 : (k + 1) * c0, 0 : 9 * c0] = mid0[0, k].astype(F32)
    flat = turned()
    for t in range(9):
        k, half = slot(t)
        row = k * LANES + half * HALF
        wd0[row : row + c0, LANES : 2 * LANES] = flat[t * c0 : (t + 1) * c0, :]
        wd0[row : row + c0, 0:LANES] = fin0[t * c0 : (t + 1) * c0, 0:LANES]
    for k in range(5):
        blank(wd0, k * LANES + c0, HALF - c0, 0, 2 * LANES)
        n = HALF + c0 if k < 4 else HALF
        blank(wd0, k * LANES + n, LANES - n, 0, 2 * LANES)
    stage[0:LANES, 0:tall] = jnp.zeros((LANES, tall), F32)
    stage[c2 - LANES : c2 - LANES + c0, 0 : 9 * c0] = mid0[0, 2].astype(F32)
    flat = turned()
    for t in range(9):
        blank(wd1v, t * LANES + c0, c0, 0, LANES)
        wd1v[t * LANES + c0 : t * LANES + 2 * c0, LANES : 2 * LANES] = flat[t * c0 : (t + 1) * c0, :]
        blank(wd1v, t * LANES + 2 * c0, LANES - 2 * c0, 0, 2 * LANES)
    depth = wd2.shape[0] // 9
    for t in range(9):
        wd1v[t * LANES : t * LANES + c0, 0:LANES] = shifted(fin0, t * c0, c0, c1, LANES, 0).astype(BF16)
        tile = shifted(fin0, t * c0, c0, c1 + LANES, c2 - LANES, 0)
        wd1v[t * LANES : t * LANES + c0, LANES : 2 * LANES] = tile.astype(BF16)
        row = t * depth + c2
        wd2[row : row + depth - c2, :] = jnp.zeros((depth - c2, c3), BF16)
        for j in range(c3 // LANES):
            tile = shifted(fin0, t * c0, c0, c1 + c2 + j * LANES, LANES, 0)
            wd2[row : row + c0, j * LANES : (j + 1) * LANES] = tile.astype(BF16)


def body(levels, *refs):
    refs = list(refs)

    def take(n):
        out = refs[:n]
        del refs[:n]
        return out

    feats, halos = take(4), take(32)
    w0_in, w1_in, w2_hbm, w3_hbm = take(4)
    biases = take(4)
    up1, up2, up3, mid0, mid1, fin0, fin1, fin2_hbm = take(8)
    outs = take(4)
    xs, hs = take(4), take(4)
    spread, odd, cols2, cols3 = take(4)
    w2, w3 = take(2)
    w0, w1, wd0, wd1a, wd1v, wd2, wd2v, stage, bpad = take(9)
    t01, v0, t2, v1, u0, u1, u2, last = take(8)
    (sems,) = take(1)
    l0, l1, l2, l3 = levels
    copies = [pltpu.make_async_copy(a, b, sems.at[i]) for i, (a, b) in enumerate(((w2_hbm, w2), (w3_hbm, w3)))]
    depth = wd2.shape[0] // 9
    bpad[...] = jnp.zeros_like(bpad)
    fin2_copies = [
        pltpu.make_async_copy(
            fin2_hbm.at[pl.ds(t * l2.chan, l2.chan)], wd2.at[pl.ds(t * depth, l2.chan)], sems.at[2 + t]
        )
        for t in range(9)
    ]
    for c in copies + fin2_copies:
        c.start()

    prepare(levels, (w0_in, w1_in, mid0, mid1, fin0, fin1), (w0, w1, wd0, wd1a, wd1v, wd2, wd2v), stage)
    for l in (0, 1):
        bpad[l, 0:2, 0 : levels[l].chan] = biases[l][...]
    bpad[0, :, :] = bpad[0, :, :] + pltpu.roll(bpad[0, :, :], HALF, 1)

    ty, tx = lax.axis_index("ty"), lax.axis_index("tx")
    top, bottom = ty == 0, ty == lax.axis_size("ty") - 1
    left, right = tx == 0, tx == lax.axis_size("tx") - 1

    def lane(shape):
        return lax.broadcasted_iota(jnp.int32, shape, len(shape) - 1)

    def rows_loop(n, run):
        def step(i, _):
            run(i)
            return 0

        if n == 1:
            run(0)
        else:
            lax.fori_loop(0, n, step, 0)

    def unfolded(value):
        value = value.astype(F32)
        C, out = l0.chan, []
        for v in (value, pltpu.roll(value, HALF, 1)):
            v = jnp.where(lane(v.shape) < C, v, 0.0)
            out.append(v + pltpu.roll(v, HALF, 1))
        return out

    def put(l, at, value):
        lv = levels[l]
        for p in range(lv.planes):
            w = min(LANES, lv.chan - p * LANES)
            part = value if l == 0 else value[:, p * LANES : p * LANES + w]
            if part.shape[1] < LANES:
                pad = jnp.zeros((part.shape[0], LANES - part.shape[1]), F32)
                part = jnp.concatenate([part, pad], axis=1)
            xs[l][p, pl.ds(at, value.shape[0]), :] = part

    for l, lv in enumerate(levels):
        for p in range(lv.planes):
            for i in range(lv.lead + lv.rows + 2):
                at = i * lv.pitch + lv.cols
                xs[l][p, at : at + lv.tail, :] = jnp.zeros((lv.tail, LANES), F32)

        @pl.when(top)
        def _(l=l, lv=lv):
            for p in range(lv.planes):
                xs[l][p, 0 : lv.at(0) - lv.tail, :] = jnp.zeros((lv.at(0) - lv.tail, LANES), F32)

        @pl.when(bottom)
        def _(l=l, lv=lv):
            for p in range(lv.planes):
                xs[l][p, lv.at(lv.rows) : lv.total, :] = jnp.zeros((lv.total - lv.at(lv.rows), LANES), F32)

    for l, lv in enumerate(levels):

        def place(source, row, l=l, lv=lv):
            def run(i):
                at = pl.multiple_of((i + row + lv.lead) * lv.pitch, 8)
                put(l, at, source[i].astype(F32))

            rows_loop(source.shape[0], run)

        def place_rows(source, row, l=l, lv=lv):
            if lv.folds == 1:
                return place(source, row)
            half = lv.cols // 2
            for i in range(source.shape[0]):
                for j, value in enumerate(unfolded(source[i])):
                    put(l, lv.at(row + i, j * half), value)

        def place_cols(source, way, l=l, lv=lv):
            dy, dx = way
            for i in range(source.shape[0]):
                col = i - lv.low if dx > 0 else lv.cols + i
                both = [source[i].astype(F32)] if lv.folds == 1 else unfolded(source[i])
                if dy > 0:
                    pieces = [(-lv.low, both[-1][lv.near - lv.low :])]
                elif dy < 0:
                    pieces = [(lv.rows, both[0][:2])]
                else:
                    pieces = [(j * lv.lines, v) for j, v in enumerate(both)]
                for row, v in pieces:
                    for p in range(lv.planes):
                        w = min(LANES, lv.chan - p * LANES)
                        at = pl.ds(lv.at(row, col), v.shape[0], stride=lv.pitch)
                        part = v if lv.folds == 2 else v[:, p * LANES : p * LANES + w]
                        if part.shape[1] < LANES:
                            part = jnp.concatenate([part, jnp.zeros((v.shape[0], LANES - w), F32)], axis=1)
                        xs[l][p, at, :] = part

        place(feats[l], 0)
        for k, way in enumerate(WAYS):

            @pl.when(on_map(way, -1))
            def _(k=k, way=way):
                source = halos[8 * l + k]
                if way[1]:
                    place_cols(source, way)
                else:
                    place_rows(source, -lv.low if way[0] > 0 else lv.rows)

    def blank(ref, lv, low, high):
        planes = ref.shape[0]

        def columns(col, n):
            start = lv.at(-low - 1)
            count = low + 1 + lv.rows + high
            for c in range(col, col + n):
                for p in range(planes):
                    ref[p, pl.ds(start + c, count, stride=lv.pitch), :] = jnp.zeros((count, LANES), F32)

        def rows(row, n):
            for p in range(planes):
                size = n * lv.pitch
                ref[p, pl.ds(lv.at(row) - lv.tail + 2, size), :] = jnp.zeros((size, LANES), F32)

        pl.when(left)(lambda: columns(lv.pitch - low, low))
        if high:
            pl.when(right)(lambda: columns(lv.cols, high))
            pl.when(bottom)(lambda: rows(lv.rows, high))

        pl.when(top)(lambda: rows(-low, low))

    def paired(piece):
        tiles = [[], [], [], [], []]
        for t in range(9):
            tiles[slot(t)[0]].append(piece(t))
        keep = lane(tiles[0][0].shape) < HALF
        tiles = [jnp.where(keep, *tile) if len(tile) > 1 else tile[0] for tile in tiles]
        return jnp.concatenate([tile.astype(BF16) for tile in tiles], axis=1)

    def wide_conv(l, src, dst, weight, bias, span, residual):
        lv = levels[l]
        start, length = span
        n, m = chunking(length, MOST)
        group = GROUP if n % GROUP == 0 else 1

        def run(i, j):
            base = pl.multiple_of(start + (i * group + j) * m, 8)

            if l == 0:
                a, b, c = (
                    src[0, pl.ds(pl.multiple_of(base - 8 + d * lv.pitch, 8), m + 16), :] for d in (-1, 0, 1)
                )
                pieces = [jnp.where(lane(a.shape) < HALF, a, b), c]
            else:
                pieces = [
                    src[0, pl.ds(base + d * lv.pitch + e, m + 16), :] for e in (-1, 1) for d in (-1, 0, 1)
                ]
            lhs = jnp.concatenate([piece.astype(BF16) for piece in pieces], axis=1)
            o = lax.dot_general(lhs, weight[...], NT, preferred_element_type=F32)
            one, two = spread.at[2 * j], spread.at[2 * j + 1]
            one[0 : m + 16, :] = o[:, 0:LANES]
            two[0 : m + 16, :] = o[:, LANES:]
            if l == 0:
                y = one[7 : 7 + m, :]
                y = jnp.where(lane(y.shape) < HALF, y, one[9 : 9 + m, :])
                y = y + pltpu.roll(y, HALF, 1) + two[8 : 8 + m, :]
            else:
                y = one[0:m, :] + two[1 : 1 + m, :]
            y = y + bias
            if residual:
                y = y + dst[0, pl.ds(base, m), :]
            dst[0, pl.ds(base, m), :] = jnp.maximum(y, 0.0)

        def several(i):
            for j in range(group):
                run(i, j)

        rows_loop(n // group, several)

    def offset(lv, t):
        return (t // 3 - 1) * lv.pitch + t % 3 - 1

    def deep_conv2(src, dst, weight, bias, span, residual):
        lv = l2
        start, length = span
        m = up_to(length, 16)
        total = lv.total
        p0, p1 = src[0, :, :], src[1, :, :]
        ids = lane((total, LANES))
        r0, r1 = pltpu.roll(p0, 64, 1), pltpu.roll(p1, 64, 1)
        odd[0, :, :] = jnp.where(ids >= 64, r0, 0.0)
        odd[1, :, :] = jnp.where(ids < 64, r0, r1)

        def piece(ref, p, t):
            return ref[p, pl.ds(start + offset(lv, t), m), :]

        for t in range(0, 9, 2):
            k = 3 * (t // 2) * LANES
            cols2[0:m, k : k + 128] = piece(src, 0, t).astype(BF16)
            tile = piece(src, 1, t)
            if t == 8:
                cols2[0:m, k + 128 : k + 192] = tile[:, 0:64].astype(BF16)
            else:
                cols2[0:m, k + 128 : k + 256] = (tile + piece(odd, 0, t + 1)).astype(BF16)
                cols2[0:m, k + 256 : k + 384] = piece(odd, 1, t + 1).astype(BF16)
        y = lax.dot_general(cols2[0:m, :], weight, NT, preferred_element_type=F32) + bias
        for p in range(2):
            w = min(LANES, lv.chan - p * LANES)
            part = y[:, p * LANES : p * LANES + w]
            if residual:
                part = part + dst[p, pl.ds(start, m), 0:w]
            dst[p, pl.ds(start, m), 0:w] = jnp.maximum(part, 0.0)

    def deep_conv3(src, dst, weight, bias, span, residual):
        lv = l3
        start, length = span
        m = up_to(length, 16)
        for t in range(9):
            for p in range(lv.planes):
                k = (t * lv.planes + p) * LANES
                cols3[0:m, k : k + LANES] = src[p, pl.ds(start + offset(lv, t), m), :].astype(BF16)
        y = lax.dot_general(cols3[0:m, :], weight, NT, preferred_element_type=F32) + bias
        for p in range(lv.planes):
            part = y[:, p * LANES : (p + 1) * LANES]
            if residual:
                part = part + dst[p, pl.ds(start, m), :]
            dst[p, pl.ds(start, m), :] = jnp.maximum(part, 0.0)

    for l in (0, 1):
        lv = levels[l]
        wide_conv(l, xs[l], hs[l], (w0, w1)[l].at[0], bpad[l, 0:1, :], lv.first(), False)
        blank(hs[l], lv, lv.rim + 1, 1)
        wide_conv(l, hs[l], xs[l], (w0, w1)[l].at[1], bpad[l, 1:2, :], lv.second(), True)
        blank(xs[l], lv, lv.rim, 0)

    hs[2][1, :, :] = jnp.zeros((l2.total, LANES), F32)
    copies[0].wait()
    deep_conv2(xs[2], hs[2], w2[0], biases[2][0:1, :], l2.first(), False)
    blank(hs[2], l2, l2.rim + 1, 1)
    deep_conv2(hs[2], xs[2], w2[1], biases[2][1:2, :], l2.second(), True)
    blank(xs[2], l2, l2.rim, 0)
    copies[1].wait()
    deep_conv3(xs[3], hs[3], w3[0], biases[3][0:1, :], l3.first(), False)
    blank(hs[3], l3, 1, 1)
    deep_conv3(hs[3], xs[3], w3[1], biases[3][1:2, :], l3.second(), True)

    def gathered(src, plane, big, small, i, t, width=None):
        width = small.pitch if width is None else width
        at = (2 * i + t // 3 - 1 + big.lead) * big.pitch + 2 * (small.cols - width) + t % 3 - 1
        return src[plane, pl.ds(at, width, stride=2), :]

    rim = RIMS[1]
    rows = up_to(rim + l1.rows, 4)

    def down0(k):
        i0 = l1.rows - rows + 4 * k
        taps = paired(
            lambda t: jnp.concatenate([gathered(xs[0], 0, l0, l1, i0 + r, t) for r in range(4)], axis=0)
        )
        o = lax.dot_general(taps, wd0[...], NN, preferred_element_type=F32)
        at = pl.multiple_of((i0 + l1.lead) * l1.pitch - l1.tail, 8)
        t01[0, pl.ds(at, 4 * l1.pitch), :] = o[:, 0:LANES]
        v0[0, pl.ds(at, 4 * l1.pitch), :] = jnp.maximum(o[:, LANES:], 0.0)

    count = rows // 4
    group = GROUP if count % GROUP == 0 else 1

    def downs0(k):
        for j in range(group):
            down0(k * group + j)

    rows_loop(count // group, downs0)
    blank(v0, l1, rim, 0)

    rows = l2.rows + 2
    at = l2.at(-2) - l2.tail
    span = rows * l2.pitch

    def down1(src, weight, form):
        taps = [
            jnp.concatenate([gathered(src, 0, l1, l2, i, t) for i in range(-2, l2.rows)], axis=0).astype(BF16)
            for t in range(9)
        ]
        return lax.dot_general(jnp.concatenate(taps, axis=1), weight[...], form, preferred_element_type=F32)

    o = down1(xs[1], wd1a, NT)
    e = down1(v0, wd1v, NN)
    second = o[:, LANES : 2 * LANES] + e[:, LANES : 2 * LANES]
    ids = lane(second.shape)
    t2[0, 0:span, :] = o[:, 0:LANES] + e[:, 0:LANES]
    t2[1, 0:span, :] = second
    v1[0, pl.ds(at, span), :] = jnp.where(ids >= 64, jnp.maximum(second, 0.0), 0.0)
    v1[1, pl.ds(at, span), :] = jnp.maximum(o[:, 2 * LANES :], 0.0)
    blank(v1, l2, 1, 0)
    def tap3(p, t):
        parts = []
        for i in range(l3.rows):
            piece = gathered(xs[2] if p < 2 else v1, p if p < 2 else 1, l2, l3, i, t, l3.cols)
            if p == 1:
                piece = piece + gathered(v1, 0, l2, l3, i, t, l3.cols)
            parts.append(piece)
        return jnp.concatenate(parts, axis=0).astype(BF16)

    taps = jnp.concatenate([tap3(2, t) for t in range(9)], axis=1)
    t3 = lax.dot_general(taps, wd2v[...], NT, preferred_element_type=F32)
    taps = jnp.concatenate([tap3(p, t) for t in range(9) for p in range(2)], axis=1)
    for c in fin2_copies:
        c.wait()
    t3 = t3 + lax.dot_general(taps, wd2[...], NN, preferred_element_type=F32)

    def center(l, i):
        lv = levels[l]
        parts = [xs[l][p, pl.ds(lv.at(i), lv.cols), :] for p in range(lv.planes)]
        return jnp.concatenate(parts, axis=1)[:, : lv.chan] if lv.planes > 1 else parts[0][:, : lv.chan]

    a3 = jnp.concatenate([center(3, i) for i in range(l3.rows)], axis=0)
    y3 = jnp.maximum(a3 + t3, 0.0).astype(BF16)
    for i in range(l3.rows):
        outs[3][i, :, :] = y3[i * l3.cols : (i + 1) * l3.cols, :]

    c0, c1, c2 = l0.chan, l1.chan, l2.chan
    a3 = a3.astype(BF16)
    up3_0 = lax.dot_general(a3, up3[0, 0:c0, :], NT, preferred_element_type=F32)
    up3_1 = lax.dot_general(a3, up3[0, c0 : c0 + c1, :], NT, preferred_element_type=F32)
    up3_2 = lax.dot_general(a3, up3[0, c0 + c1 :, :], NT, preferred_element_type=F32)

    def enlarge(value, dst, plane, width, rows, cols):
        for i in range(rows):
            line = value[i * cols : (i + 1) * cols, :]
            for di in range(2):
                for dj in range(2):
                    base = (2 * i + di) * 2 * cols + dj
                    dst[plane, pl.ds(base, cols, stride=2), 0:width] = line

    enlarge(up3_0, u2, 0, c0, l3.rows, l3.cols)
    enlarge(up3_1, u2, 1, c1, l3.rows, l3.cols)
    enlarge(up3_2[:, 0:LANES], u2, 2, LANES, l3.rows, l3.cols)
    enlarge(up3_2[:, LANES:], u2, 3, c2 - LANES, l3.rows, l3.cols)
    a2 = jnp.concatenate([center(2, i) for i in range(l2.rows)], axis=0)
    a2b = a2.astype(BF16)
    up2_0 = lax.dot_general(a2b, up2[0, 0:c0, :], NT, preferred_element_type=F32) + u2[0, :, 0:c0]
    up2_1 = lax.dot_general(a2b, up2[0, c0:, :], NT, preferred_element_type=F32) + u2[1, :, 0:c1]
    for i in range(l2.rows):
        for p in range(2):
            w = min(LANES, c2 - p * LANES)
            line = xs[2][p, pl.ds(l2.at(i), l2.cols), 0:w]
            line = line + t2[p, pl.ds((i + 2) * l2.pitch + l2.tail, l2.cols), 0:w]
            line = line + u2[2 + p, pl.ds(i * l2.cols, l2.cols), 0:w]
            outs[2][i, :, p * LANES : p * LANES + w] = jnp.maximum(line, 0.0).astype(BF16)
    enlarge(up2_0, u1, 0, c0, l2.rows, l2.cols)
    enlarge(up2_1, u1, 1, c1, l2.rows, l2.cols)

    def join1(k):
        lines = []
        for r in range(4):
            i = 4 * k + r
            at = pl.multiple_of((i + l1.lead) * l1.pitch, 8)
            line = xs[1][0, pl.ds(at, l1.cols), 0:c1]
            lines.append(line)
            total = line + t01[0, pl.ds(at, l1.cols), 0:c1]
            total = total + u1[1, pl.ds(pl.multiple_of(i * l1.cols, 8), l1.cols), 0:c1]
            outs[1][i, :, :] = jnp.maximum(total, 0.0).astype(BF16)
        a1 = jnp.concatenate(lines, axis=0).astype(BF16)
        n = 4 * l1.cols
        y = lax.dot_general(a1, up1[0], NT, preferred_element_type=F32)
        y = y + u1[0, pl.ds(pl.multiple_of(k * n, 8), n), 0:c0]
        for r in range(4):
            line = y[r * l1.cols : (r + 1) * l1.cols, :]
            for dj in range(2):
                u0[0, pl.ds(dj, l1.cols, stride=2), 0:c0] = line
            up = u0[0, 0 : l0.cols, 0:c0]
            for di in range(2):
                i = 2 * (4 * k + r) + di
                at = pl.multiple_of((i + l0.lead) * l0.pitch, 8)
                total = jnp.maximum(xs[0][0, pl.ds(at, l0.cols), 0:c0] + up, 0.0)
                last[pl.ds(i, c0, stride=l0.rows + 1), :] = total.T

    rows_loop(l1.rows // 4, join1)

    def leave(k):
        for j in range(8):
            at = pl.multiple_of(8 * k * (l0.rows + 1), 8) + j * (l0.rows + 1)
            outs[0][8 * k + j] = last[pl.ds(at, l0.rows), :].astype(BF16)

    rows_loop(c0 // 8, leave)


def per_device(*args):
    feats, weights, biases, rest = args[0:4], args[4:8], args[8:12], args[12:20]
    levels = [Level(l, f.shape[1:] + f.shape[:1]) for l, f in enumerate(feats)]
    feats = [feats[0]] + [f.transpose(1, 2, 0) for f in feats[1:]]
    l0, l1, l2, l3 = levels
    c0, c1, c2, c3 = (lv.chan for lv in levels)
    *halos, first = halos_of(levels, feats)
    feats[0] = first
    up1, up2, up3, mid0, mid1, fin0, fin1, fin2 = rest
    fin0, fin2 = fin0[0].T, fin2[0].T
    vmem, any_ = pl.BlockSpec(memory_space=pltpu.VMEM), pl.BlockSpec(memory_space=pl.ANY)
    V = pltpu.VMEM
    maps = [V((lv.planes, lv.total, LANES), F32) for lv in levels]
    m2, m3 = up_to(l2.first()[1], 16), up_to(l3.first()[1], 16)
    most = max(chunking(s[1], MOST)[1] for lv in levels[:2] for s in (lv.first(), lv.second()))
    scratch = maps * 2 + [
        V((2 * GROUP, most + 16, LANES), F32),
        V((2, l2.total, LANES), F32),
        V((m2, 9 * c2), BF16),
        V((m3, 9 * c3), BF16),
        V(weights[2].shape, BF16),
        V(weights[3].shape, BF16),
        V((2, 2 * LANES, 2 * LANES), BF16),
        V((2, 2 * LANES, 6 * LANES), BF16),
        V((5 * LANES, 2 * LANES), BF16),
        V((3 * LANES, 9 * LANES), BF16),
        V((9 * LANES, 2 * LANES), BF16),
        V((9 * up_to(c2, LANES), c3), BF16),
        V((c3, 9 * LANES), BF16),
        V((LANES, up_to(9 * c0, LANES)), F32),
        V((2, 8, LANES), F32),
        V((1, l1.total, LANES), F32),
        V((1, l1.total, LANES), F32),
        V((2, (l2.rows + 2) * l2.pitch, LANES), F32),
        V((2, l2.total, LANES), F32),
        V((1, l0.cols, LANES), F32),
        V((2, l1.rows * l1.cols, LANES), F32),
        V((4, l2.rows * l2.cols, LANES), F32),
        V((c0 * (l0.rows + 1), l0.cols), F32),
        pltpu.SemaphoreType.DMA((11,)),
    ]
    outs = pl.pallas_call(
        functools.partial(body, levels),
        out_shape=[jax.ShapeDtypeStruct(args[0].shape, BF16)]
        + [jax.ShapeDtypeStruct(f.shape, BF16) for f in feats[1:]],
        in_specs=[vmem] * 38 + [any_] * 2 + [vmem] * 11 + [any_],
        out_specs=[vmem] * 4,
        scratch_shapes=scratch,
        compiler_params=pltpu.CompilerParams(vmem_limit_bytes=60 * 2**20),
    )(*feats, *halos, *weights, *biases, up1, up2, up3, mid0, mid1, fin0, fin1, fin2)
    return (outs[0], *(o.transpose(2, 0, 1) for o in outs[1:]))


def solution(mesh):
    tiled = P(None, "ty", "tx")
    return jax.shard_map(
        per_device,
        mesh=mesh,
        in_specs=(tiled,) * 4 + (P(),) * 16,
        out_specs=(tiled,) * 4,
        check_vma=False,
    )
```

```python
import functools

import jax
import jax.numpy as jnp
from jax import lax
from jax.experimental import pallas as pl
from jax.experimental.pallas import tpu as pltpu
from jax.sharding import PartitionSpec as P

RIMS = (7, 3, 1, 0)
GROUP = 3
MOST = 656
LANES = 128
HALF = 64
NT = (((1,), (1,)), ((), ()))
NN = (((1,), (0,)), ((), ()))
WAYS = [(1, 1), (0, 1), (1, 0), (1, -1), (-1, 1), (0, -1), (-1, 0), (-1, -1)]
F32, BF16 = jnp.float32, jnp.bfloat16


def up_to(n, m):
    return -(-n // m) * m


class Level:
    def __init__(self, level, shape):
        self.rows, self.cols, self.chan = shape
        self.rim = RIMS[level]
        self.low = self.rim + 2
        self.pitch = up_to(self.cols + 2 + self.low, 8 if level < 3 else 4)
        self.lead = self.low + 1
        self.tail = self.pitch - self.cols
        self.planes = up_to(self.chan, LANES) // LANES
        self.near = up_to(self.low, 8)
        self.total = (self.lead + self.rows + 4) * self.pitch
        self.folds = 2 if 2 * self.chan <= LANES else 1
        self.lines = self.rows // self.folds
        self.wide = LANES if self.folds == 2 else self.chan

    def at(self, row, col=0):
        return (row + self.lead) * self.pitch + col

    def first(self):
        start = self.at(-self.rim - 1) - self.tail
        return start, self.at(self.rows) + self.cols + 8 - start

    def second(self):
        start = self.at(-self.rim) - self.tail
        return start, self.at(self.rows - 1) + self.cols - start


def window(lv, way):
    lines = lv.lines
    if way[0] == 0:
        return 0, lines
    return (lines - lv.near, lv.near) if way[0] > 0 else (0, 8)


def message(lv, way):
    dy, dx = way
    if dx == 0:
        rows = lv.low if dy > 0 else 2
        return (rows, lv.cols // lv.folds, lv.wide)
    return (lv.low if dx > 0 else 2, window(lv, way)[1], lv.wide)


def on_map(way, side):
    ok = True
    for step, axis in zip(way, ("ty", "tx")):
        if step:
            place = lax.axis_index(axis) + side * step
            ok = ok & (place >= 0) & (place < lax.axis_size(axis))
    return ok


def exchange(levels, *refs):
    given, outs, turned = refs[:4], refs[4:36], refs[36]
    rows_sent, cols_sent = refs[37:39], refs[39:47]
    stage, maps, side, send, recv, local = refs[47:53]
    feats = refs[53:]
    loads = [pltpu.make_async_copy(a, b, local.at[i]) for i, (a, b) in enumerate(zip(given, feats))]
    for load_ in loads:
        load_.start()
    here = {a: lax.axis_index(a) for a in ("ty", "tx")}
    barrier = pltpu.get_barrier_semaphore()
    l0 = levels[0]

    def there(way):
        return {"ty": here["ty"] + way[0], "tx": here["tx"] + way[1]}

    count = 0
    for way in WAYS:
        ok = on_map(way, 1)

        @pl.when(ok)
        def _(way=way):
            pl.semaphore_signal(barrier, 1, device_id=there(way))

        count = count + jnp.where(ok, 1, 0)

    C, R, W = l0.chan, l0.rows, l0.cols
    for load_ in loads:
        load_.wait()

    tall, wide = R + 1, W + 1

    def load(i, _):
        for j in range(8):
            at = pl.multiple_of(i * 8 * tall, 8) + j * tall
            stage[pl.ds(at, R), :] = feats[0][8 * i + j].astype(F32)
        return 0

    lax.fori_loop(0, C // 8, load, 0)

    def turn(i, _):
        for j in range(8):
            r = 8 * i + j
            value = stage[pl.ds(r, C, stride=tall), :]
            value = jnp.concatenate([value, jnp.zeros((HALF - C, W), F32), value], axis=0).T
            at = pl.multiple_of(i * 8 * wide, 8) + j * wide
            maps[pl.ds(at, W), 0 : HALF + C] = value
            turned[r] = value.astype(BF16)
        return 0

    lax.fori_loop(0, R // 8, turn, 0)

    def folded(a, b):
        ids = lax.broadcasted_iota(jnp.int32, a.shape, 1)
        a, b = jnp.where(ids < C, a, 0.0), jnp.where(ids < C, b, 0.0)
        return (a + pltpu.roll(b, HALF, 1)).astype(BF16)

    half = W // 2
    for to, first, n in ((rows_sent[0], R - l0.low, l0.low), (rows_sent[1], 0, 2)):
        for i in range(n):
            at = (first + i) * wide
            to[i] = folded(maps[at : at + half, :], maps[at + half : at + W, :])
    half = R // 2
    for to, first, n in ((cols_sent[0], W - l0.low, l0.low), (cols_sent[1], 0, 2)):
        for i in range(n):
            a = maps[pl.ds(first + i, half, stride=wide), :]
            to[i] = folded(a, maps[pl.ds(half * wide + first + i, half, stride=wide), :])
    for l in range(1, 4):
        lv = levels[l]
        for d, (base, n) in enumerate(((lv.cols - 8, lv.low), (0, 2))):
            to = cols_sent[2 * l + d]
            for p in range(lv.planes):
                w = min(LANES, lv.chan - p * LANES)
                slot = 6 * l + 3 * d + p
                for r in range(lv.rows):
                    block = feats[l][r, base : base + 8, p * LANES : p * LANES + w]
                    side[slot, 9 * r : 9 * r + 8, 0:w] = block.astype(F32)
                for i in range(n):
                    at = i + (8 - n if d == 0 else 0)
                    value = side[slot, pl.ds(at, lv.rows, stride=9), 0:w]
                    to[i, :, p * LANES : p * LANES + w] = value.astype(BF16)

    pl.semaphore_wait(barrier, count)

    def copy(l, k):
        lv, way = levels[l], WAYS[k]
        dy, dx = way
        if dx:
            src = cols_sent[2 * l + (0 if dx > 0 else 1)]
            first, n = window(lv, way)
            if dy:
                src = src.at[:, pl.ds(first, n)]
        elif l == 0:
            src = rows_sent[0 if dy > 0 else 1]
        else:
            src = feats[l].at[pl.ds(lv.rows - lv.low, lv.low) if dy > 0 else pl.ds(0, 2)]
        return pltpu.make_async_remote_copy(
            src, outs[8 * l + k], send.at[8 * l + k], recv.at[8 * l + k], device_id=there(way)
        )

    for k, way in enumerate(WAYS):

        @pl.when(on_map(way, 1))
        def _(k=k):
            for l in range(4):
                copy(l, k).start()

    for k, way in enumerate(WAYS):

        @pl.when(on_map(way, 1))
        def _(k=k):
            for l in range(4):
                copy(l, k).wait_send()

        @pl.when(on_map(way, -1))
        def _(k=k):
            for l in range(4):
                copy(l, k).wait_recv()


def halos_of(levels, feats):
    V = pltpu.VMEM
    l0 = levels[0]
    shapes = [jax.ShapeDtypeStruct(message(lv, way), BF16) for lv in levels for way in WAYS]
    shapes.append(jax.ShapeDtypeStruct((l0.rows, l0.cols, HALF + l0.chan), BF16))
    vmem, hbm = pl.BlockSpec(memory_space=pltpu.VMEM), pl.BlockSpec(memory_space=pl.ANY)
    scratch = [V(message(l0, (d, 0)), BF16) for d in (1, -1)]
    scratch += [V(message(lv, (0, d)), BF16) for lv in levels for d in (1, -1)]
    scratch += [
        V((l0.chan * (l0.rows + 1), l0.cols), F32),
        V((l0.rows * (l0.cols + 1), LANES), F32),
        V((24, 9 * levels[1].rows, LANES), F32),
        pltpu.SemaphoreType.DMA((32,)),
        pltpu.SemaphoreType.DMA((32,)),
        pltpu.SemaphoreType.DMA((4,)),
    ]
    scratch += [V(f.shape, BF16) for f in feats]
    return pl.pallas_call(
        functools.partial(exchange, levels),
        out_shape=shapes,
        in_specs=[hbm] * 4,
        out_specs=[hbm] * 32 + [vmem],
        scratch_shapes=scratch,
        compiler_params=pltpu.CompilerParams(collective_id=0, has_side_effects=True),
    )(*feats)


def slot(t):
    p, q = divmod(t, 3)
    return (q, p) if p < 2 else (3 + q // 2, q % 2)


def chunking(length, most):
    n = -(-length // most)
    return n, up_to(-(-length // n), 16)


def prepare(levels, given, made, stage, part):
    w0_in, w1_in, mid0, mid1, fin0, fin1 = given
    w0, w1, wd0, wd1a, wd1v, wd2, wd2v = made
    c0, c1, c2, c3 = (lv.chan for lv in levels)

    def blank(ref, row, n, col, m):
        ref[row : row + n, col : col + m] = jnp.zeros((n, m), BF16)

    def shifted(ref, row, n, off, width, to):
        def tile(k):
            part = ref[row : row + n, k * LANES : min((k + 1) * LANES, ref.shape[1])].astype(F32)
            if part.shape[1] < LANES:
                part = jnp.concatenate([part, jnp.zeros((n, LANES - part.shape[1]), F32)], axis=1)
            return part

        k, s = divmod(off, LANES)
        a = tile(k)
        ids = lax.broadcasted_iota(jnp.int32, a.shape, 1)
        if s + width > LANES:
            a = jnp.where(ids >= s, a, tile(k + 1))
        if (to - s) % LANES:
            a = pltpu.roll(a, (to - s) % LANES, 1)
        if width == LANES:
            return a
        return jnp.where((ids >= to) & (ids < to + width), a, 0.0)

    if part == 0:
        w0[...] = jnp.zeros_like(w0)
        for i in range(2):
            for q, rows in ((0, (0,)), (2, (HALF,)), (1, (LANES, LANES + HALF))):
                tile0 = shifted(w0_in.at[i], 0, c0, c0 * q, c0, 0) + shifted(w0_in.at[i], 0, c0, c0 * (3 + q), c0, HALF)
                tile1 = shifted(w0_in.at[i], 0, c0, c0 * (6 + q), c0, 0)
                for row in rows:
                    w0[i, row : row + c0, 0:LANES] = tile0.astype(BF16)
                    w0[i, row : row + c0, LANES : 2 * LANES] = tile1.astype(BF16)
            for row in (0, LANES):
                blank(w1.at[i], row + c1, LANES - c1, 0, 6 * LANES)
            blank(w1.at[i], LANES, c1, 3 * LANES, 3 * LANES)
            for p in range(3):
                for q, row, col in ((0, 0, p), (2, 0, 3 + p), (1, LANES, p)):
                    tile = shifted(w1_in.at[i], 0, c1, c1 * (3 * p + q), c1, 0)
                    w1[i, row : row + c1, col * LANES : (col + 1) * LANES] = tile.astype(BF16)
        return

    def apart(ref, first, to, row):
        for t in range(9):
            tile = shifted(ref, first, c1, c1 * t, c1, 0)
            to[row : row + c1, t * LANES : (t + 1) * LANES] = tile.astype(BF16)

    if part == 1:
        blank(wd1a, c2, 2 * LANES - c2, 0, 9 * LANES)
        blank(wd1a, 2 * LANES + c1, LANES - c1, 0, 9 * LANES)
        for k in range(c2 // c1):
            apart(fin1.at[0], k * c1, wd1a, k * c1)
        apart(mid1.at[0, 0], 0, wd1a, 2 * LANES)
        for k in range(c3 // c1):
            apart(fin1.at[0], c2 + k * c1, wd2v, k * c1)
        return

    tall = up_to(9 * c0, LANES)

    def turned():
        return stage[0:LANES, 0:tall].T.astype(BF16)

    stage[0:LANES, 0:tall] = jnp.zeros((LANES, tall), F32)
    for k in range(2):
        stage[k * c0 : (k + 1) * c0, 0 : 9 * c0] = mid0[0, k].astype(F32)
    flat = turned()
    for t in range(9):
        k, half = slot(t)
        row = k * LANES + half * HALF
        wd0[row : row + c0, LANES : 2 * LANES] = flat[t * c0 : (t + 1) * c0, :]
        wd0[row : row + c0, 0:LANES] = fin0[t * c0 : (t + 1) * c0, 0:LANES]
    for k in range(5):
        blank(wd0, k * LANES + c0, HALF - c0, 0, 2 * LANES)
        n = HALF + c0 if k < 4 else HALF
        blank(wd0, k * LANES + n, LANES - n, 0, 2 * LANES)
    stage[0:LANES, 0:tall] = jnp.zeros((LANES, tall), F32)
    stage[c2 - LANES : c2 - LANES + c0, 0 : 9 * c0] = mid0[0, 2].astype(F32)
    flat = turned()
    for t in range(9):
        blank(wd1v, t * LANES + c0, c0, 0, LANES)
        wd1v[t * LANES + c0 : t * LANES + 2 * c0, LANES : 2 * LANES] = flat[t * c0 : (t + 1) * c0, :]
        blank(wd1v, t * LANES + 2 * c0, LANES - 2 * c0, 0, 2 * LANES)
    depth = wd2.shape[0] // 9
    for t in range(9):
        wd1v[t * LANES : t * LANES + c0, 0:LANES] = shifted(fin0, t * c0, c0, c1, LANES, 0).astype(BF16)
        tile = shifted(fin0, t * c0, c0, c1 + LANES, c2 - LANES, 0)
        wd1v[t * LANES : t * LANES + c0, LANES : 2 * LANES] = tile.astype(BF16)
        row = t * depth + c2
        wd2[row : row + depth - c2, :] = jnp.zeros((depth - c2, c3), BF16)
        for j in range(c3 // LANES):
            tile = shifted(fin0, t * c0, c0, c1 + c2 + j * LANES, LANES, 0)
            wd2[row : row + c0, j * LANES : (j + 1) * LANES] = tile.astype(BF16)


def body(levels, *refs):
    refs = list(refs)

    def take(n):
        out = refs[:n]
        del refs[:n]
        return out

    feats, halos = take(4), take(32)
    w0_in, w1_in, w2_hbm, w3_hbm = take(4)
    biases = take(4)
    late, fin2_hbm = take(7), take(1)[0]
    outs = take(4)
    xs, hs = take(4), take(4)
    spread, odd, cols2, cols3 = take(4)
    w2, w3 = take(2)
    up1, up2, up3, mid0, mid1, fin0, fin1 = arrived = take(7)
    w0, w1, wd0, wd1a, wd1v, wd2, wd2v, stage, bpad = take(9)
    t01, v0, t2, v1, u0, u1, u2, last = take(8)
    (sems,) = take(1)
    l0, l1, l2, l3 = levels
    pairs = [(w2_hbm, w2), (w3_hbm, w3), *zip(late, arrived)]
    copies = [pltpu.make_async_copy(a, b, sems.at[i]) for i, (a, b) in enumerate(pairs)]
    depth = wd2.shape[0] // 9
    bpad[...] = jnp.zeros_like(bpad)
    fin2_copies = [
        pltpu.make_async_copy(
            fin2_hbm.at[pl.ds(t * l2.chan, l2.chan)], wd2.at[pl.ds(t * depth, l2.chan)], sems.at[len(pairs) + t]
        )
        for t in range(9)
    ]
    for c in copies + fin2_copies:
        c.start()

    ready = functools.partial(
        prepare, levels, (w0_in, w1_in, mid0, mid1, fin0, fin1), (w0, w1, wd0, wd1a, wd1v, wd2, wd2v), stage
    )
    ready(0)
    for l in (0, 1):
        bpad[l, 0:2, 0 : levels[l].chan] = biases[l][...]
    bpad[0, :, :] = bpad[0, :, :] + pltpu.roll(bpad[0, :, :], HALF, 1)

    ty, tx = lax.axis_index("ty"), lax.axis_index("tx")
    top, bottom = ty == 0, ty == lax.axis_size("ty") - 1
    left, right = tx == 0, tx == lax.axis_size("tx") - 1

    def lane(shape):
        return lax.broadcasted_iota(jnp.int32, shape, len(shape) - 1)

    def rows_loop(n, run):
        def step(i, _):
            run(i)
            return 0

        if n == 1:
            run(0)
        else:
            lax.fori_loop(0, n, step, 0)

    def unfolded(value):
        value = value.astype(F32)
        C, out = l0.chan, []
        for v in (value, pltpu.roll(value, HALF, 1)):
            v = jnp.where(lane(v.shape) < C, v, 0.0)
            out.append(v + pltpu.roll(v, HALF, 1))
        return out

    def put(l, at, value):
        lv = levels[l]
        for p in range(lv.planes):
            w = min(LANES, lv.chan - p * LANES)
            part = value if l == 0 else value[:, p * LANES : p * LANES + w]
            if part.shape[1] < LANES:
                pad = jnp.zeros((part.shape[0], LANES - part.shape[1]), F32)
                part = jnp.concatenate([part, pad], axis=1)
            xs[l][p, pl.ds(at, value.shape[0]), :] = part

    for l, lv in enumerate(levels):
        for p in range(lv.planes):
            for i in range(lv.lead + lv.rows + 2):
                at = i * lv.pitch + lv.cols
                xs[l][p, at : at + lv.tail, :] = jnp.zeros((lv.tail, LANES), F32)

        @pl.when(top)
        def _(l=l, lv=lv):
            for p in range(lv.planes):
                xs[l][p, 0 : lv.at(0) - lv.tail, :] = jnp.zeros((lv.at(0) - lv.tail, LANES), F32)

        @pl.when(bottom)
        def _(l=l, lv=lv):
            for p in range(lv.planes):
                xs[l][p, lv.at(lv.rows) : lv.total, :] = jnp.zeros((lv.total - lv.at(lv.rows), LANES), F32)

    for l, lv in enumerate(levels):

        def place(source, row, l=l, lv=lv):
            n = source.shape[0]
            group = 8 if n % 8 == 0 else 1

            def run(i):
                for j in range(group):
                    k = i * group + j
                    at = (k + row + lv.lead) * lv.pitch
                    if not isinstance(i, int) and lv.pitch % 8 == 0:
                        at = pl.multiple_of(at, 8)
                    put(l, at, source[k].astype(F32))

            if n % 8:
                for i in range(n):
                    run(i)
            else:
                rows_loop(n // 8, run)

        def place_rows(source, row, l=l, lv=lv):
            if lv.folds == 1:
                return place(source, row)
            half = lv.cols // 2
            for i in range(source.shape[0]):
                for j, value in enumerate(unfolded(source[i])):
                    put(l, lv.at(row + i, j * half), value)

        def place_cols(source, way, l=l, lv=lv):
            dy, dx = way
            for i in range(source.shape[0]):
                col = i - lv.low if dx > 0 else lv.cols + i
                both = [source[i].astype(F32)] if lv.folds == 1 else unfolded(source[i])
                if dy > 0:
                    pieces = [(-lv.low, both[-1][lv.near - lv.low :])]
                elif dy < 0:
                    pieces = [(lv.rows, both[0][:2])]
                else:
                    pieces = [(j * lv.lines, v) for j, v in enumerate(both)]
                for row, v in pieces:
                    for p in range(lv.planes):
                        w = min(LANES, lv.chan - p * LANES)
                        at = pl.ds(lv.at(row, col), v.shape[0], stride=lv.pitch)
                        part = v if lv.folds == 2 else v[:, p * LANES : p * LANES + w]
                        if part.shape[1] < LANES:
                            part = jnp.concatenate([part, jnp.zeros((v.shape[0], LANES - w), F32)], axis=1)
                        xs[l][p, at, :] = part

        place(feats[l], 0)
        for k, way in enumerate(WAYS):

            @pl.when(on_map(way, -1))
            def _(k=k, way=way):
                source = halos[8 * l + k]
                if way[1]:
                    place_cols(source, way)
                else:
                    place_rows(source, -lv.low if way[0] > 0 else lv.rows)

    def blank(ref, lv, low, high):
        planes = ref.shape[0]

        def columns(col, n):
            start = lv.at(-low - 1)
            count = low + 1 + lv.rows + high
            for c in range(col, col + n):
                for p in range(planes):
                    ref[p, pl.ds(start + c, count, stride=lv.pitch), :] = jnp.zeros((count, LANES), F32)

        def rows(row, n):
            for p in range(planes):
                size = n * lv.pitch
                ref[p, pl.ds(lv.at(row) - lv.tail + 2, size), :] = jnp.zeros((size, LANES), F32)

        def before():
            for p in range(planes):
                for i in range(lv.lead - low - 1, lv.lead + lv.rows + high - 1):
                    end = (i + 1) * lv.pitch
                    ref[p, end - low : end, :] = jnp.zeros((low, LANES), F32)

        pl.when(left)(before)
        if high:
            pl.when(right)(lambda: columns(lv.cols, high))
            pl.when(bottom)(lambda: rows(lv.rows, high))

        pl.when(top)(lambda: rows(-low, low))

    def paired(piece):
        tiles = [[], [], [], [], []]
        for t in range(9):
            tiles[slot(t)[0]].append(piece(t))
        keep = lane(tiles[0][0].shape) < HALF
        tiles = [jnp.where(keep, *tile) if len(tile) > 1 else tile[0] for tile in tiles]
        return jnp.concatenate([tile.astype(BF16) for tile in tiles], axis=1)

    def wide_conv(l, src, dst, weight, bias, span, residual):
        lv = levels[l]
        start, length = span
        n, m = chunking(length, MOST)
        group = GROUP if n % GROUP == 0 else 1

        def run(i, j):
            base = pl.multiple_of(start + (i * group + j) * m, 8)

            if l == 0:
                a, b, c = (
                    src[0, pl.ds(pl.multiple_of(base - 8 + d * lv.pitch, 8), m + 16), :] for d in (-1, 0, 1)
                )
                pieces = [jnp.where(lane(a.shape) < HALF, a, b), c]
            else:
                pieces = [
                    src[0, pl.ds(base + d * lv.pitch + e, m + 16), :] for e in (-1, 1) for d in (-1, 0, 1)
                ]
            lhs = jnp.concatenate([piece.astype(BF16) for piece in pieces], axis=1)
            o = lax.dot_general(lhs, weight[...], NT, preferred_element_type=F32)
            one, two = spread.at[2 * j], spread.at[2 * j + 1]
            one[0 : m + 16, :] = o[:, 0:LANES]
            two[0 : m + 16, :] = o[:, LANES:]
            if l == 0:
                y = one[7 : 7 + m, :]
                y = jnp.where(lane(y.shape) < HALF, y, one[9 : 9 + m, :])
                y = y + pltpu.roll(y, HALF, 1) + two[8 : 8 + m, :]
            else:
                y = one[0:m, :] + two[1 : 1 + m, :]
            y = y + bias
            if residual:
                y = y + dst[0, pl.ds(base, m), :]
            dst[0, pl.ds(base, m), :] = jnp.maximum(y, 0.0)

        def several(i):
            for j in range(group):
                run(i, j)

        rows_loop(n // group, several)

    def offset(lv, t):
        return (t // 3 - 1) * lv.pitch + t % 3 - 1

    def deep_conv2(src, dst, weight, bias, span, residual):
        lv = l2
        start, length = span
        m = up_to(length, 16)
        total = lv.total
        p0, p1 = src[0, :, :], src[1, :, :]
        ids = lane((total, LANES))
        r0, r1 = pltpu.roll(p0, 64, 1), pltpu.roll(p1, 64, 1)
        odd[0, :, :] = jnp.where(ids >= 64, r0, 0.0)
        odd[1, :, :] = jnp.where(ids < 64, r0, r1)

        def piece(ref, p, t):
            return ref[p, pl.ds(start + offset(lv, t), m), :]

        for t in range(0, 9, 2):
            k = 3 * (t // 2) * LANES
            cols2[0:m, k : k + 128] = piece(src, 0, t).astype(BF16)
            tile = piece(src, 1, t)
            if t == 8:
                cols2[0:m, k + 128 : k + 192] = tile[:, 0:64].astype(BF16)
            else:
                cols2[0:m, k + 128 : k + 256] = (tile + piece(odd, 0, t + 1)).astype(BF16)
                cols2[0:m, k + 256 : k + 384] = piece(odd, 1, t + 1).astype(BF16)
        y = lax.dot_general(cols2[0:m, :], weight, NT, preferred_element_type=F32) + bias
        for p in range(2):
            w = min(LANES, lv.chan - p * LANES)
            part = y[:, p * LANES : p * LANES + w]
            if residual:
                part = part + dst[p, pl.ds(start, m), 0:w]
            dst[p, pl.ds(start, m), 0:w] = jnp.maximum(part, 0.0)

    def deep_conv3(src, dst, weight, bias, span, residual):
        lv = l3
        start, length = span
        m = up_to(length, 16)
        for t in range(9):
            for p in range(lv.planes):
                k = (t * lv.planes + p) * LANES
                cols3[0:m, k : k + LANES] = src[p, pl.ds(start + offset(lv, t), m), :].astype(BF16)
        y = lax.dot_general(cols3[0:m, :], weight, NT, preferred_element_type=F32) + bias
        for p in range(lv.planes):
            part = y[:, p * LANES : (p + 1) * LANES]
            if residual:
                part = part + dst[p, pl.ds(start, m), :]
            dst[p, pl.ds(start, m), :] = jnp.maximum(part, 0.0)

    wide_conv(0, xs[0], hs[0], w0.at[0], bpad[0, 0:1, :], l0.first(), False)
    blank(hs[0], l0, l0.rim + 1, 1)
    wide_conv(0, hs[0], xs[0], w0.at[1], bpad[0, 1:2, :], l0.second(), True)
    blank(xs[0], l0, l0.rim, 0)
    for c in copies:
        c.wait()
    hs[2][1, :, :] = jnp.zeros((l2.total, LANES), F32)
    wide_conv(1, xs[1], hs[1], w1.at[0], bpad[1, 0:1, :], l1.first(), False)
    deep_conv2(xs[2], hs[2], w2[0], biases[2][0:1, :], l2.first(), False)
    deep_conv3(xs[3], hs[3], w3[0], biases[3][0:1, :], l3.first(), False)
    ready(1)
    for l in (1, 2, 3):
        blank(hs[l], levels[l], levels[l].rim + 1, 1)
    wide_conv(1, hs[1], xs[1], w1.at[1], bpad[1, 1:2, :], l1.second(), True)
    deep_conv2(hs[2], xs[2], w2[1], biases[2][1:2, :], l2.second(), True)
    deep_conv3(hs[3], xs[3], w3[1], biases[3][1:2, :], l3.second(), True)
    ready(2)
    for l in (1, 2):
        blank(xs[l], levels[l], levels[l].rim, 0)

    def gathered(src, plane, big, small, i, t, width=None):
        width = small.pitch if width is None else width
        at = (2 * i + t // 3 - 1 + big.lead) * big.pitch + 2 * (small.cols - width) + t % 3 - 1
        return src[plane, pl.ds(at, width, stride=2), :]

    rim = RIMS[1]
    rows = up_to(rim + l1.rows, 4)

    def down0(k):
        i0 = l1.rows - rows + 4 * k
        taps = paired(
            lambda t: jnp.concatenate([gathered(xs[0], 0, l0, l1, i0 + r, t) for r in range(4)], axis=0)
        )
        o = lax.dot_general(taps, wd0[...], NN, preferred_element_type=F32)
        at = pl.multiple_of((i0 + l1.lead) * l1.pitch - l1.tail, 8)
        t01[0, pl.ds(at, 4 * l1.pitch), :] = o[:, 0:LANES]
        v0[0, pl.ds(at, 4 * l1.pitch), :] = jnp.maximum(o[:, LANES:], 0.0)

    count = rows // 4
    group = GROUP if count % GROUP == 0 else 1

    def downs0(k):
        for j in range(group):
            down0(k * group + j)

    rows_loop(count // group, downs0)
    blank(v0, l1, rim, 0)

    rows = l2.rows + 2
    at = l2.at(-2) - l2.tail
    span = rows * l2.pitch

    def down1(src, weight, form):
        taps = [
            jnp.concatenate([gathered(src, 0, l1, l2, i, t) for i in range(-2, l2.rows)], axis=0).astype(BF16)
            for t in range(9)
        ]
        return lax.dot_general(jnp.concatenate(taps, axis=1), weight[...], form, preferred_element_type=F32)

    o = down1(xs[1], wd1a, NT)
    e = down1(v0, wd1v, NN)
    second = o[:, LANES : 2 * LANES] + e[:, LANES : 2 * LANES]
    ids = lane(second.shape)
    t2[0, 0:span, :] = o[:, 0:LANES] + e[:, 0:LANES]
    t2[1, 0:span, :] = second
    v1[0, pl.ds(at, span), :] = jnp.where(ids >= 64, jnp.maximum(second, 0.0), 0.0)
    v1[1, pl.ds(at, span), :] = jnp.maximum(o[:, 2 * LANES :], 0.0)
    blank(v1, l2, 1, 0)
    def tap3(p, t):
        parts = []
        for i in range(l3.rows):
            piece = gathered(xs[2] if p < 2 else v1, p if p < 2 else 1, l2, l3, i, t, l3.cols)
            if p == 1:
                piece = piece + gathered(v1, 0, l2, l3, i, t, l3.cols)
            parts.append(piece)
        return jnp.concatenate(parts, axis=0).astype(BF16)

    taps = jnp.concatenate([tap3(2, t) for t in range(9)], axis=1)
    t3 = lax.dot_general(taps, wd2v[...], NT, preferred_element_type=F32)
    taps = jnp.concatenate([tap3(p, t) for t in range(9) for p in range(2)], axis=1)
    for c in fin2_copies:
        c.wait()
    t3 = t3 + lax.dot_general(taps, wd2[...], NN, preferred_element_type=F32)

    def center(l, i):
        lv = levels[l]
        parts = [xs[l][p, pl.ds(lv.at(i), lv.cols), :] for p in range(lv.planes)]
        return jnp.concatenate(parts, axis=1)[:, : lv.chan] if lv.planes > 1 else parts[0][:, : lv.chan]

    a3 = jnp.concatenate([center(3, i) for i in range(l3.rows)], axis=0)
    y3 = jnp.maximum(a3 + t3, 0.0).astype(BF16)
    for i in range(l3.rows):
        outs[3][i, :, :] = y3[i * l3.cols : (i + 1) * l3.cols, :]

    c0, c1, c2 = l0.chan, l1.chan, l2.chan
    a3 = a3.astype(BF16)
    up3_0 = lax.dot_general(a3, up3[0, 0:c0, :], NT, preferred_element_type=F32)
    up3_1 = lax.dot_general(a3, up3[0, c0 : c0 + c1, :], NT, preferred_element_type=F32)
    up3_2 = lax.dot_general(a3, up3[0, c0 + c1 :, :], NT, preferred_element_type=F32)

    def enlarge(value, dst, plane, width, rows, cols):
        for i in range(rows):
            line = value[i * cols : (i + 1) * cols, :]
            for di in range(2):
                for dj in range(2):
                    base = (2 * i + di) * 2 * cols + dj
                    dst[plane, pl.ds(base, cols, stride=2), 0:width] = line

    enlarge(up3_0, u2, 0, c0, l3.rows, l3.cols)
    enlarge(up3_1, u2, 1, c1, l3.rows, l3.cols)
    enlarge(up3_2[:, 0:LANES], u2, 2, LANES, l3.rows, l3.cols)
    enlarge(up3_2[:, LANES:], u2, 3, c2 - LANES, l3.rows, l3.cols)
    a2 = jnp.concatenate([center(2, i) for i in range(l2.rows)], axis=0)
    a2b = a2.astype(BF16)
    up2_0 = lax.dot_general(a2b, up2[0, 0:c0, :], NT, preferred_element_type=F32) + u2[0, :, 0:c0]
    up2_1 = lax.dot_general(a2b, up2[0, c0:, :], NT, preferred_element_type=F32) + u2[1, :, 0:c1]
    for i in range(l2.rows):
        for p in range(2):
            w = min(LANES, c2 - p * LANES)
            line = xs[2][p, pl.ds(l2.at(i), l2.cols), 0:w]
            line = line + t2[p, pl.ds((i + 2) * l2.pitch + l2.tail, l2.cols), 0:w]
            line = line + u2[2 + p, pl.ds(i * l2.cols, l2.cols), 0:w]
            outs[2][i, :, p * LANES : p * LANES + w] = jnp.maximum(line, 0.0).astype(BF16)
    enlarge(up2_0, u1, 0, c0, l2.rows, l2.cols)
    enlarge(up2_1, u1, 1, c1, l2.rows, l2.cols)

    def join1(k):
        lines = []
        for r in range(4):
            i = 4 * k + r
            at = pl.multiple_of((i + l1.lead) * l1.pitch, 8)
            line = xs[1][0, pl.ds(at, l1.cols), 0:c1]
            lines.append(line)
            total = line + t01[0, pl.ds(at, l1.cols), 0:c1]
            total = total + u1[1, pl.ds(pl.multiple_of(i * l1.cols, 8), l1.cols), 0:c1]
            outs[1][i, :, :] = jnp.maximum(total, 0.0).astype(BF16)
        a1 = jnp.concatenate(lines, axis=0).astype(BF16)
        n = 4 * l1.cols
        y = lax.dot_general(a1, up1[0], NT, preferred_element_type=F32)
        y = y + u1[0, pl.ds(pl.multiple_of(k * n, 8), n), 0:c0]
        for r in range(4):
            line = y[r * l1.cols : (r + 1) * l1.cols, :]
            for dj in range(2):
                u0[0, pl.ds(dj, l1.cols, stride=2), 0:c0] = line
            up = u0[0, 0 : l0.cols, 0:c0]
            for di in range(2):
                i = 2 * (4 * k + r) + di
                at = pl.multiple_of((i + l0.lead) * l0.pitch, 8)
                total = jnp.maximum(xs[0][0, pl.ds(at, l0.cols), 0:c0] + up, 0.0)
                last[pl.ds(i, c0, stride=l0.rows + 1), :] = total.T

    rows_loop(l1.rows // 4, join1)

    def leave(k):
        for j in range(8):
            at = pl.multiple_of(8 * k * (l0.rows + 1), 8) + j * (l0.rows + 1)
            outs[0][8 * k + j] = last[pl.ds(at, l0.rows), :].astype(BF16)

    rows_loop(c0 // 8, leave)


def per_device(*args):
    feats, weights, biases, rest = args[0:4], args[4:8], args[8:12], args[12:20]
    levels = [Level(l, f.shape[1:] + f.shape[:1]) for l, f in enumerate(feats)]
    feats = [feats[0]] + [f.transpose(1, 2, 0) for f in feats[1:]]
    l0, l1, l2, l3 = levels
    c0, c1, c2, c3 = (lv.chan for lv in levels)
    *halos, first = halos_of(levels, feats)
    feats[0] = first
    up1, up2, up3, mid0, mid1, fin0, fin1, fin2 = rest
    fin0, fin2 = fin0[0].T, fin2[0].T
    vmem, any_ = pl.BlockSpec(memory_space=pltpu.VMEM), pl.BlockSpec(memory_space=pl.ANY)
    V = pltpu.VMEM
    maps = [V((lv.planes, lv.total, LANES), F32) for lv in levels]
    m2, m3 = up_to(l2.first()[1], 16), up_to(l3.first()[1], 16)
    most = max(chunking(s[1], MOST)[1] for lv in levels[:2] for s in (lv.first(), lv.second()))
    scratch = maps * 2 + [
        V((2 * GROUP, most + 16, LANES), F32),
        V((2, l2.total, LANES), F32),
        V((m2, 9 * c2), BF16),
        V((m3, 9 * c3), BF16),
        V(weights[2].shape, BF16),
        V(weights[3].shape, BF16),
        *(V(r.shape, BF16) for r in (up1, up2, up3, mid0, mid1, fin0, fin1)),
        V((2, 2 * LANES, 2 * LANES), BF16),
        V((2, 2 * LANES, 6 * LANES), BF16),
        V((5 * LANES, 2 * LANES), BF16),
        V((3 * LANES, 9 * LANES), BF16),
        V((9 * LANES, 2 * LANES), BF16),
        V((9 * up_to(c2, LANES), c3), BF16),
        V((c3, 9 * LANES), BF16),
        V((LANES, up_to(9 * c0, LANES)), F32),
        V((2, 8, LANES), F32),
        V((1, l1.total, LANES), F32),
        V((1, l1.total, LANES), F32),
        V((2, (l2.rows + 2) * l2.pitch, LANES), F32),
        V((2, l2.total, LANES), F32),
        V((1, l0.cols, LANES), F32),
        V((2, l1.rows * l1.cols, LANES), F32),
        V((4, l2.rows * l2.cols, LANES), F32),
        V((c0 * (l0.rows + 1), l0.cols), F32),
        pltpu.SemaphoreType.DMA((18,)),
    ]
    outs = pl.pallas_call(
        functools.partial(body, levels),
        out_shape=[jax.ShapeDtypeStruct(args[0].shape, BF16)]
        + [jax.ShapeDtypeStruct(f.shape, BF16) for f in feats[1:]],
        in_specs=[vmem] * 38 + [any_] * 2 + [vmem] * 4 + [any_] * 8,
        out_specs=[vmem] * 4,
        scratch_shapes=scratch,
        compiler_params=pltpu.CompilerParams(vmem_limit_bytes=60 * 2**20),
    )(*feats, *halos, *weights, *biases, up1, up2, up3, mid0, mid1, fin0, fin1, fin2)
    return (outs[0], *(o.transpose(2, 0, 1) for o in outs[1:]))


def solution(mesh):
    tiled = P(None, "ty", "tx")
    return jax.shard_map(
        per_device,
        mesh=mesh,
        in_specs=(tiled,) * 4 + (P(),) * 16,
        out_specs=(tiled,) * 4,
        check_vma=False,
    )
```

```python
import functools
import math

import jax
import jax.numpy as jnp
from jax import lax
from jax.experimental import pallas as pl
from jax.experimental.pallas import tpu as pltpu
from jax.sharding import PartitionSpec as P

RIMS = (7, 3, 1, 0)
GROUP = 9
MOST = 656
LANES = 128
HALF = 64
NT = (((1,), (1,)), ((), ()))
NN = (((1,), (0,)), ((), ()))
WAYS = [(1, 1), (0, 1), (1, 0), (1, -1), (-1, 1), (0, -1), (-1, 0), (-1, -1)]
F32, BF16 = jnp.float32, jnp.bfloat16


def up_to(n, m):
    return -(-n // m) * m


class Level:
    def __init__(self, level, shape):
        self.rows, self.cols, self.chan = shape
        self.rim = RIMS[level]
        self.low = self.rim + 2
        self.pitch = up_to(self.cols + 2 + self.low, 8 if level < 3 else 4)
        self.lead = self.low + 1
        self.tail = self.pitch - self.cols
        self.planes = up_to(self.chan, LANES) // LANES
        self.near = up_to(self.low, 8)
        self.total = (self.lead + self.rows + 4) * self.pitch
        self.folds = 2 if 2 * self.chan <= LANES else 1
        self.lines = self.rows // self.folds
        self.wide = LANES if self.folds == 2 else self.chan

    def at(self, row, col=0):
        return (row + self.lead) * self.pitch + col

    def first(self):
        start = self.at(-self.rim - 1) - self.tail
        return start, self.at(self.rows) + self.cols + 8 - start

    def second(self):
        start = self.at(-self.rim) - self.tail
        return start, self.at(self.rows - 1) + self.cols - start


def window(lv, way):
    lines = lv.lines
    if way[0] == 0:
        return 0, lines
    return (lines - lv.near, lv.near) if way[0] > 0 else (0, 8)


def message(lv, way):
    dy, dx = way
    if dx == 0:
        rows = lv.low if dy > 0 else 2
        return (rows, lv.cols // lv.folds, lv.wide)
    return (lv.low if dx > 0 else 2, window(lv, way)[1], lv.wide)


def on_map(way, side):
    ok = True
    for step, axis in zip(way, ("ty", "tx")):
        if step:
            place = lax.axis_index(axis) + side * step
            ok = ok & (place >= 0) & (place < lax.axis_size(axis))
    return ok


def exchange(levels, *refs):
    given, outs, turned = refs[:4], refs[4:36], refs[36]
    rows_sent, cols_sent = refs[37:39], refs[39:47]
    stage, maps, side, send, recv, local = refs[47:53]
    feats = refs[53:]
    loads = [pltpu.make_async_copy(a, b, local.at[i]) for i, (a, b) in enumerate(zip(given, feats))]
    for load_ in loads:
        load_.start()
    here = {a: lax.axis_index(a) for a in ("ty", "tx")}
    barrier = pltpu.get_barrier_semaphore()
    l0 = levels[0]

    def there(way):
        return {"ty": here["ty"] + way[0], "tx": here["tx"] + way[1]}

    count = 0
    for way in WAYS:
        ok = on_map(way, 1)

        @pl.when(ok)
        def _(way=way):
            pl.semaphore_signal(barrier, 1, device_id=there(way))

        count = count + jnp.where(ok, 1, 0)

    C, R, W = l0.chan, l0.rows, l0.cols
    for load_ in loads:
        load_.wait()

    tall, wide = R + 1, W + 1

    def load(i, _):
        for j in range(8):
            at = pl.multiple_of(i * 8 * tall, 8) + j * tall
            stage[pl.ds(at, R), :] = feats[0][8 * i + j].astype(F32)
        return 0

    lax.fori_loop(0, C // 8, load, 0)

    def turn(i, _):
        for j in range(8):
            r = 8 * i + j
            value = stage[pl.ds(r, C, stride=tall), :]
            value = jnp.concatenate([value, jnp.zeros((HALF - C, W), F32), value], axis=0).T
            at = pl.multiple_of(i * 8 * wide, 8) + j * wide
            maps[pl.ds(at, W), 0 : HALF + C] = value
            turned[r] = value.astype(BF16)
        return 0

    lax.fori_loop(0, R // 8, turn, 0)

    def folded(a, b):
        ids = lax.broadcasted_iota(jnp.int32, a.shape, 1)
        a, b = jnp.where(ids < C, a, 0.0), jnp.where(ids < C, b, 0.0)
        return (a + pltpu.roll(b, HALF, 1)).astype(BF16)

    half = W // 2
    for to, first, n in ((rows_sent[0], R - l0.low, l0.low), (rows_sent[1], 0, 2)):
        for i in range(n):
            at = (first + i) * wide
            to[i] = folded(maps[at : at + half, :], maps[at + half : at + W, :])
    half = R // 2
    for to, first, n in ((cols_sent[0], W - l0.low, l0.low), (cols_sent[1], 0, 2)):
        for i in range(n):
            a = maps[pl.ds(first + i, half, stride=wide), :]
            to[i] = folded(a, maps[pl.ds(half * wide + first + i, half, stride=wide), :])
    for l in range(1, 4):
        lv = levels[l]
        for d, (base, n) in enumerate(((lv.cols - 8, lv.low), (0, 2))):
            to = cols_sent[2 * l + d]
            for p in range(lv.planes):
                w = min(LANES, lv.chan - p * LANES)
                slot = 6 * l + 3 * d + p
                for r in range(lv.rows):
                    block = feats[l][r, base : base + 8, p * LANES : p * LANES + w]
                    side[slot, 9 * r : 9 * r + 8, 0:w] = block.astype(F32)
                for i in range(n):
                    at = i + (8 - n if d == 0 else 0)
                    value = side[slot, pl.ds(at, lv.rows, stride=9), 0:w]
                    to[i, :, p * LANES : p * LANES + w] = value.astype(BF16)

    pl.semaphore_wait(barrier, count)

    def copy(l, k):
        lv, way = levels[l], WAYS[k]
        dy, dx = way
        if dx:
            src = cols_sent[2 * l + (0 if dx > 0 else 1)]
            first, n = window(lv, way)
            if dy:
                src = src.at[:, pl.ds(first, n)]
        elif l == 0:
            src = rows_sent[0 if dy > 0 else 1]
        else:
            src = feats[l].at[pl.ds(lv.rows - lv.low, lv.low) if dy > 0 else pl.ds(0, 2)]
        return pltpu.make_async_remote_copy(
            src, outs[8 * l + k], send.at[8 * l + k], recv.at[8 * l + k], device_id=there(way)
        )

    for k, way in enumerate(WAYS):

        @pl.when(on_map(way, 1))
        def _(k=k):
            for l in range(4):
                copy(l, k).start()

    for k, way in enumerate(WAYS):

        @pl.when(on_map(way, 1))
        def _(k=k):
            for l in range(4):
                copy(l, k).wait_send()

        @pl.when(on_map(way, -1))
        def _(k=k):
            for l in range(4):
                copy(l, k).wait_recv()


def halos_of(levels, feats):
    V = pltpu.VMEM
    l0 = levels[0]
    shapes = [jax.ShapeDtypeStruct(message(lv, way), BF16) for lv in levels for way in WAYS]
    shapes.append(jax.ShapeDtypeStruct((l0.rows, l0.cols, HALF + l0.chan), BF16))
    vmem, hbm = pl.BlockSpec(memory_space=pltpu.VMEM), pl.BlockSpec(memory_space=pl.ANY)
    scratch = [V(message(l0, (d, 0)), BF16) for d in (1, -1)]
    scratch += [V(message(lv, (0, d)), BF16) for lv in levels for d in (1, -1)]
    scratch += [
        V((l0.chan * (l0.rows + 1), l0.cols), F32),
        V((l0.rows * (l0.cols + 1), LANES), F32),
        V((24, 9 * levels[1].rows, LANES), F32),
        pltpu.SemaphoreType.DMA((32,)),
        pltpu.SemaphoreType.DMA((32,)),
        pltpu.SemaphoreType.DMA((4,)),
    ]
    scratch += [V(f.shape, BF16) for f in feats]
    return pl.pallas_call(
        functools.partial(exchange, levels),
        out_shape=shapes,
        in_specs=[hbm] * 4,
        out_specs=[hbm] * 32 + [vmem],
        scratch_shapes=scratch,
        compiler_params=pltpu.CompilerParams(collective_id=0, has_side_effects=True),
    )(*feats)


def slot(t):
    p, q = divmod(t, 3)
    return (q, p) if p < 2 else (3 + q // 2, q % 2)


def chunking(length, most):
    n = -(-length // most)
    return n, up_to(-(-length // n), 16)


def prepare(levels, given, made, stage, part):
    w0_in, w1_in, mid0, mid1, fin0, fin1 = given
    w0, w1, wd0, wd1a, wd1v, wd2, wd2v = made
    c0, c1, c2, c3 = (lv.chan for lv in levels)

    def blank(ref, row, n, col, m):
        ref[row : row + n, col : col + m] = jnp.zeros((n, m), BF16)

    def shifted(ref, row, n, off, width, to):
        def tile(k):
            part = ref[row : row + n, k * LANES : min((k + 1) * LANES, ref.shape[1])].astype(F32)
            if part.shape[1] < LANES:
                part = jnp.concatenate([part, jnp.zeros((n, LANES - part.shape[1]), F32)], axis=1)
            return part

        k, s = divmod(off, LANES)
        a = tile(k)
        ids = lax.broadcasted_iota(jnp.int32, a.shape, 1)
        if s + width > LANES:
            a = jnp.where(ids >= s, a, tile(k + 1))
        if (to - s) % LANES:
            a = pltpu.roll(a, (to - s) % LANES, 1)
        if width == LANES:
            return a
        return jnp.where((ids >= to) & (ids < to + width), a, 0.0)

    if part == 0:
        w0[...] = jnp.zeros_like(w0)
        for i in range(2):
            for q, rows in ((0, (0,)), (2, (HALF,)), (1, (LANES, LANES + HALF))):
                tile0 = shifted(w0_in.at[i], 0, c0, c0 * q, c0, 0) + shifted(w0_in.at[i], 0, c0, c0 * (3 + q), c0, HALF)
                tile1 = shifted(w0_in.at[i], 0, c0, c0 * (6 + q), c0, 0)
                for row in rows:
                    w0[i, row : row + c0, 0:LANES] = tile0.astype(BF16)
                    w0[i, row : row + c0, LANES : 2 * LANES] = tile1.astype(BF16)
            for row in (0, LANES):
                blank(w1.at[i], row + c1, LANES - c1, 0, 6 * LANES)
            blank(w1.at[i], LANES, c1, 3 * LANES, 3 * LANES)
            for p in range(3):
                for q, row, col in ((0, 0, p), (2, 0, 3 + p), (1, LANES, p)):
                    tile = shifted(w1_in.at[i], 0, c1, c1 * (3 * p + q), c1, 0)
                    w1[i, row : row + c1, col * LANES : (col + 1) * LANES] = tile.astype(BF16)
        return

    def apart(ref, first, to, row):
        for t in range(9):
            tile = shifted(ref, first, c1, c1 * t, c1, 0)
            to[row : row + c1, t * LANES : (t + 1) * LANES] = tile.astype(BF16)

    if part == 1:
        blank(wd1a, c2, 2 * LANES - c2, 0, 9 * LANES)
        blank(wd1a, 2 * LANES + c1, LANES - c1, 0, 9 * LANES)
        for k in range(c2 // c1):
            apart(fin1.at[0], k * c1, wd1a, k * c1)
        apart(mid1.at[0, 0], 0, wd1a, 2 * LANES)
        for k in range(c3 // c1):
            apart(fin1.at[0], c2 + k * c1, wd2v, k * c1)
        return

    tall = up_to(9 * c0, LANES)

    def turned():
        return stage[0:LANES, 0:tall].T.astype(BF16)

    stage[0:LANES, 0:tall] = jnp.zeros((LANES, tall), F32)
    for k in range(2):
        stage[k * c0 : (k + 1) * c0, 0 : 9 * c0] = mid0[0, k].astype(F32)
    flat = turned()
    for t in range(9):
        k, half = slot(t)
        row = k * LANES + half * HALF
        wd0[row : row + c0, LANES : 2 * LANES] = flat[t * c0 : (t + 1) * c0, :]
        wd0[row : row + c0, 0:LANES] = fin0[t * c0 : (t + 1) * c0, 0:LANES]
    for k in range(5):
        blank(wd0, k * LANES + c0, HALF - c0, 0, 2 * LANES)
        n = HALF + c0 if k < 4 else HALF
        blank(wd0, k * LANES + n, LANES - n, 0, 2 * LANES)
    stage[0:LANES, 0:tall] = jnp.zeros((LANES, tall), F32)
    stage[c2 - LANES : c2 - LANES + c0, 0 : 9 * c0] = mid0[0, 2].astype(F32)
    flat = turned()
    for t in range(9):
        blank(wd1v, t * LANES + c0, c0, 0, LANES)
        wd1v[t * LANES + c0 : t * LANES + 2 * c0, LANES : 2 * LANES] = flat[t * c0 : (t + 1) * c0, :]
        blank(wd1v, t * LANES + 2 * c0, LANES - 2 * c0, 0, 2 * LANES)
    depth = wd2.shape[0] // 9
    for t in range(9):
        wd1v[t * LANES : t * LANES + c0, 0:LANES] = shifted(fin0, t * c0, c0, c1, LANES, 0).astype(BF16)
        tile = shifted(fin0, t * c0, c0, c1 + LANES, c2 - LANES, 0)
        wd1v[t * LANES : t * LANES + c0, LANES : 2 * LANES] = tile.astype(BF16)
        row = t * depth + c2
        wd2[row : row + depth - c2, :] = jnp.zeros((depth - c2, c3), BF16)
        for j in range(c3 // LANES):
            tile = shifted(fin0, t * c0, c0, c1 + c2 + j * LANES, LANES, 0)
            wd2[row : row + c0, j * LANES : (j + 1) * LANES] = tile.astype(BF16)


def body(levels, *refs):
    refs = list(refs)

    def take(n):
        out = refs[:n]
        del refs[:n]
        return out

    feats, halos = take(4), take(32)
    w0_in, w1_in, w2_hbm, w3_hbm = take(4)
    biases = take(4)
    late, fin2_hbm = take(7), take(1)[0]
    outs = take(4)
    xs, hs = take(4), take(4)
    spread, odd, cols2, cols3 = take(4)
    w2, w3 = take(2)
    up1, up2, up3, mid0, mid1, fin0, fin1 = arrived = take(7)
    w0, w1, wd0, wd1a, wd1v, wd2, wd2v, stage, bpad = take(9)
    t01, v0, t2, v1, u0, u1, u2, last = take(8)
    (sems,) = take(1)
    l0, l1, l2, l3 = levels
    pairs = [(w2_hbm, w2), (w3_hbm, w3), *zip(late, arrived)]
    copies = [pltpu.make_async_copy(a, b, sems.at[i]) for i, (a, b) in enumerate(pairs)]
    depth = wd2.shape[0] // 9
    bpad[...] = jnp.zeros_like(bpad)
    fin2_copies = [
        pltpu.make_async_copy(
            fin2_hbm.at[pl.ds(t * l2.chan, l2.chan)], wd2.at[pl.ds(t * depth, l2.chan)], sems.at[len(pairs) + t]
        )
        for t in range(9)
    ]
    for c in copies + fin2_copies:
        c.start()

    ready = functools.partial(
        prepare, levels, (w0_in, w1_in, mid0, mid1, fin0, fin1), (w0, w1, wd0, wd1a, wd1v, wd2, wd2v), stage
    )
    ready(0)
    for l in (0, 1):
        bpad[l, 0:2, 0 : levels[l].chan] = biases[l][...]
    bpad[0, :, :] = bpad[0, :, :] + pltpu.roll(bpad[0, :, :], HALF, 1)

    ty, tx = lax.axis_index("ty"), lax.axis_index("tx")
    top, bottom = ty == 0, ty == lax.axis_size("ty") - 1
    left, right = tx == 0, tx == lax.axis_size("tx") - 1

    def lane(shape):
        return lax.broadcasted_iota(jnp.int32, shape, len(shape) - 1)

    def rows_loop(n, run):
        def step(i, _):
            run(i)
            return 0

        if n == 1:
            run(0)
        else:
            lax.fori_loop(0, n, step, 0)

    def unfolded(value):
        value = value.astype(F32)
        C, out = l0.chan, []
        for v in (value, pltpu.roll(value, HALF, 1)):
            v = jnp.where(lane(v.shape) < C, v, 0.0)
            out.append(v + pltpu.roll(v, HALF, 1))
        return out

    def put(l, at, value):
        lv = levels[l]
        for p in range(lv.planes):
            w = min(LANES, lv.chan - p * LANES)
            part = value if l == 0 else value[:, p * LANES : p * LANES + w]
            if part.shape[1] < LANES:
                pad = jnp.zeros((part.shape[0], LANES - part.shape[1]), F32)
                part = jnp.concatenate([part, pad], axis=1)
            xs[l][p, pl.ds(at, value.shape[0]), :] = part

    for l, lv in enumerate(levels):
        for p in range(lv.planes):
            for i in range(lv.lead + lv.rows + 2):
                at = i * lv.pitch + lv.cols
                xs[l][p, at : at + lv.tail, :] = jnp.zeros((lv.tail, LANES), F32)

        @pl.when(top)
        def _(l=l, lv=lv):
            for p in range(lv.planes):
                xs[l][p, 0 : lv.at(0) - lv.tail, :] = jnp.zeros((lv.at(0) - lv.tail, LANES), F32)

        @pl.when(bottom)
        def _(l=l, lv=lv):
            for p in range(lv.planes):
                xs[l][p, lv.at(lv.rows) : lv.total, :] = jnp.zeros((lv.total - lv.at(lv.rows), LANES), F32)

    for l, lv in enumerate(levels):

        def place(source, row, l=l, lv=lv):
            n = source.shape[0]
            group = 8 if n % 8 == 0 else 1

            def run(i):
                for j in range(group):
                    k = i * group + j
                    at = (k + row + lv.lead) * lv.pitch
                    if not isinstance(i, int) and lv.pitch % 8 == 0:
                        at = pl.multiple_of(at, 8)
                    put(l, at, source[k].astype(F32))

            if n % 8:
                for i in range(n):
                    run(i)
            else:
                rows_loop(n // 8, run)

        def place_rows(source, row, l=l, lv=lv):
            if lv.folds == 1:
                return place(source, row)
            half = lv.cols // 2
            for i in range(source.shape[0]):
                for j, value in enumerate(unfolded(source[i])):
                    put(l, lv.at(row + i, j * half), value)

        def place_cols(source, way, l=l, lv=lv):
            dy, dx = way
            for i in range(source.shape[0]):
                col = i - lv.low if dx > 0 else lv.cols + i
                both = [source[i].astype(F32)] if lv.folds == 1 else unfolded(source[i])
                if dy > 0:
                    pieces = [(-lv.low, both[-1][lv.near - lv.low :])]
                elif dy < 0:
                    pieces = [(lv.rows, both[0][:2])]
                else:
                    pieces = [(j * lv.lines, v) for j, v in enumerate(both)]
                for row, v in pieces:
                    for p in range(lv.planes):
                        w = min(LANES, lv.chan - p * LANES)
                        at = pl.ds(lv.at(row, col), v.shape[0], stride=lv.pitch)
                        part = v if lv.folds == 2 else v[:, p * LANES : p * LANES + w]
                        if part.shape[1] < LANES:
                            part = jnp.concatenate([part, jnp.zeros((v.shape[0], LANES - w), F32)], axis=1)
                        xs[l][p, at, :] = part

        place(feats[l], 0)
        for k, way in enumerate(WAYS):

            @pl.when(on_map(way, -1))
            def _(k=k, way=way):
                source = halos[8 * l + k]
                if way[1]:
                    place_cols(source, way)
                else:
                    place_rows(source, -lv.low if way[0] > 0 else lv.rows)

    def blank(ref, lv, low, high):
        planes = ref.shape[0]

        def columns(col, n):
            start = lv.at(-low - 1)
            count = low + 1 + lv.rows + high
            for c in range(col, col + n):
                for p in range(planes):
                    ref[p, pl.ds(start + c, count, stride=lv.pitch), :] = jnp.zeros((count, LANES), F32)

        def rows(row, n):
            for p in range(planes):
                size = n * lv.pitch
                ref[p, pl.ds(lv.at(row) - lv.tail + 2, size), :] = jnp.zeros((size, LANES), F32)

        def before():
            for p in range(planes):
                for i in range(lv.lead - low - 1, lv.lead + lv.rows + high - 1):
                    end = (i + 1) * lv.pitch
                    ref[p, end - low : end, :] = jnp.zeros((low, LANES), F32)

        pl.when(left)(before)
        if high:
            pl.when(right)(lambda: columns(lv.cols, high))
            pl.when(bottom)(lambda: rows(lv.rows, high))

        pl.when(top)(lambda: rows(-low, low))

    def paired(piece):
        tiles = [[], [], [], [], []]
        for t in range(9):
            tiles[slot(t)[0]].append(piece(t))
        keep = lane(tiles[0][0].shape) < HALF
        tiles = [jnp.where(keep, *tile) if len(tile) > 1 else tile[0] for tile in tiles]
        return jnp.concatenate([tile.astype(BF16) for tile in tiles], axis=1)

    def wide_conv(l, src, dst, weight, bias, span, residual):
        lv = levels[l]
        start, length = span
        n, m = chunking(length, MOST)
        group = math.gcd(n, GROUP)

        def run(i, j):
            base = pl.multiple_of(start + (i * group + j) * m, 8)

            if l == 0:
                a, b, c = (
                    src[0, pl.ds(pl.multiple_of(base - 8 + d * lv.pitch, 8), m + 16), :] for d in (-1, 0, 1)
                )
                pieces = [jnp.where(lane(a.shape) < HALF, a, b), c]
            else:
                pieces = [
                    src[0, pl.ds(base + d * lv.pitch + e, m + 16), :] for e in (-1, 1) for d in (-1, 0, 1)
                ]
            lhs = jnp.concatenate([piece.astype(BF16) for piece in pieces], axis=1)
            o = lax.dot_general(lhs, weight[...], NT, preferred_element_type=F32)
            one, two = spread.at[2 * j], spread.at[2 * j + 1]
            one[0 : m + 16, :] = o[:, 0:LANES]
            two[0 : m + 16, :] = o[:, LANES:]
            if l == 0:
                y = one[7 : 7 + m, :]
                y = jnp.where(lane(y.shape) < HALF, y, one[9 : 9 + m, :])
                y = y + pltpu.roll(y, HALF, 1) + two[8 : 8 + m, :]
            else:
                y = one[0:m, :] + two[1 : 1 + m, :]
            y = y + bias
            if residual:
                y = y + dst[0, pl.ds(base, m), :]
            dst[0, pl.ds(base, m), :] = jnp.maximum(y, 0.0)

        def several(i):
            for j in range(group):
                run(i, j)

        rows_loop(n // group, several)

    def offset(lv, t):
        return (t // 3 - 1) * lv.pitch + t % 3 - 1

    def deep_conv2(src, dst, weight, bias, span, residual):
        lv = l2
        start, length = span
        m = up_to(length, 16)
        total = lv.total
        p0, p1 = src[0, :, :], src[1, :, :]
        ids = lane((total, LANES))
        r0, r1 = pltpu.roll(p0, 64, 1), pltpu.roll(p1, 64, 1)
        odd[0, :, :] = jnp.where(ids >= 64, r0, 0.0)
        odd[1, :, :] = jnp.where(ids < 64, r0, r1)

        def piece(ref, p, t):
            return ref[p, pl.ds(start + offset(lv, t), m), :]

        for t in range(0, 9, 2):
            k = 3 * (t // 2) * LANES
            cols2[0:m, k : k + 128] = piece(src, 0, t).astype(BF16)
            tile = piece(src, 1, t)
            if t == 8:
                cols2[0:m, k + 128 : k + 192] = tile[:, 0:64].astype(BF16)
            else:
                cols2[0:m, k + 128 : k + 256] = (tile + piece(odd, 0, t + 1)).astype(BF16)
                cols2[0:m, k + 256 : k + 384] = piece(odd, 1, t + 1).astype(BF16)
        y = lax.dot_general(cols2[0:m, :], weight, NT, preferred_element_type=F32) + bias
        for p in range(2):
            w = min(LANES, lv.chan - p * LANES)
            part = y[:, p * LANES : p * LANES + w]
            if residual:
                part = part + dst[p, pl.ds(start, m), 0:w]
            dst[p, pl.ds(start, m), 0:w] = jnp.maximum(part, 0.0)

    def deep_conv3(src, dst, weight, bias, span, residual):
        lv = l3
        start, length = span
        m = up_to(length, 16)
        for t in range(9):
            for p in range(lv.planes):
                k = (t * lv.planes + p) * LANES
                cols3[0:m, k : k + LANES] = src[p, pl.ds(start + offset(lv, t), m), :].astype(BF16)
        y = lax.dot_general(cols3[0:m, :], weight, NT, preferred_element_type=F32) + bias
        for p in range(lv.planes):
            part = y[:, p * LANES : (p + 1) * LANES]
            if residual:
                part = part + dst[p, pl.ds(start, m), :]
            dst[p, pl.ds(start, m), :] = jnp.maximum(part, 0.0)

    hs[2][1, :, :] = jnp.zeros((l2.total, LANES), F32)
    wide_conv(0, xs[0], hs[0], w0.at[0], bpad[0, 0:1, :], l0.first(), False)
    wide_conv(1, xs[1], hs[1], w1.at[0], bpad[1, 0:1, :], l1.first(), False)
    for l in (0, 1):
        blank(hs[l], levels[l], levels[l].rim + 1, 1)
    for c in copies:
        c.wait()
    deep_conv2(xs[2], hs[2], w2[0], biases[2][0:1, :], l2.first(), False)
    wide_conv(0, hs[0], xs[0], w0.at[1], bpad[0, 1:2, :], l0.second(), True)
    deep_conv3(xs[3], hs[3], w3[0], biases[3][0:1, :], l3.first(), False)
    ready(1)
    for l in (2, 3):
        blank(hs[l], levels[l], levels[l].rim + 1, 1)
    blank(xs[0], l0, l0.rim, 0)
    wide_conv(1, hs[1], xs[1], w1.at[1], bpad[1, 1:2, :], l1.second(), True)
    deep_conv2(hs[2], xs[2], w2[1], biases[2][1:2, :], l2.second(), True)
    deep_conv3(hs[3], xs[3], w3[1], biases[3][1:2, :], l3.second(), True)
    ready(2)
    for l in (1, 2):
        blank(xs[l], levels[l], levels[l].rim, 0)

    def gathered(src, plane, big, small, i, t, width=None):
        width = small.pitch if width is None else width
        at = (2 * i + t // 3 - 1 + big.lead) * big.pitch + 2 * (small.cols - width) + t % 3 - 1
        return src[plane, pl.ds(at, width, stride=2), :]

    rim = RIMS[1]
    rows = up_to(rim + l1.rows, 4)

    def down0(k):
        i0 = l1.rows - rows + 4 * k
        taps = paired(
            lambda t: jnp.concatenate([gathered(xs[0], 0, l0, l1, i0 + r, t) for r in range(4)], axis=0)
        )
        o = lax.dot_general(taps, wd0[...], NN, preferred_element_type=F32)
        at = pl.multiple_of((i0 + l1.lead) * l1.pitch - l1.tail, 8)
        t01[0, pl.ds(at, 4 * l1.pitch), :] = o[:, 0:LANES]
        v0[0, pl.ds(at, 4 * l1.pitch), :] = jnp.maximum(o[:, LANES:], 0.0)

    count = rows // 4
    group = math.gcd(count, GROUP)

    def downs0(k):
        for j in range(group):
            down0(k * group + j)

    rows_loop(count // group, downs0)
    blank(v0, l1, rim, 0)

    rows = l2.rows + 2
    at = l2.at(-2) - l2.tail
    span = rows * l2.pitch

    def down1(src, weight, form):
        taps = [
            jnp.concatenate([gathered(src, 0, l1, l2, i, t) for i in range(-2, l2.rows)], axis=0).astype(BF16)
            for t in range(9)
        ]
        return lax.dot_general(jnp.concatenate(taps, axis=1), weight[...], form, preferred_element_type=F32)

    o = down1(xs[1], wd1a, NT)
    e = down1(v0, wd1v, NN)
    second = o[:, LANES : 2 * LANES] + e[:, LANES : 2 * LANES]
    ids = lane(second.shape)
    t2[0, 0:span, :] = o[:, 0:LANES] + e[:, 0:LANES]
    t2[1, 0:span, :] = second
    v1[0, pl.ds(at, span), :] = jnp.where(ids >= 64, jnp.maximum(second, 0.0), 0.0)
    v1[1, pl.ds(at, span), :] = jnp.maximum(o[:, 2 * LANES :], 0.0)
    blank(v1, l2, 1, 0)
    def tap3(p, t):
        parts = []
        for i in range(l3.rows):
            piece = gathered(xs[2] if p < 2 else v1, p if p < 2 else 1, l2, l3, i, t, l3.cols)
            if p == 1:
                piece = piece + gathered(v1, 0, l2, l3, i, t, l3.cols)
            parts.append(piece)
        return jnp.concatenate(parts, axis=0).astype(BF16)

    taps = jnp.concatenate([tap3(2, t) for t in range(9)], axis=1)
    t3 = lax.dot_general(taps, wd2v[...], NT, preferred_element_type=F32)
    taps = jnp.concatenate([tap3(p, t) for t in range(9) for p in range(2)], axis=1)
    for c in fin2_copies:
        c.wait()
    t3 = t3 + lax.dot_general(taps, wd2[...], NN, preferred_element_type=F32)

    def center(l, i):
        lv = levels[l]
        parts = [xs[l][p, pl.ds(lv.at(i), lv.cols), :] for p in range(lv.planes)]
        return jnp.concatenate(parts, axis=1)[:, : lv.chan] if lv.planes > 1 else parts[0][:, : lv.chan]

    a3 = jnp.concatenate([center(3, i) for i in range(l3.rows)], axis=0)
    y3 = jnp.maximum(a3 + t3, 0.0).astype(BF16)
    for i in range(l3.rows):
        outs[3][i, :, :] = y3[i * l3.cols : (i + 1) * l3.cols, :]

    c0, c1, c2 = l0.chan, l1.chan, l2.chan
    a3 = a3.astype(BF16)
    up3_0 = lax.dot_general(a3, up3[0, 0:c0, :], NT, preferred_element_type=F32)
    up3_1 = lax.dot_general(a3, up3[0, c0 : c0 + c1, :], NT, preferred_element_type=F32)
    up3_2 = lax.dot_general(a3, up3[0, c0 + c1 :, :], NT, preferred_element_type=F32)

    def enlarge(value, dst, plane, width, rows, cols):
        for i in range(rows):
            line = value[i * cols : (i + 1) * cols, :]
            for di in range(2):
                for dj in range(2):
                    base = (2 * i + di) * 2 * cols + dj
                    dst[plane, pl.ds(base, cols, stride=2), 0:width] = line

    enlarge(up3_0, u2, 0, c0, l3.rows, l3.cols)
    enlarge(up3_1, u2, 1, c1, l3.rows, l3.cols)
    enlarge(up3_2[:, 0:LANES], u2, 2, LANES, l3.rows, l3.cols)
    enlarge(up3_2[:, LANES:], u2, 3, c2 - LANES, l3.rows, l3.cols)
    a2 = jnp.concatenate([center(2, i) for i in range(l2.rows)], axis=0)
    a2b = a2.astype(BF16)
    up2_0 = lax.dot_general(a2b, up2[0, 0:c0, :], NT, preferred_element_type=F32) + u2[0, :, 0:c0]
    up2_1 = lax.dot_general(a2b, up2[0, c0:, :], NT, preferred_element_type=F32) + u2[1, :, 0:c1]
    for i in range(l2.rows):
        for p in range(2):
            w = min(LANES, c2 - p * LANES)
            line = xs[2][p, pl.ds(l2.at(i), l2.cols), 0:w]
            line = line + t2[p, pl.ds((i + 2) * l2.pitch + l2.tail, l2.cols), 0:w]
            line = line + u2[2 + p, pl.ds(i * l2.cols, l2.cols), 0:w]
            outs[2][i, :, p * LANES : p * LANES + w] = jnp.maximum(line, 0.0).astype(BF16)
    enlarge(up2_0, u1, 0, c0, l2.rows, l2.cols)
    enlarge(up2_1, u1, 1, c1, l2.rows, l2.cols)

    def join1(k):
        lines = []
        for r in range(4):
            i = 4 * k + r
            at = pl.multiple_of((i + l1.lead) * l1.pitch, 8)
            line = xs[1][0, pl.ds(at, l1.cols), 0:c1]
            lines.append(line)
            total = line + t01[0, pl.ds(at, l1.cols), 0:c1]
            total = total + u1[1, pl.ds(pl.multiple_of(i * l1.cols, 8), l1.cols), 0:c1]
            outs[1][i, :, :] = jnp.maximum(total, 0.0).astype(BF16)
        a1 = jnp.concatenate(lines, axis=0).astype(BF16)
        n = 4 * l1.cols
        y = lax.dot_general(a1, up1[0], NT, preferred_element_type=F32)
        y = y + u1[0, pl.ds(pl.multiple_of(k * n, 8), n), 0:c0]
        for r in range(4):
            line = y[r * l1.cols : (r + 1) * l1.cols, :]
            for dj in range(2):
                u0[0, pl.ds(dj, l1.cols, stride=2), 0:c0] = line
            up = u0[0, 0 : l0.cols, 0:c0]
            for di in range(2):
                i = 2 * (4 * k + r) + di
                at = pl.multiple_of((i + l0.lead) * l0.pitch, 8)
                total = jnp.maximum(xs[0][0, pl.ds(at, l0.cols), 0:c0] + up, 0.0)
                last[pl.ds(i, c0, stride=l0.rows + 1), :] = total.T

    rows_loop(l1.rows // 4, join1)

    def leave(k):
        for j in range(8):
            at = pl.multiple_of(8 * k * (l0.rows + 1), 8) + j * (l0.rows + 1)
            outs[0][8 * k + j] = last[pl.ds(at, l0.rows), :].astype(BF16)

    rows_loop(c0 // 8, leave)


def per_device(*args):
    feats, weights, biases, rest = args[0:4], args[4:8], args[8:12], args[12:20]
    levels = [Level(l, f.shape[1:] + f.shape[:1]) for l, f in enumerate(feats)]
    feats = [feats[0]] + [f.transpose(1, 2, 0) for f in feats[1:]]
    l0, l1, l2, l3 = levels
    c0, c1, c2, c3 = (lv.chan for lv in levels)
    *halos, first = halos_of(levels, feats)
    feats[0] = first
    up1, up2, up3, mid0, mid1, fin0, fin1, fin2 = rest
    fin0, fin2 = fin0[0].T, fin2[0].T
    vmem, any_ = pl.BlockSpec(memory_space=pltpu.VMEM), pl.BlockSpec(memory_space=pl.ANY)
    V = pltpu.VMEM
    maps = [V((lv.planes, lv.total, LANES), F32) for lv in levels]
    m2, m3 = up_to(l2.first()[1], 16), up_to(l3.first()[1], 16)
    most = max(chunking(s[1], MOST)[1] for lv in levels[:2] for s in (lv.first(), lv.second()))
    scratch = maps * 2 + [
        V((2 * GROUP, most + 16, LANES), F32),
        V((2, l2.total, LANES), F32),
        V((m2, 9 * c2), BF16),
        V((m3, 9 * c3), BF16),
        V(weights[2].shape, BF16),
        V(weights[3].shape, BF16),
        *(V(r.shape, BF16) for r in (up1, up2, up3, mid0, mid1, fin0, fin1)),
        V((2, 2 * LANES, 2 * LANES), BF16),
        V((2, 2 * LANES, 6 * LANES), BF16),
        V((5 * LANES, 2 * LANES), BF16),
        V((3 * LANES, 9 * LANES), BF16),
        V((9 * LANES, 2 * LANES), BF16),
        V((9 * up_to(c2, LANES), c3), BF16),
        V((c3, 9 * LANES), BF16),
        V((LANES, up_to(9 * c0, LANES)), F32),
        V((2, 8, LANES), F32),
        V((1, l1.total, LANES), F32),
        V((1, l1.total, LANES), F32),
        V((2, (l2.rows + 2) * l2.pitch, LANES), F32),
        V((2, l2.total, LANES), F32),
        V((1, l0.cols, LANES), F32),
        V((2, l1.rows * l1.cols, LANES), F32),
        V((4, l2.rows * l2.cols, LANES), F32),
        V((c0 * (l0.rows + 1), l0.cols), F32),
        pltpu.SemaphoreType.DMA((18,)),
    ]
    outs = pl.pallas_call(
        functools.partial(body, levels),
        out_shape=[jax.ShapeDtypeStruct(args[0].shape, BF16)]
        + [jax.ShapeDtypeStruct(f.shape, BF16) for f in feats[1:]],
        in_specs=[vmem] * 38 + [any_] * 2 + [vmem] * 4 + [any_] * 8,
        out_specs=[vmem] * 4,
        scratch_shapes=scratch,
        compiler_params=pltpu.CompilerParams(vmem_limit_bytes=60 * 2**20),
    )(*feats, *halos, *weights, *biases, up1, up2, up3, mid0, mid1, fin0, fin1, fin2)
    return (outs[0], *(o.transpose(2, 0, 1) for o in outs[1:]))


def solution(mesh):
    tiled = P(None, "ty", "tx")
    return jax.shard_map(
        per_device,
        mesh=mesh,
        in_specs=(tiled,) * 4 + (P(),) * 16,
        out_specs=(tiled,) * 4,
        check_vma=False,
    )
```

```python
import functools
import math

import jax
import jax.numpy as jnp
from jax import lax
from jax.experimental import pallas as pl
from jax.experimental.pallas import tpu as pltpu
from jax.sharding import PartitionSpec as P

RIMS = (7, 3, 1, 0)
GROUP = 9
MOST = 656
LANES = 128
HALF = 64
NT = (((1,), (1,)), ((), ()))
NN = (((1,), (0,)), ((), ()))
WAYS = [(1, 1), (0, 1), (1, 0), (1, -1), (-1, 1), (0, -1), (-1, 0), (-1, -1)]
F32, BF16 = jnp.float32, jnp.bfloat16


def up_to(n, m):
    return -(-n // m) * m


class Level:
    def __init__(self, level, shape):
        self.rows, self.cols, self.chan = shape
        self.rim = RIMS[level]
        self.low = self.rim + 2
        self.pitch = up_to(self.cols + 2 + self.low, 8 if level < 3 else 4)
        self.lead = self.low + 1
        self.tail = self.pitch - self.cols
        self.planes = up_to(self.chan, LANES) // LANES
        self.near = up_to(self.low, 8)
        self.total = (self.lead + self.rows + 4) * self.pitch
        self.folds = 2 if 2 * self.chan <= LANES else 1
        self.lines = self.rows // self.folds
        self.wide = LANES if self.folds == 2 else self.chan

    def at(self, row, col=0):
        return (row + self.lead) * self.pitch + col

    def first(self):
        start = self.at(-self.rim - 1) - self.tail
        return start, self.at(self.rows) + self.cols + 8 - start

    def second(self):
        start = self.at(-self.rim) - self.tail
        return start, self.at(self.rows - 1) + self.cols - start


def window(lv, way):
    lines = lv.lines
    if way[0] == 0:
        return 0, lines
    return (lines - lv.near, lv.near) if way[0] > 0 else (0, 8)


def message(lv, way):
    dy, dx = way
    if dx == 0:
        rows = lv.low if dy > 0 else 2
        return (rows, lv.cols // lv.folds, lv.wide)
    return (lv.low if dx > 0 else 2, window(lv, way)[1], lv.wide)


def on_map(way, side):
    ok = True
    for step, axis in zip(way, ("ty", "tx")):
        if step:
            place = lax.axis_index(axis) + side * step
            ok = ok & (place >= 0) & (place < lax.axis_size(axis))
    return ok


def exchange(levels, *refs):
    given, outs, turned = refs[:4], refs[4:36], refs[36]
    rows_sent, cols_sent = refs[37:39], refs[39:47]
    stage, maps, side, send, recv, local = refs[47:53]
    feats = refs[53:]
    loads = [pltpu.make_async_copy(a, b, local.at[i]) for i, (a, b) in enumerate(zip(given, feats))]
    for load_ in loads:
        load_.start()
    here = {a: lax.axis_index(a) for a in ("ty", "tx")}
    barrier = pltpu.get_barrier_semaphore()
    l0 = levels[0]

    def there(way):
        return {"ty": here["ty"] + way[0], "tx": here["tx"] + way[1]}

    count = 0
    for way in WAYS:
        ok = on_map(way, 1)

        @pl.when(ok)
        def _(way=way):
            pl.semaphore_signal(barrier, 1, device_id=there(way))

        count = count + jnp.where(ok, 1, 0)

    C, R, W = l0.chan, l0.rows, l0.cols
    for load_ in loads:
        load_.wait()

    tall, wide = R + 1, W + 1

    def load(i, _):
        for j in range(8):
            at = pl.multiple_of(i * 8 * tall, 8) + j * tall
            stage[pl.ds(at, R), :] = feats[0][8 * i + j].astype(F32)
        return 0

    lax.fori_loop(0, C // 8, load, 0)

    def turn(i, _):
        for j in range(16):
            r = 16 * i + j
            value = stage[pl.ds(r, C, stride=tall), :]
            value = jnp.concatenate([value, jnp.zeros((HALF - C, W), F32), value], axis=0).T
            at = pl.multiple_of(i * 16 * wide, 8) + j * wide
            maps[pl.ds(at, W), 0 : HALF + C] = value
            turned[r] = value.astype(BF16)
        return 0

    lax.fori_loop(0, R // 16, turn, 0)

    def folded(a, b):
        ids = lax.broadcasted_iota(jnp.int32, a.shape, 1)
        a, b = jnp.where(ids < C, a, 0.0), jnp.where(ids < C, b, 0.0)
        return (a + pltpu.roll(b, HALF, 1)).astype(BF16)

    half = W // 2
    for to, first, n in ((rows_sent[0], R - l0.low, l0.low), (rows_sent[1], 0, 2)):
        for i in range(n):
            at = (first + i) * wide
            to[i] = folded(maps[at : at + half, :], maps[at + half : at + W, :])
    half = R // 2
    for to, first, n in ((cols_sent[0], W - l0.low, l0.low), (cols_sent[1], 0, 2)):
        for i in range(n):
            a = maps[pl.ds(first + i, half, stride=wide), :]
            to[i] = folded(a, maps[pl.ds(half * wide + first + i, half, stride=wide), :])
    for l in range(1, 4):
        lv = levels[l]
        for d, (base, n) in enumerate(((lv.cols - 8, lv.low), (0, 2))):
            to = cols_sent[2 * l + d]
            for p in range(lv.planes):
                w = min(LANES, lv.chan - p * LANES)
                slot = 6 * l + 3 * d + p
                for r in range(lv.rows):
                    block = feats[l][r, base : base + 8, p * LANES : p * LANES + w]
                    side[slot, 9 * r : 9 * r + 8, 0:w] = block.astype(F32)
                for i in range(n):
                    at = i + (8 - n if d == 0 else 0)
                    value = side[slot, pl.ds(at, lv.rows, stride=9), 0:w]
                    to[i, :, p * LANES : p * LANES + w] = value.astype(BF16)

    pl.semaphore_wait(barrier, count)

    def copy(l, k):
        lv, way = levels[l], WAYS[k]
        dy, dx = way
        if dx:
            src = cols_sent[2 * l + (0 if dx > 0 else 1)]
            first, n = window(lv, way)
            if dy:
                src = src.at[:, pl.ds(first, n)]
        elif l == 0:
            src = rows_sent[0 if dy > 0 else 1]
        else:
            src = feats[l].at[pl.ds(lv.rows - lv.low, lv.low) if dy > 0 else pl.ds(0, 2)]
        return pltpu.make_async_remote_copy(
            src, outs[8 * l + k], send.at[8 * l + k], recv.at[8 * l + k], device_id=there(way)
        )

    for k, way in enumerate(WAYS):

        @pl.when(on_map(way, 1))
        def _(k=k):
            for l in range(4):
                copy(l, k).start()

    for k, way in enumerate(WAYS):

        @pl.when(on_map(way, 1))
        def _(k=k):
            for l in range(4):
                copy(l, k).wait_send()

        @pl.when(on_map(way, -1))
        def _(k=k):
            for l in range(4):
                copy(l, k).wait_recv()


def halos_of(levels, feats):
    V = pltpu.VMEM
    l0 = levels[0]
    shapes = [jax.ShapeDtypeStruct(message(lv, way), BF16) for lv in levels for way in WAYS]
    shapes.append(jax.ShapeDtypeStruct((l0.rows, l0.cols, HALF + l0.chan), BF16))
    vmem, hbm = pl.BlockSpec(memory_space=pltpu.VMEM), pl.BlockSpec(memory_space=pl.ANY)
    scratch = [V(message(l0, (d, 0)), BF16) for d in (1, -1)]
    scratch += [V(message(lv, (0, d)), BF16) for lv in levels for d in (1, -1)]
    scratch += [
        V((l0.chan * (l0.rows + 1), l0.cols), F32),
        V((l0.rows * (l0.cols + 1), LANES), F32),
        V((24, 9 * levels[1].rows, LANES), F32),
        pltpu.SemaphoreType.DMA((32,)),
        pltpu.SemaphoreType.DMA((32,)),
        pltpu.SemaphoreType.DMA((4,)),
    ]
    scratch += [V(f.shape, BF16) for f in feats]
    return pl.pallas_call(
        functools.partial(exchange, levels),
        out_shape=shapes,
        in_specs=[hbm] * 4,
        out_specs=[hbm] * 32 + [vmem],
        scratch_shapes=scratch,
        compiler_params=pltpu.CompilerParams(collective_id=0, has_side_effects=True),
    )(*feats)


def slot(t):
    p, q = divmod(t, 3)
    return (q, p) if p < 2 else (3 + q // 2, q % 2)


def chunking(length, most):
    n = -(-length // most)
    return n, up_to(-(-length // n), 16)


def prepare(levels, given, made, stage, part):
    w0_in, w1_in, mid0, mid1, fin0, fin1 = given
    w0, w1, wd0, wd1a, wd1v, wd2, wd2v = made
    c0, c1, c2, c3 = (lv.chan for lv in levels)

    def blank(ref, row, n, col, m):
        ref[row : row + n, col : col + m] = jnp.zeros((n, m), BF16)

    def shifted(ref, row, n, off, width, to):
        def tile(k):
            part = ref[row : row + n, k * LANES : min((k + 1) * LANES, ref.shape[1])].astype(F32)
            if part.shape[1] < LANES:
                part = jnp.concatenate([part, jnp.zeros((n, LANES - part.shape[1]), F32)], axis=1)
            return part

        k, s = divmod(off, LANES)
        a = tile(k)
        ids = lax.broadcasted_iota(jnp.int32, a.shape, 1)
        if s + width > LANES:
            a = jnp.where(ids >= s, a, tile(k + 1))
        if (to - s) % LANES:
            a = pltpu.roll(a, (to - s) % LANES, 1)
        if width == LANES:
            return a
        return jnp.where((ids >= to) & (ids < to + width), a, 0.0)

    if part == 0:
        w0[...] = jnp.zeros_like(w0)
        for i in range(2):
            for q, rows in ((0, (0,)), (2, (HALF,)), (1, (LANES, LANES + HALF))):
                tile0 = shifted(w0_in.at[i], 0, c0, c0 * q, c0, 0) + shifted(w0_in.at[i], 0, c0, c0 * (3 + q), c0, HALF)
                tile1 = shifted(w0_in.at[i], 0, c0, c0 * (6 + q), c0, 0)
                for row in rows:
                    w0[i, row : row + c0, 0:LANES] = tile0.astype(BF16)
                    w0[i, row : row + c0, LANES : 2 * LANES] = tile1.astype(BF16)
            for row in (0, LANES):
                blank(w1.at[i], row + c1, LANES - c1, 0, 6 * LANES)
            blank(w1.at[i], LANES, c1, 3 * LANES, 3 * LANES)
            for p in range(3):
                for q, row, col in ((0, 0, p), (2, 0, 3 + p), (1, LANES, p)):
                    tile = shifted(w1_in.at[i], 0, c1, c1 * (3 * p + q), c1, 0)
                    w1[i, row : row + c1, col * LANES : (col + 1) * LANES] = tile.astype(BF16)
        return

    def apart(ref, first, to, row):
        for t in range(9):
            tile = shifted(ref, first, c1, c1 * t, c1, 0)
            to[row : row + c1, t * LANES : (t + 1) * LANES] = tile.astype(BF16)

    if part == 1:
        blank(wd1a, c2, 2 * LANES - c2, 0, 9 * LANES)
        blank(wd1a, 2 * LANES + c1, LANES - c1, 0, 9 * LANES)
        for k in range(c2 // c1):
            apart(fin1.at[0], k * c1, wd1a, k * c1)
        apart(mid1.at[0, 0], 0, wd1a, 2 * LANES)
        for k in range(c3 // c1):
            apart(fin1.at[0], c2 + k * c1, wd2v, k * c1)
        return

    tall = up_to(9 * c0, LANES)

    def turned():
        return stage[0:LANES, 0:tall].T.astype(BF16)

    stage[0:LANES, 0:tall] = jnp.zeros((LANES, tall), F32)
    for k in range(2):
        stage[k * c0 : (k + 1) * c0, 0 : 9 * c0] = mid0[0, k].astype(F32)
    flat = turned()
    for t in range(9):
        k, half = slot(t)
        row = k * LANES + half * HALF
        wd0[row : row + c0, LANES : 2 * LANES] = flat[t * c0 : (t + 1) * c0, :]
        wd0[row : row + c0, 0:LANES] = fin0[t * c0 : (t + 1) * c0, 0:LANES]
    for k in range(5):
        blank(wd0, k * LANES + c0, HALF - c0, 0, 2 * LANES)
        n = HALF + c0 if k < 4 else HALF
        blank(wd0, k * LANES + n, LANES - n, 0, 2 * LANES)
    stage[0:LANES, 0:tall] = jnp.zeros((LANES, tall), F32)
    stage[c2 - LANES : c2 - LANES + c0, 0 : 9 * c0] = mid0[0, 2].astype(F32)
    flat = turned()
    for t in range(9):
        blank(wd1v, t * LANES + c0, c0, 0, LANES)
        wd1v[t * LANES + c0 : t * LANES + 2 * c0, LANES : 2 * LANES] = flat[t * c0 : (t + 1) * c0, :]
        blank(wd1v, t * LANES + 2 * c0, LANES - 2 * c0, 0, 2 * LANES)
    depth = wd2.shape[0] // 9
    for t in range(9):
        wd1v[t * LANES : t * LANES + c0, 0:LANES] = shifted(fin0, t * c0, c0, c1, LANES, 0).astype(BF16)
        tile = shifted(fin0, t * c0, c0, c1 + LANES, c2 - LANES, 0)
        wd1v[t * LANES : t * LANES + c0, LANES : 2 * LANES] = tile.astype(BF16)
        row = t * depth + c2
        wd2[row : row + depth - c2, :] = jnp.zeros((depth - c2, c3), BF16)
        for j in range(c3 // LANES):
            tile = shifted(fin0, t * c0, c0, c1 + c2 + j * LANES, LANES, 0)
            wd2[row : row + c0, j * LANES : (j + 1) * LANES] = tile.astype(BF16)


def body(levels, *refs):
    refs = list(refs)

    def take(n):
        out = refs[:n]
        del refs[:n]
        return out

    feats, halos = take(4), take(32)
    w0_in, w1_in, w2_hbm, w3_hbm = take(4)
    biases = take(4)
    late, fin2_hbm = take(7), take(1)[0]
    outs = take(4)
    xs, hs = take(4), take(4)
    spread, odd, cols2, cols3 = take(4)
    w2, w3 = take(2)
    up1, up2, up3, mid0, mid1, fin0, fin1 = arrived = take(7)
    w0, w1, wd0, wd1a, wd1v, wd2, wd2v, stage, bpad = take(9)
    t01, v0, t2, v1, u0, u1, u2, last = take(8)
    (sems,) = take(1)
    l0, l1, l2, l3 = levels
    pairs = [(w2_hbm, w2), (w3_hbm, w3), *zip(late, arrived)]
    copies = [pltpu.make_async_copy(a, b, sems.at[i]) for i, (a, b) in enumerate(pairs)]
    depth = wd2.shape[0] // 9
    bpad[...] = jnp.zeros_like(bpad)
    fin2_copies = [
        pltpu.make_async_copy(
            fin2_hbm.at[pl.ds(t * l2.chan, l2.chan)], wd2.at[pl.ds(t * depth, l2.chan)], sems.at[len(pairs) + t]
        )
        for t in range(9)
    ]
    for c in copies + fin2_copies:
        c.start()

    ready = functools.partial(
        prepare, levels, (w0_in, w1_in, mid0, mid1, fin0, fin1), (w0, w1, wd0, wd1a, wd1v, wd2, wd2v), stage
    )
    ready(0)
    for l in (0, 1):
        bpad[l, 0:2, 0 : levels[l].chan] = biases[l][...]
    bpad[0, :, :] = bpad[0, :, :] + pltpu.roll(bpad[0, :, :], HALF, 1)

    ty, tx = lax.axis_index("ty"), lax.axis_index("tx")
    top, bottom = ty == 0, ty == lax.axis_size("ty") - 1
    left, right = tx == 0, tx == lax.axis_size("tx") - 1

    def lane(shape):
        return lax.broadcasted_iota(jnp.int32, shape, len(shape) - 1)

    def rows_loop(n, run):
        def step(i, _):
            run(i)
            return 0

        if n == 1:
            run(0)
        else:
            lax.fori_loop(0, n, step, 0)

    def unfolded(value):
        value = value.astype(F32)
        C, out = l0.chan, []
        for v in (value, pltpu.roll(value, HALF, 1)):
            v = jnp.where(lane(v.shape) < C, v, 0.0)
            out.append(v + pltpu.roll(v, HALF, 1))
        return out

    def put(l, at, value):
        lv = levels[l]
        for p in range(lv.planes):
            w = min(LANES, lv.chan - p * LANES)
            part = value if l == 0 else value[:, p * LANES : p * LANES + w]
            if part.shape[1] < LANES:
                pad = jnp.zeros((part.shape[0], LANES - part.shape[1]), F32)
                part = jnp.concatenate([part, pad], axis=1)
            xs[l][p, pl.ds(at, value.shape[0]), :] = part

    for l, lv in enumerate(levels):
        for p in range(lv.planes):
            for i in range(lv.lead + lv.rows + 2):
                at = i * lv.pitch + lv.cols
                xs[l][p, at : at + lv.tail, :] = jnp.zeros((lv.tail, LANES), F32)

        @pl.when(top)
        def _(l=l, lv=lv):
            for p in range(lv.planes):
                xs[l][p, 0 : lv.at(0) - lv.tail, :] = jnp.zeros((lv.at(0) - lv.tail, LANES), F32)

        @pl.when(bottom)
        def _(l=l, lv=lv):
            for p in range(lv.planes):
                xs[l][p, lv.at(lv.rows) : lv.total, :] = jnp.zeros((lv.total - lv.at(lv.rows), LANES), F32)

    for l, lv in enumerate(levels):

        def place(source, row, l=l, lv=lv):
            n = source.shape[0]
            group = 8 if n % 8 == 0 else 1

            def run(i):
                for j in range(group):
                    k = i * group + j
                    at = (k + row + lv.lead) * lv.pitch
                    if not isinstance(i, int) and lv.pitch % 8 == 0:
                        at = pl.multiple_of(at, 8)
                    put(l, at, source[k].astype(F32))

            if n % 8:
                for i in range(n):
                    run(i)
            else:
                rows_loop(n // 8, run)

        def place_rows(source, row, l=l, lv=lv):
            if lv.folds == 1:
                return place(source, row)
            half = lv.cols // 2
            for i in range(source.shape[0]):
                for j, value in enumerate(unfolded(source[i])):
                    put(l, lv.at(row + i, j * half), value)

        def place_cols(source, way, l=l, lv=lv):
            dy, dx = way
            for i in range(source.shape[0]):
                col = i - lv.low if dx > 0 else lv.cols + i
                both = [source[i].astype(F32)] if lv.folds == 1 else unfolded(source[i])
                if dy > 0:
                    pieces = [(-lv.low, both[-1][lv.near - lv.low :])]
                elif dy < 0:
                    pieces = [(lv.rows, both[0][:2])]
                else:
                    pieces = [(j * lv.lines, v) for j, v in enumerate(both)]
                for row, v in pieces:
                    for p in range(lv.planes):
                        w = min(LANES, lv.chan - p * LANES)
                        at = pl.ds(lv.at(row, col), v.shape[0], stride=lv.pitch)
                        part = v if lv.folds == 2 else v[:, p * LANES : p * LANES + w]
                        if part.shape[1] < LANES:
                            part = jnp.concatenate([part, jnp.zeros((v.shape[0], LANES - w), F32)], axis=1)
                        xs[l][p, at, :] = part

        place(feats[l], 0)
        for k, way in enumerate(WAYS):

            @pl.when(on_map(way, -1))
            def _(k=k, way=way):
                source = halos[8 * l + k]
                if way[1]:
                    place_cols(source, way)
                else:
                    place_rows(source, -lv.low if way[0] > 0 else lv.rows)

    def blank(ref, lv, low, high):
        planes = ref.shape[0]

        def columns(col, n):
            start = lv.at(-low - 1)
            count = low + 1 + lv.rows + high
            for c in range(col, col + n):
                for p in range(planes):
                    ref[p, pl.ds(start + c, count, stride=lv.pitch), :] = jnp.zeros((count, LANES), F32)

        def rows(row, n):
            for p in range(planes):
                size = n * lv.pitch
                ref[p, pl.ds(lv.at(row) - lv.tail + 2, size), :] = jnp.zeros((size, LANES), F32)

        def before():
            for p in range(planes):
                for i in range(lv.lead - low - 1, lv.lead + lv.rows + high - 1):
                    end = (i + 1) * lv.pitch
                    ref[p, end - low : end, :] = jnp.zeros((low, LANES), F32)

        pl.when(left)(before)
        if high:
            pl.when(right)(lambda: columns(lv.cols, high))
            pl.when(bottom)(lambda: rows(lv.rows, high))

        pl.when(top)(lambda: rows(-low, low))

    def paired(piece):
        tiles = [[], [], [], [], []]
        for t in range(9):
            tiles[slot(t)[0]].append(piece(t))
        keep = lane(tiles[0][0].shape) < HALF
        tiles = [jnp.where(keep, *tile) if len(tile) > 1 else tile[0] for tile in tiles]
        return jnp.concatenate([tile.astype(BF16) for tile in tiles], axis=1)

    def wide_conv(l, src, dst, weight, bias, span, residual):
        lv = levels[l]
        start, length = span
        n, m = chunking(length, MOST)
        group = math.gcd(n, GROUP)

        def run(i, j):
            base = pl.multiple_of(start + (i * group + j) * m, 8)

            if l == 0:
                a, b, c = (
                    src[0, pl.ds(pl.multiple_of(base - 8 + d * lv.pitch, 8), m + 16), :] for d in (-1, 0, 1)
                )
                pieces = [jnp.where(lane(a.shape) < HALF, a, b), c]
            else:
                pieces = [
                    src[0, pl.ds(base + d * lv.pitch + e, m + 16), :] for e in (-1, 1) for d in (-1, 0, 1)
                ]
            lhs = jnp.concatenate([piece.astype(BF16) for piece in pieces], axis=1)
            o = lax.dot_general(lhs, weight[...], NT, preferred_element_type=F32)
            one, two = spread.at[2 * j], spread.at[2 * j + 1]
            one[0 : m + 16, :] = o[:, 0:LANES]
            two[0 : m + 16, :] = o[:, LANES:]
            if l == 0:
                y = one[7 : 7 + m, :]
                y = jnp.where(lane(y.shape) < HALF, y, one[9 : 9 + m, :])
                y = y + pltpu.roll(y, HALF, 1) + two[8 : 8 + m, :]
            else:
                y = one[0:m, :] + two[1 : 1 + m, :]
            y = y + bias
            if residual:
                y = y + dst[0, pl.ds(base, m), :]
            dst[0, pl.ds(base, m), :] = jnp.maximum(y, 0.0)

        def several(i):
            for j in range(group):
                run(i, j)

        rows_loop(n // group, several)

    def offset(lv, t):
        return (t // 3 - 1) * lv.pitch + t % 3 - 1

    def deep_conv2(src, dst, weight, bias, span, residual):
        lv = l2
        start, length = span
        m = up_to(length, 16)
        total = lv.total
        p0, p1 = src[0, :, :], src[1, :, :]
        ids = lane((total, LANES))
        r0, r1 = pltpu.roll(p0, 64, 1), pltpu.roll(p1, 64, 1)
        odd[0, :, :] = jnp.where(ids >= 64, r0, 0.0)
        odd[1, :, :] = jnp.where(ids < 64, r0, r1)

        def piece(ref, p, t):
            return ref[p, pl.ds(start + offset(lv, t), m), :]

        for t in range(0, 9, 2):
            k = 3 * (t // 2) * LANES
            cols2[0:m, k : k + 128] = piece(src, 0, t).astype(BF16)
            tile = piece(src, 1, t)
            if t == 8:
                cols2[0:m, k + 128 : k + 192] = tile[:, 0:64].astype(BF16)
            else:
                cols2[0:m, k + 128 : k + 256] = (tile + piece(odd, 0, t + 1)).astype(BF16)
                cols2[0:m, k + 256 : k + 384] = piece(odd, 1, t + 1).astype(BF16)
        y = lax.dot_general(cols2[0:m, :], weight, NT, preferred_element_type=F32) + bias
        for p in range(2):
            w = min(LANES, lv.chan - p * LANES)
            part = y[:, p * LANES : p * LANES + w]
            if residual:
                part = part + dst[p, pl.ds(start, m), 0:w]
            dst[p, pl.ds(start, m), 0:w] = jnp.maximum(part, 0.0)

    def deep_conv3(src, dst, weight, bias, span, residual):
        lv = l3
        start, length = span
        m = up_to(length, 16)
        for t in range(9):
            for p in range(lv.planes):
                k = (t * lv.planes + p) * LANES
                cols3[0:m, k : k + LANES] = src[p, pl.ds(start + offset(lv, t), m), :].astype(BF16)
        y = lax.dot_general(cols3[0:m, :], weight, NT, preferred_element_type=F32) + bias
        for p in range(lv.planes):
            part = y[:, p * LANES : (p + 1) * LANES]
            if residual:
                part = part + dst[p, pl.ds(start, m), :]
            dst[p, pl.ds(start, m), :] = jnp.maximum(part, 0.0)

    hs[2][1, :, :] = jnp.zeros((l2.total, LANES), F32)
    wide_conv(0, xs[0], hs[0], w0.at[0], bpad[0, 0:1, :], l0.first(), False)
    wide_conv(1, xs[1], hs[1], w1.at[0], bpad[1, 0:1, :], l1.first(), False)
    for l in (0, 1):
        blank(hs[l], levels[l], levels[l].rim + 1, 1)
    for c in copies:
        c.wait()
    deep_conv2(xs[2], hs[2], w2[0], biases[2][0:1, :], l2.first(), False)
    wide_conv(0, hs[0], xs[0], w0.at[1], bpad[0, 1:2, :], l0.second(), True)
    deep_conv3(xs[3], hs[3], w3[0], biases[3][0:1, :], l3.first(), False)
    ready(1)
    for l in (2, 3):
        blank(hs[l], levels[l], levels[l].rim + 1, 1)
    blank(xs[0], l0, l0.rim, 0)
    wide_conv(1, hs[1], xs[1], w1.at[1], bpad[1, 1:2, :], l1.second(), True)
    deep_conv2(hs[2], xs[2], w2[1], biases[2][1:2, :], l2.second(), True)
    deep_conv3(hs[3], xs[3], w3[1], biases[3][1:2, :], l3.second(), True)
    ready(2)
    for l in (1, 2):
        blank(xs[l], levels[l], levels[l].rim, 0)

    def gathered(src, plane, big, small, i, t, width=None):
        width = small.pitch if width is None else width
        at = (2 * i + t // 3 - 1 + big.lead) * big.pitch + 2 * (small.cols - width) + t % 3 - 1
        return src[plane, pl.ds(at, width, stride=2), :]

    rim = RIMS[1]
    rows = up_to(rim + l1.rows, 4)

    def down0(k):
        i0 = l1.rows - rows + 4 * k
        taps = paired(
            lambda t: jnp.concatenate([gathered(xs[0], 0, l0, l1, i0 + r, t) for r in range(4)], axis=0)
        )
        o = lax.dot_general(taps, wd0[...], NN, preferred_element_type=F32)
        at = pl.multiple_of((i0 + l1.lead) * l1.pitch - l1.tail, 8)
        t01[0, pl.ds(at, 4 * l1.pitch), :] = o[:, 0:LANES]
        v0[0, pl.ds(at, 4 * l1.pitch), :] = jnp.maximum(o[:, LANES:], 0.0)

    count = rows // 4
    group = math.gcd(count, GROUP)

    def downs0(k):
        for j in range(group):
            down0(k * group + j)

    rows_loop(count // group, downs0)
    blank(v0, l1, rim, 0)

    rows = l2.rows + 2
    at = l2.at(-2) - l2.tail
    span = rows * l2.pitch

    def down1(src, weight, form):
        taps = [
            jnp.concatenate([gathered(src, 0, l1, l2, i, t) for i in range(-2, l2.rows)], axis=0).astype(BF16)
            for t in range(9)
        ]
        return lax.dot_general(jnp.concatenate(taps, axis=1), weight[...], form, preferred_element_type=F32)

    o = down1(xs[1], wd1a, NT)
    e = down1(v0, wd1v, NN)
    second = o[:, LANES : 2 * LANES] + e[:, LANES : 2 * LANES]
    ids = lane(second.shape)
    t2[0, 0:span, :] = o[:, 0:LANES] + e[:, 0:LANES]
    t2[1, 0:span, :] = second
    v1[0, pl.ds(at, span), :] = jnp.where(ids >= 64, jnp.maximum(second, 0.0), 0.0)
    v1[1, pl.ds(at, span), :] = jnp.maximum(o[:, 2 * LANES :], 0.0)
    blank(v1, l2, 1, 0)
    def tap3(p, t):
        parts = []
        for i in range(l3.rows):
            piece = gathered(xs[2] if p < 2 else v1, p if p < 2 else 1, l2, l3, i, t, l3.cols)
            if p == 1:
                piece = piece + gathered(v1, 0, l2, l3, i, t, l3.cols)
            parts.append(piece)
        return jnp.concatenate(parts, axis=0).astype(BF16)

    taps = jnp.concatenate([tap3(2, t) for t in range(9)], axis=1)
    t3 = lax.dot_general(taps, wd2v[...], NT, preferred_element_type=F32)
    taps = jnp.concatenate([tap3(p, t) for t in range(9) for p in range(2)], axis=1)
    for c in fin2_copies:
        c.wait()
    t3 = t3 + lax.dot_general(taps, wd2[...], NN, preferred_element_type=F32)

    def center(l, i):
        lv = levels[l]
        parts = [xs[l][p, pl.ds(lv.at(i), lv.cols), :] for p in range(lv.planes)]
        return jnp.concatenate(parts, axis=1)[:, : lv.chan] if lv.planes > 1 else parts[0][:, : lv.chan]

    a3 = jnp.concatenate([center(3, i) for i in range(l3.rows)], axis=0)
    y3 = jnp.maximum(a3 + t3, 0.0).astype(BF16)
    for i in range(l3.rows):
        outs[3][i, :, :] = y3[i * l3.cols : (i + 1) * l3.cols, :]

    c0, c1, c2 = l0.chan, l1.chan, l2.chan
    a3 = a3.astype(BF16)
    up3_0 = lax.dot_general(a3, up3[0, 0:c0, :], NT, preferred_element_type=F32)
    up3_1 = lax.dot_general(a3, up3[0, c0 : c0 + c1, :], NT, preferred_element_type=F32)
    up3_2 = lax.dot_general(a3, up3[0, c0 + c1 :, :], NT, preferred_element_type=F32)

    def enlarge(value, dst, plane, width, rows, cols):
        for i in range(rows):
            line = value[i * cols : (i + 1) * cols, :]
            for di in range(2):
                for dj in range(2):
                    base = (2 * i + di) * 2 * cols + dj
                    dst[plane, pl.ds(base, cols, stride=2), 0:width] = line

    enlarge(up3_0, u2, 0, c0, l3.rows, l3.cols)
    enlarge(up3_1, u2, 1, c1, l3.rows, l3.cols)
    enlarge(up3_2[:, 0:LANES], u2, 2, LANES, l3.rows, l3.cols)
    enlarge(up3_2[:, LANES:], u2, 3, c2 - LANES, l3.rows, l3.cols)
    a2 = jnp.concatenate([center(2, i) for i in range(l2.rows)], axis=0)
    a2b = a2.astype(BF16)
    up2_0 = lax.dot_general(a2b, up2[0, 0:c0, :], NT, preferred_element_type=F32) + u2[0, :, 0:c0]
    up2_1 = lax.dot_general(a2b, up2[0, c0:, :], NT, preferred_element_type=F32) + u2[1, :, 0:c1]
    for i in range(l2.rows):
        for p in range(2):
            w = min(LANES, c2 - p * LANES)
            line = xs[2][p, pl.ds(l2.at(i), l2.cols), 0:w]
            line = line + t2[p, pl.ds((i + 2) * l2.pitch + l2.tail, l2.cols), 0:w]
            line = line + u2[2 + p, pl.ds(i * l2.cols, l2.cols), 0:w]
            outs[2][i, :, p * LANES : p * LANES + w] = jnp.maximum(line, 0.0).astype(BF16)
    enlarge(up2_0, u1, 0, c0, l2.rows, l2.cols)
    enlarge(up2_1, u1, 1, c1, l2.rows, l2.cols)

    def join1(k, slots):
        lines = []
        for r in range(4):
            i = 4 * k + r
            at = pl.multiple_of((i + l1.lead) * l1.pitch, 8)
            line = xs[1][0, pl.ds(at, l1.cols), 0:c1]
            lines.append(line)
            total = line + t01[0, pl.ds(at, l1.cols), 0:c1]
            total = total + u1[1, pl.ds(pl.multiple_of(i * l1.cols, 8), l1.cols), 0:c1]
            outs[1][i, :, :] = jnp.maximum(total, 0.0).astype(BF16)
        a1 = jnp.concatenate(lines, axis=0).astype(BF16)
        n = 4 * l1.cols
        y = lax.dot_general(a1, up1[0], NT, preferred_element_type=F32)
        y = y + u1[0, pl.ds(pl.multiple_of(k * n, 8), n), 0:c0]
        for r in range(4):
            line = y[r * l1.cols : (r + 1) * l1.cols, :]
            for dj in range(2):
                u0[slots + r, pl.ds(dj, l1.cols, stride=2), 0:c0] = line
            up = u0[slots + r, 0 : l0.cols, 0:c0]
            for di in range(2):
                i = 2 * (4 * k + r) + di
                at = pl.multiple_of((i + l0.lead) * l0.pitch, 8)
                total = jnp.maximum(xs[0][0, pl.ds(at, l0.cols), 0:c0] + up, 0.0)
                last[pl.ds(i, c0, stride=l0.rows + 1), :] = total.T

    count = l1.rows // 4
    pair = math.gcd(count, 8)

    def joins1(k):
        for j in range(pair):
            join1(k * pair + j, 4 * j)

    rows_loop(count // pair, joins1)

    def leave(k):
        for j in range(8):
            at = pl.multiple_of(8 * k * (l0.rows + 1), 8) + j * (l0.rows + 1)
            outs[0][8 * k + j] = last[pl.ds(at, l0.rows), :].astype(BF16)

    rows_loop(c0 // 8, leave)


def per_device(*args):
    feats, weights, biases, rest = args[0:4], args[4:8], args[8:12], args[12:20]
    levels = [Level(l, f.shape[1:] + f.shape[:1]) for l, f in enumerate(feats)]
    feats = [feats[0]] + [f.transpose(1, 2, 0) for f in feats[1:]]
    l0, l1, l2, l3 = levels
    c0, c1, c2, c3 = (lv.chan for lv in levels)
    *halos, first = halos_of(levels, feats)
    feats[0] = first
    up1, up2, up3, mid0, mid1, fin0, fin1, fin2 = rest
    fin0, fin2 = fin0[0].T, fin2[0].T
    vmem, any_ = pl.BlockSpec(memory_space=pltpu.VMEM), pl.BlockSpec(memory_space=pl.ANY)
    V = pltpu.VMEM
    maps = [V((lv.planes, lv.total, LANES), F32) for lv in levels]
    m2, m3 = up_to(l2.first()[1], 16), up_to(l3.first()[1], 16)
    most = max(chunking(s[1], MOST)[1] for lv in levels[:2] for s in (lv.first(), lv.second()))
    scratch = maps * 2 + [
        V((2 * GROUP, most + 16, LANES), F32),
        V((2, l2.total, LANES), F32),
        V((m2, 9 * c2), BF16),
        V((m3, 9 * c3), BF16),
        V(weights[2].shape, BF16),
        V(weights[3].shape, BF16),
        *(V(r.shape, BF16) for r in (up1, up2, up3, mid0, mid1, fin0, fin1)),
        V((2, 2 * LANES, 2 * LANES), BF16),
        V((2, 2 * LANES, 6 * LANES), BF16),
        V((5 * LANES, 2 * LANES), BF16),
        V((3 * LANES, 9 * LANES), BF16),
        V((9 * LANES, 2 * LANES), BF16),
        V((9 * up_to(c2, LANES), c3), BF16),
        V((c3, 9 * LANES), BF16),
        V((LANES, up_to(9 * c0, LANES)), F32),
        V((2, 8, LANES), F32),
        V((1, l1.total, LANES), F32),
        V((1, l1.total, LANES), F32),
        V((2, (l2.rows + 2) * l2.pitch, LANES), F32),
        V((2, l2.total, LANES), F32),
        V((32, l0.cols, LANES), F32),
        V((2, l1.rows * l1.cols, LANES), F32),
        V((4, l2.rows * l2.cols, LANES), F32),
        V((c0 * (l0.rows + 1), l0.cols), F32),
        pltpu.SemaphoreType.DMA((18,)),
    ]
    outs = pl.pallas_call(
        functools.partial(body, levels),
        out_shape=[jax.ShapeDtypeStruct(args[0].shape, BF16)]
        + [jax.ShapeDtypeStruct(f.shape, BF16) for f in feats[1:]],
        in_specs=[vmem] * 38 + [any_] * 2 + [vmem] * 4 + [any_] * 8,
        out_specs=[vmem] * 4,
        scratch_shapes=scratch,
        compiler_params=pltpu.CompilerParams(vmem_limit_bytes=60 * 2**20),
    )(*feats, *halos, *weights, *biases, up1, up2, up3, mid0, mid1, fin0, fin1, fin2)
    return (outs[0], *(o.transpose(2, 0, 1) for o in outs[1:]))


def solution(mesh):
    tiled = P(None, "ty", "tx")
    return jax.shard_map(
        per_device,
        mesh=mesh,
        in_specs=(tiled,) * 4 + (P(),) * 16,
        out_specs=(tiled,) * 4,
        check_vma=False,
    )
```
